32 devices in a mesh: fsdp: 8 (over z, y), grp: 4 (over x, core).
Axes of the slice: x: 2, y: 2, z: 4, core: 2. Of those that a mesh axis runs over, the one named last changes fastest.
Arguments:
- tokens: int32 [64, 512], P(('fsdp', 'grp')), may hold values from 0 to 30521
- positions: int32 [64, 512], P(('fsdp', 'grp')), may hold values from 0 to 511
- lengths: int32 [64], P(('fsdp', 'grp')), may hold values from 1 to 512, 16384 in all
- labels: int32 [64], P(('fsdp', 'grp')), may hold values from 0 to 2
- word_table: float32 [768, 30522], P('fsdp'), may hold values from -0.3 to 0.3
- word_first: float32 [768, 30522], P('fsdp'), may hold values from -0.00012207031 to 0.00012207031
- word_second: float32 [768, 30522], P('fsdp'), may hold values from 3.176203e-11 to 1.2704812e-10
- place_table: float32 [768, 512], P('fsdp'), may hold values from -0.3 to 0.3
- place_first: float32 [768, 512], P('fsdp'), may hold values from -0.00012207031 to 0.00012207031
- place_second: float32 [768, 512], P('fsdp'), may hold values from 3.176203e-11 to 1.2704812e-10
- square_weights: float32 [768, 3840], P('fsdp')
- square_first: float32 [768, 3840], P('fsdp'), may hold values from -0.00012207031 to 0.00012207031
- square_second: float32 [768, 3840], P('fsdp'), may hold values from 3.176203e-11 to 1.2704812e-10
- widen_weights: float32 [768, 3072], P('fsdp'), may hold values from -0.21875 to 0.21875
- widen_first: float32 [768, 3072], P('fsdp'), may hold values from -0.00012207031 to 0.00012207031
- widen_second: float32 [768, 3072], P('fsdp'), may hold values from 3.176203e-11 to 1.2704812e-10
- narrow_weights: float32 [3072, 768], P('fsdp'), may hold values from -0.109375 to 0.109375
- narrow_first: float32 [3072, 768], P('fsdp'), may hold values from -0.00012207031 to 0.00012207031
- narrow_second: float32 [3072, 768], P('fsdp'), may hold values from 3.176203e-11 to 1.2704812e-10
- small_params: float32 [18, 768], replicated
- small_first: float32 [18, 768], replicated, may hold values from -0.00048828125 to 0.00048828125
- small_second: float32 [18, 768], replicated, may hold values from 5.081925e-10 to 2.03277e-09
- class_bias: float32 [3], replicated, may hold values from -3 to 3
- class_first: float32 [3], replicated, may hold values from -0.00048828125 to 0.00048828125
- class_second: float32 [3], replicated, may hold values from 5.081925e-10 to 2.03277e-09
- teacher_word: bfloat16 [768, 30522], P('grp'), may hold values from -6 to 6
- teacher_place: bfloat16 [768, 512], P('grp'), may hold values from -6 to 6
- teacher_attention: bfloat16 [2, 4, 768, 768], P(None, None, None, 'grp')
- teacher_feedforward: bfloat16 [2, 2, 768, 3072], P(None, None, None, 'grp'), may hold values from -0.21875 to 0.21875
- teacher_pooler: bfloat16 [768, 768], replicated, may hold values from -0.21875 to 0.21875
- teacher_vectors: float32 [30, 768], replicated
Outputs:
- total_loss: float32 [], replicated
- gradient_norm: float32 [], replicated
- new_word_table: float32 [768, 30522], P('fsdp')
- new_word_first: float32 [768, 30522], P('fsdp')
- new_word_second: float32 [768, 30522], P('fsdp')
- new_place_table: float32 [768, 512], P('fsdp')
- new_place_first: float32 [768, 512], P('fsdp')
- new_place_second: float32 [768, 512], P('fsdp')
- new_square_weights: float32 [768, 3840], P('fsdp')
- new_square_first: float32 [768, 3840], P('fsdp')
- updated_square_moment: float32 [768, 3840], P('fsdp')
- new_widen_weights: float32 [768, 3072], P('fsdp')
- new_widen_first: float32 [768, 3072], P('fsdp')
- new_widen_second: float32 [768, 3072], P('fsdp')
- new_narrow_weights: float32 [3072, 768], P('fsdp')
- new_narrow_first: float32 [3072, 768], P('fsdp')
- new_narrow_second: float32 [3072, 768], P('fsdp')
- new_small_params: float32 [18, 768], replicated
- new_small_first: float32 [18, 768], replicated
- new_small_second: float32 [18, 768], replicated
- new_class_bias: float32 [3], replicated
- new_class_first: float32 [3], replicated
- new_class_second: float32 [3], replicated
The draws below stay inside these ranges and needn't reach their ends.
Inputs may be any that keep to these rules, and one draw needn't show every extreme that they name: `lengths`: the longest sequence has exactly 512 tokens.
All inputs are finite; a program needn't handle non-finite values. No bound on the sum of `lengths` on one device may be relied on, other than what follows from the above.
Results may differ from the reference program's by a relative error of at most 0.005.
The reference program's roundings to bfloat16 on the way count: a program that leaves them out, or rounds other values in their place, can miss the bound.
Values may be sent and summed in bfloat16 or wider, within the bound.
No kernel may reach another device: no remote copies, remote signals or barrier semaphores. Data moves between devices by JAX's collectives and lax.ppermute only.
A program may use at most 256 MiB of HBM per device.

```python
import math
import jax
import jax.numpy as jnp
import numpy as np
from jax import lax

D = 768
HEADS = 12
HDIM = 64
FF = 3072
VOCAB = 30522
POSITIONS = 512
CLASSES = 3
LEN = 512
SEQS = 64
GROWS = 18
TROWS = 30


def rough_normal(key, shape):
    return jax.random.truncated_normal(key, -4.0, 4.0, shape, jnp.float32)


def draw_square_weights(key, part):
    values = rough_normal(key, (D, 5 * D))
    column_block = jnp.arange(5 * D) // D
    scale_row = jnp.where(column_block == 3, 4.0, 1.0) * D ** (-0.5)
    return values * scale_row[None, :]


def draw_teacher_attention(key, part):
    values = rough_normal(key, (2, 4, D, D))
    scale_row = jnp.where(jnp.arange(4) == 3, 4.0, 1.0) * D ** (-0.5)
    return (values * scale_row[None, :, None, None]).astype(jnp.bfloat16)


def vector_table(key, row_count, gain_matrix_rows, class_start):
    values = rough_normal(key, (row_count, D))
    row_index = jnp.arange(row_count)[:, None]
    is_gain = jnp.isin(row_index, jnp.array(gain_matrix_rows))
    gain_part = 1.0 + 0.1 * values
    classifier_portion = 3.0 * D ** (-0.5) * values
    bias_part = 0.3 * values
    return jnp.where(is_gain, gain_part, jnp.where(row_index >= class_start, classifier_portion, bias_part))


def draw_small_params(key, part):
    spread_rows = FF // D
    return vector_table(key, GROWS, (0, 5, 8 + spread_rows), 11 + spread_rows)


def draw_teacher_vectors(key, part):
    spread_rows = FF // D
    block_rows = 8 + spread_rows
    gain_matrix_rows = (0, 5, 8 + spread_rows, 5 + block_rows, 8 + spread_rows + block_rows)
    return vector_table(key, TROWS, gain_matrix_rows, 3 + 2 * block_rows)


def set_ends(result, rng, smallest, top_value):
    index_at = [jax.random.randint(jax.random.fold_in(rng, axis), (), 0, length) for axis, length in enumerate(result.shape)]
    widest = result.shape.index(max(result.shape))
    neighbour = index_at[:widest] + [(index_at[widest] + 1) % result.shape[widest]] + index_at[widest + 1:]
    return result.at[tuple(index_at)].set(smallest).at[tuple(neighbour)].set(top_value)


def steps_of(own_key, shape, cuts, least, top_value):
    def one(dim, shards_of):
        steps = jax.random.uniform(jax.random.fold_in(jax.random.fold_in(own_key, 6), dim), (shards_of,), jnp.float32, least / len(cuts), top_value / len(cuts))
        return jnp.repeat(jnp.exp(steps), shape[dim] // shards_of).reshape((-1,) + (1,) * (len(shape) - dim - 1))

    loudness = one(*cuts[0])
    for cut in cuts[1:]:
        loudness = loudness * one(*cut)
    return loudness


def rank_table(number_of, slope):
    portions = [(1 << 20) // math.isqrt(rank ** slope) + 1 for rank in range(1, number_of + 1)]
    scale = 1 + sum(portions) // (1 << 30)
    return np.cumsum(np.array([max(1, weight // scale) for weight in portions]))


def skewed_ids(key, shape, number_of, lean):
    listing = rank_table(number_of, lean)
    pick = jax.random.randint(jax.random.fold_in(key, 1), shape, 0, int(listing[number_of - 1]))
    rank = jnp.searchsorted(jnp.asarray(listing, jnp.int32), pick, side="right")
    return jax.random.permutation(jax.random.fold_in(key, 2), number_of)[rank].astype(jnp.int32)


def split_up(amount, total, limit, slope):
    portions = [(1 << 20) // math.isqrt(standing ** slope) + 1 for standing in range(2, amount + 1)]
    spare, given = total - limit - (amount - 1), [1] * (amount - 1)
    while spare > 0:
        movable = [i for i in range(amount - 1) if given[i] < limit]
        pool, remaining = sum([portions[i] for i in movable]), spare
        for i in movable:
            more = min(limit - given[i], max(1, remaining * portions[i] // pool), spare)
            given[i] = given[i] + more
            spare = spare - more
    return np.array([limit] + given)


def uneven(own_key, count, total, limit, lean):
    if count == 2:
        one = jax.random.randint(own_key, (), max(1, total - limit), min(limit, total - 1) + 1)
        return jnp.stack([one, total - one])
    sizes = jnp.asarray(split_up(count, total, limit, lean), jnp.int32)
    couples = (count - 1) // 2
    giver, taker = sizes[1:1 + 2 * couples:2], sizes[2:2 + 2 * couples:2]
    margin = jnp.minimum(giver - 1, limit - taker)
    moved = jax.random.randint(jax.random.fold_in(own_key, 1), (couples,), 0, 1 << 20) % (margin + 1)
    sizes = sizes.at[1:1 + 2 * couples:2].set(giver - moved).at[2:2 + 2 * couples:2].set(taker + moved)
    return sizes[jax.random.permutation(jax.random.fold_in(own_key, 2), count)]


def bell_draw(stream_key, extent, width, most, cuts=(), held_as=jnp.bfloat16):
    level = steps_of(stream_key, extent, cuts, -0.22, 0.18) if cuts else 1.0
    drawn = jax.random.normal(stream_key, extent, jnp.float32) * width * level
    return jnp.minimum(jnp.maximum(drawn, -most), most).astype(held_as)


def setup_inputs(seed: int = 0) -> dict:
    keys = jax.random.split(jax.random.key(seed), 32)
    tokens = set_ends(skewed_ids(keys[0], (SEQS, LEN), VOCAB, 2), jax.random.fold_in(keys[0], 3), 0, VOCAB - 1).astype(jnp.int32)
    positions = set_ends(jax.random.randint(keys[1], (SEQS, LEN), 0, POSITIONS), jax.random.fold_in(keys[1], 1), 0, POSITIONS - 1).astype(jnp.int32)
    lengths = uneven(keys[2], SEQS, SEQS * LEN // 2, LEN, 2).astype(jnp.int32)
    labels = set_ends(jax.random.randint(keys[3], (SEQS,), 0, CLASSES), jax.random.fold_in(keys[3], 1), 0, CLASSES - 1).astype(jnp.int32)
    word_table = bell_draw(keys[4], (D, VOCAB), 0.05, 0.3, ((0, 8),), jnp.float32)
    word_first = bell_draw(keys[5], (D, VOCAB), ((VOCAB * D + POSITIONS * D + 5 * D * D + 2 * D * FF + GROWS * D) ** -0.5 / 9), 0.00012207031, ((0, 8),), jnp.float32)
    word_second = jnp.clip(jnp.exp(math.log(1.2704812202279925e-10) - 1.3862944 * jax.random.uniform(keys[6], (D, VOCAB), jnp.float32) ** steps_of(keys[6], (D, VOCAB), ((0, 8),), -0.2, 0.2)), 3.176203050569981e-11, 1.2704812202279925e-10)
    place_table = bell_draw(keys[7], (D, POSITIONS), 0.05, 0.3, ((0, 8),), jnp.float32)
    place_first = bell_draw(keys[8], (D, POSITIONS), ((VOCAB * D + POSITIONS * D + 5 * D * D + 2 * D * FF + GROWS * D) ** -0.5 / 9), 0.00012207031, ((0, 8),), jnp.float32)
    place_second = jnp.clip(jnp.exp(math.log(1.2704812202279925e-10) - 1.3862944 * jax.random.uniform(keys[9], (D, POSITIONS), jnp.float32) ** steps_of(keys[9], (D, POSITIONS), ((0, 8),), -0.2, 0.2)), 3.176203050569981e-11, 1.2704812202279925e-10)
    square_weights = draw_square_weights(jax.random.fold_in(keys[31], 71), 0)
    square_first = bell_draw(keys[11], (D, 5 * D), ((VOCAB * D + POSITIONS * D + 5 * D * D + 2 * D * FF + GROWS * D) ** -0.5 / 9), 0.00012207031, ((0, 8),), jnp.float32)
    square_second = jnp.clip(jnp.exp(math.log(1.2704812202279925e-10) - 1.3862944 * jax.random.uniform(keys[12], (D, 5 * D), jnp.float32) ** steps_of(keys[12], (D, 5 * D), ((0, 8),), -0.2, 0.2)), 3.176203050569981e-11, 1.2704812202279925e-10)
    widen_weights = bell_draw(keys[13], (D, FF), D ** -0.5, 0.21875, ((0, 8),), jnp.float32)
    widen_first = bell_draw(keys[14], (D, FF), ((VOCAB * D + POSITIONS * D + 5 * D * D + 2 * D * FF + GROWS * D) ** -0.5 / 9), 0.00012207031, ((0, 8),), jnp.float32)
    widen_second = jnp.clip(jnp.exp(math.log(1.2704812202279925e-10) - 1.3862944 * jax.random.uniform(keys[15], (D, FF), jnp.float32) ** steps_of(keys[15], (D, FF), ((0, 8),), -0.2, 0.2)), 3.176203050569981e-11, 1.2704812202279925e-10)
    narrow_weights = bell_draw(keys[16], (FF, D), FF ** -0.5, 0.109375, ((0, 8),), jnp.float32)
    narrow_first = bell_draw(keys[17], (FF, D), ((VOCAB * D + POSITIONS * D + 5 * D * D + 2 * D * FF + GROWS * D) ** -0.5 / 9), 0.00012207031, ((0, 8),), jnp.float32)
    narrow_second = jnp.clip(jnp.exp(math.log(1.2704812202279925e-10) - 1.3862944 * jax.random.uniform(keys[18], (FF, D), jnp.float32) ** steps_of(keys[18], (FF, D), ((0, 8),), -0.2, 0.2)), 3.176203050569981e-11, 1.2704812202279925e-10)
    small_params = draw_small_params(jax.random.fold_in(keys[31], 71), 0)
    small_first = bell_draw(keys[20], (GROWS, D), (4 * (VOCAB * D + POSITIONS * D + 5 * D * D + 2 * D * FF + GROWS * D) ** -0.5 / 9), 0.00048828125, (), jnp.float32)
    small_second = jnp.clip(jnp.exp(jax.random.uniform(keys[21], (GROWS, D), jnp.float32, math.log(5.08192488091197e-10), math.log(2.032769952364788e-09))), 5.08192488091197e-10, 2.032769952364788e-09)
    class_bias = bell_draw(keys[22], (CLASSES,), 0.5, 3.0, (), jnp.float32)
    class_first = bell_draw(keys[23], (CLASSES,), (4 * (VOCAB * D + POSITIONS * D + 5 * D * D + 2 * D * FF + GROWS * D) ** -0.5 / 9), 0.00048828125, (), jnp.float32)
    class_second = jnp.clip(jnp.exp(jax.random.uniform(keys[24], (CLASSES,), jnp.float32, math.log(5.08192488091197e-10), math.log(2.032769952364788e-09))), 5.08192488091197e-10, 2.032769952364788e-09)
    teacher_word = bell_draw(keys[25], (D, VOCAB), 1.0, 6.0, ((0, 4),))
    teacher_place = bell_draw(keys[26], (D, POSITIONS), 1.0, 6.0, ((0, 4),))
    teacher_attention = draw_teacher_attention(jax.random.fold_in(keys[31], 71), 0)
    teacher_feedforward = bell_draw(keys[28], (2, 2, D, FF), D ** -0.5, 0.21875, ((3, 4),))
    teacher_pooler = bell_draw(keys[29], (D, D), D ** -0.5, 0.21875)
    teacher_vectors = draw_teacher_vectors(jax.random.fold_in(keys[31], 71), 0)
    return dict(tokens=tokens, positions=positions, lengths=lengths, labels=labels, word_table=word_table, word_first=word_first, word_second=word_second, place_table=place_table, place_first=place_first, place_second=place_second, square_weights=square_weights, square_first=square_first, square_second=square_second, widen_weights=widen_weights, widen_first=widen_first, widen_second=widen_second, narrow_weights=narrow_weights, narrow_first=narrow_first, narrow_second=narrow_second, small_params=small_params, small_first=small_first, small_second=small_second, class_bias=class_bias, class_first=class_first, class_second=class_second, teacher_word=teacher_word, teacher_place=teacher_place, teacher_attention=teacher_attention, teacher_feedforward=teacher_feedforward, teacher_pooler=teacher_pooler, teacher_vectors=teacher_vectors)


@jax.custom_vjp
def low(v):
    return lax.optimization_barrier(v.astype(jnp.bfloat16)).astype(jnp.float32)

@jax.custom_vjp
def low_back(v):
    return v

def low_keep(v):
    return (low(v), None)

def low_pass(kept, grad):
    return (grad,)

def back_keep(v):
    return (v, None)

def back_low(kept, grad):
    return (low(grad),)
low.defvjp(low_keep, low_pass)
low_back.defvjp(back_keep, back_low)
highest = lax.Precision.HIGHEST
layer_eps = 1e-06
dist_eps = 1e-06
temper = 10.0
beta_one = 0.9
beta_two = 0.999
learn_rate = 0.05
decay_rate = 0.01
adam_eps = 1e-08
adam_steps = 10
clip_bound = 1.0

def matmul_high(left, right):
    return jnp.matmul(left, right, precision=highest)

def layer_norm(values, scale_row, shift_row):
    center = values - lax.optimization_barrier(jnp.mean(values, -1, keepdims=True))
    spread = lax.optimization_barrier(jnp.mean(center * center, -1, keepdims=True))
    return center * lax.rsqrt(spread + layer_eps) * scale_row + shift_row

def both_ways(values):
    return low(low_back(values))

def attend(query_rows, key_rows, value_rows, length):
    query_heads = query_rows.reshape(query_rows.shape[0], HEADS, HDIM)
    key_heads = key_rows.reshape(key_rows.shape[0], HEADS, HDIM)
    value_heads = value_rows.reshape(value_rows.shape[0], HEADS, HDIM)
    scores = low_back(jnp.einsum('qhd,khd->hqk', query_heads, key_heads, precision=highest) * HDIM ** (-0.5))
    key_valid = jnp.arange(key_rows.shape[0]) < length
    scores = jnp.where(key_valid, scores, -1e+30)
    shifted = jnp.exp(scores - lax.optimization_barrier(jnp.max(scores, -1, keepdims=True)))
    soft_weights = shifted / lax.optimization_barrier(jnp.sum(shifted, -1, keepdims=True))
    context = jnp.einsum('hqk,khd->qhd', low(soft_weights), value_heads, precision=highest)
    return context.reshape(query_rows.shape[0], HEADS * HDIM)

def layer_forward(rows, weights, layer_vectors, length, full):
    query_weight, key_weight, value_weight, out_weight, widen, narrow = weights
    spread_rows = FF // D
    rows_reduced_precision = low(rows)
    key_rows = both_ways(matmul_high(rows_reduced_precision, key_weight))
    value_rows = both_ways(matmul_high(rows_reduced_precision, value_weight) + layer_vectors[1])
    if full:
        residual, query_in = (rows, rows_reduced_precision)
    else:
        residual, query_in = (rows[:1], rows_reduced_precision[:1])
    query_rows = both_ways(matmul_high(query_in, query_weight) + layer_vectors[0])
    context = both_ways(attend(query_rows, key_rows, value_rows, length))
    branch = low_back(matmul_high(context, out_weight) + layer_vectors[2])
    hidden = layer_norm(residual + branch, layer_vectors[3], layer_vectors[4])
    pre_active = low_back(matmul_high(low(hidden), widen) + layer_vectors[5:5 + spread_rows].reshape(-1))
    active = low(jax.nn.gelu(pre_active, approximate=False))
    output = low_back(matmul_high(active, narrow) + layer_vectors[5 + spread_rows])
    return layer_norm(hidden + output, layer_vectors[6 + spread_rows], layer_vectors[7 + spread_rows])

def teacher_one(tables, token_row, place_row, length):
    word_rows, place_rows, attention, feedforward, pooler, vectors = tables
    block_rows = 8 + FF // D
    rows = layer_norm(low(word_rows[:, token_row].T + place_rows[:, place_row].T), vectors[0], vectors[1])
    for layer_index in range(2):
        weights = (attention[layer_index, 0], attention[layer_index, 1], attention[layer_index, 2], attention[layer_index, 3].T, feedforward[layer_index, 0], feedforward[layer_index, 1].T)
        start_row = 2 + layer_index * block_rows
        rows = layer_forward(rows, weights, vectors[start_row:start_row + block_rows], length, layer_index == 0)
    teacher_cls = rows[0]
    pooled = jnp.tanh(matmul_high(low(teacher_cls), pooler) + vectors[2 + 2 * block_rows])
    logits = matmul_high(low(vectors[3 + 2 * block_rows:]), low(pooled))
    return (teacher_cls, logits)

def student_term(params, token_row, place_row, length, label, teacher_cls, teacher_logits):
    word_rows, place_rows, square, widen, narrow, small_rows, bias_row = params
    block_rows = 8 + FF // D
    rows = layer_norm(low(word_rows[:, token_row].T + place_rows[:, place_row].T), small_rows[0], small_rows[1])
    weights = (square[:, :D], square[:, D:2 * D], square[:, 2 * D:3 * D], square[:, 3 * D:4 * D], widen, narrow)
    first_vector = layer_forward(rows, weights, small_rows[2:2 + block_rows], length, False)[0]
    pooled = jnp.tanh(matmul_high(low(first_vector), square[:, 4 * D:]) + small_rows[2 + block_rows])
    logits = matmul_high(low(small_rows[3 + block_rows:]), low(pooled)) + bias_row
    log_probs = jax.nn.log_softmax(logits)
    hard_loss = -jnp.sum(jnp.where(jnp.arange(CLASSES) == label, log_probs, 0.0))
    teacher_soft = jax.nn.log_softmax(teacher_logits / temper)
    student_soft = jax.nn.log_softmax(logits / temper)
    divergence = jnp.sum(jnp.exp(teacher_soft) * (teacher_soft - student_soft))
    student_unit = first_vector * lax.rsqrt(jnp.sum(first_vector * first_vector) + dist_eps)
    teacher_unit = teacher_cls * lax.rsqrt(jnp.sum(teacher_cls * teacher_cls) + dist_eps)
    distance = jnp.sum((student_unit - teacher_unit) ** 2)
    return hard_loss + temper * temper * divergence + 100.0 * distance

def adam_update(weight, moment_one, moment_two, gradient, factor):
    gradient = gradient * factor
    first_new = beta_one * moment_one + (1.0 - beta_one) * gradient
    second_new = beta_two * moment_two + (1.0 - beta_two) * gradient * gradient
    first_hat = first_new / (1.0 - beta_one ** adam_steps)
    second_hat = second_new / (1.0 - beta_two ** adam_steps)
    weight_new = weight - learn_rate * (first_hat / (jnp.sqrt(second_hat) + adam_eps) + decay_rate * weight)
    return (weight_new, first_new, second_new)

def reference(tokens, positions, lengths, labels, word_table, word_first, word_second, place_table, place_first, place_second, square_weights, square_first, square_second, widen_weights, widen_first, widen_second, narrow_weights, narrow_first, narrow_second, small_params, small_first, small_second, class_bias, class_first, class_second, teacher_word, teacher_place, teacher_attention, teacher_feedforward, teacher_pooler, teacher_vectors):
    tables = (teacher_word.astype(jnp.float32), teacher_place.astype(jnp.float32), teacher_attention.astype(jnp.float32), teacher_feedforward.astype(jnp.float32), teacher_pooler.astype(jnp.float32), teacher_vectors)
    teacher_cls, teacher_logits = lax.map(lambda pieces: teacher_one(tables, *pieces), (tokens, positions, lengths))
    params = (word_table, place_table, square_weights, widen_weights, narrow_weights, small_params, class_bias)

    def total_loss_of(weights):
        word_rows, place_rows, square, widen, narrow, small_rows, bias_row = weights
        lowered = (low(word_rows), low(place_rows), low(square), low(widen), low(narrow), small_rows, bias_row)

        def scan_step(carry, pieces):
            return (carry + jax.checkpoint(student_term)(lowered, *pieces), None)
        total, unused = lax.scan(scan_step, jnp.zeros((), jnp.float32), (tokens, positions, lengths, labels, teacher_cls, teacher_logits))
        return total / SEQS
    total_loss, pullback = jax.vjp(total_loss_of, params)
    grads = pullback(jnp.ones_like(total_loss))[0]
    total_square = jnp.zeros((), jnp.float32)
    for gradient in grads:
        total_square = total_square + jnp.sum(gradient * gradient)
    gradient_norm = jnp.sqrt(total_square)
    factor = jnp.minimum(1.0, clip_bound / gradient_norm)
    word_new = adam_update(word_table, word_first, word_second, grads[0], factor)
    place_new = adam_update(place_table, place_first, place_second, grads[1], factor)
    square_new = adam_update(square_weights, square_first, square_second, grads[2], factor)
    widen_new = adam_update(widen_weights, widen_first, widen_second, grads[3], factor)
    narrow_new = adam_update(narrow_weights, narrow_first, narrow_second, grads[4], factor)
    small_new = adam_update(small_params, small_first, small_second, grads[5], factor)
    class_new = adam_update(class_bias, class_first, class_second, grads[6], factor)
    return (total_loss, gradient_norm, word_new[0], word_new[1], word_new[2], place_new[0], place_new[1], place_new[2], square_new[0], square_new[1], square_new[2], widen_new[0], widen_new[1], widen_new[2], narrow_new[0], narrow_new[1], narrow_new[2], small_new[0], small_new[1], small_new[2], class_new[0], class_new[1], class_new[2])
```

```python
import jax
import jax.numpy as jnp
from jax import lax
from jax.experimental import pallas as pl
from jax.experimental.pallas import tpu as pltpu
from jax.sharding import PartitionSpec as P

HDIM = 64
BF = jnp.bfloat16
F32 = jnp.float32
ALL = ("fsdp", "grp")
MIB = 2**20

highest = lax.Precision.HIGHEST
layer_eps = 1e-06
dist_eps = 1e-06
temper = 10.0
beta_one = 0.9
beta_two = 0.999
learn_rate = 0.05
decay_rate = 0.01
adam_eps = 1e-08
adam_steps = 10
clip_bound = 1.0
LANES = 128
CODE = 512
COEF = 32


def layer_norm(values, scale_row, shift_row):
    center = values - jnp.mean(values, -1, keepdims=True)
    spread = jnp.mean(center * center, -1, keepdims=True)
    return center * lax.rsqrt(spread + layer_eps) * scale_row + shift_row


def norm_back(values, scale_row, shift_row, cotangent):
    outputs, pullback = jax.vjp(layer_norm, values, scale_row, shift_row)
    return pullback(cotangent)


def low(values):
    return lax.reduce_precision(values, exponent_bits=8, mantissa_bits=7)


def ein(spec, left, right):
    return jnp.einsum(spec, left, right, preferred_element_type=F32)


def split_two(values):
    high_part = low(values)
    return high_part.astype(BF), (values - high_part).astype(BF)


def ein_split(spec, left, right):
    high_part, low_part = split_two(left)
    return ein(spec, high_part, right) + ein(spec, low_part, right)


def ein_split_right(spec, left, right):
    high_part, low_part = split_two(right)
    return ein(spec, left, high_part) + ein(spec, left, low_part)


def exchange(values, axes):
    return lax.all_to_all(values, axes, split_axis=0, concat_axis=0, tiled=True)


def spread_to(values, axes, count):
    return exchange(jnp.broadcast_to(values[None], (count,) + values.shape), axes)


def group_swap(values, distance, count):
    return lax.ppermute(values, "grp", [(i, i ^ distance) for i in range(count)])


def group_shards(own, count):
    shards = [own]
    if count > 2:
        assert count == 4
        far = group_swap(own, 2, count)
        return [own, group_swap(own, 1, count), far, group_swap(far, 1, count)]
    if count == 2:
        shards.append(group_swap(own, 1, count))
    return shards


def lookup_kernel(width, table_block, table_steps, length_slots, codes, lens, table, place, out, rows, spots, stage):
    step = pl.program_id(0)

    @pl.when(step == 0)
    def first():
        spots[:, 0:width] = place[...].astype(BF).astype(F32).T

    @pl.when(step < table_steps)
    def turn():
        start = pl.multiple_of(step * table_block, table_block)
        rows[pl.ds(start, table_block), 0:width] = table[...].astype(BF).astype(F32).T

    @pl.when(step >= table_steps)
    def fetch():
        item = step - table_steps
        live = lens[item]
        unroll = 16

        def some(index, carry):
            for k in range(unroll):
                slot = index * unroll + k
                code = codes[item, slot]
                word = lax.shift_right_logical(code, 9)
                spot = jnp.bitwise_and(code, CODE - 1)
                stage[pl.ds(slot, 1), :] = rows[pl.ds(word, 1), :] + spots[pl.ds(spot, 1), :]
            return carry

        lax.fori_loop(0, pl.cdiv(live, unroll), some, 0)
        slots = lax.broadcasted_iota(jnp.int32, (length_slots, width), 0)
        out[0] = jnp.where(slots < live, stage[:, 0:width], 0.0).astype(BF)


def lookup(codes, lens, table, place):
    count, length_slots = codes.shape
    width, entries = table.shape
    table_block = 2048
    table_steps = pl.cdiv(entries, table_block)
    wide = pl.cdiv(width, LANES) * LANES
    import functools

    return pl.pallas_call(
        functools.partial(lookup_kernel, width, table_block, table_steps, length_slots),
        name="lookup",
        grid_spec=pltpu.PrefetchScalarGridSpec(
            num_scalar_prefetch=2,
            grid=(table_steps + count,),
            in_specs=[
                pl.BlockSpec((width, table_block), lambda i, c, n: (0, jnp.minimum(i, table_steps - 1))),
                pl.BlockSpec(place.shape, lambda i, c, n: (0, 0)),
            ],
            out_specs=pl.BlockSpec((1, length_slots, width), lambda i, c, n: (jnp.maximum(i - table_steps, 0), 0, 0)),
            scratch_shapes=[
                pltpu.VMEM((table_steps * table_block, wide), F32),
                pltpu.VMEM((place.shape[1], wide), F32),
                pltpu.VMEM((length_slots, wide), F32),
            ],
        ),
        out_shape=jax.ShapeDtypeStruct((count, length_slots, width), BF),
        compiler_params=pltpu.CompilerParams(vmem_limit_bytes=58 * MIB),
        cost_estimate=pl.CostEstimate(flops=0, transcendentals=0, bytes_accessed=60 * MIB),
    )(codes, lens, table, place)


def attend_kernel(heads, query_block, lens, block, out):
    live = lens[pl.program_id(0)]
    length_slots = block.shape[1]
    width = heads * HDIM

    @pl.loop(0, length_slots // query_block)
    def some(index):
        @pl.when(index * query_block < live)
        def work():
            start = pl.multiple_of(index * query_block, query_block)
            pieces = []
            for head in range(heads):
                query = block[0, pl.ds(start, query_block), head * HDIM : (head + 1) * HDIM]
                keys = block[0, :, width + head * HDIM : width + (head + 1) * HDIM]
                vals = block[0, :, 2 * width + head * HDIM : 2 * width + (head + 1) * HDIM]
                scores = lax.dot_general(
                    query, keys, (((1,), (1,)), ((), ())), preferred_element_type=F32
                ) * HDIM ** (-0.5)
                spots = lax.broadcasted_iota(jnp.int32, scores.shape, 1)
                scores = jnp.where(spots < live, scores, -1e30)
                shifted = jnp.exp(scores - jnp.max(scores, -1, keepdims=True))
                weights = shifted * (1.0 / jnp.sum(shifted, -1, keepdims=True))
                pieces.append(jnp.dot(weights.astype(BF), vals, preferred_element_type=F32))
            out[0, pl.ds(start, query_block), :] = jnp.concatenate(pieces, 1).astype(BF)

        @pl.when(index * query_block >= live)
        def blank():
            start = pl.multiple_of(index * query_block, query_block)
            out[0, pl.ds(start, query_block), :] = jnp.zeros((query_block, width), BF)


def attend_full(block, lens):
    import functools

    count, length_slots, three = block.shape
    width = three // 3
    return pl.pallas_call(
        functools.partial(attend_kernel, width // HDIM, 128),
        name="attend",
        grid_spec=pltpu.PrefetchScalarGridSpec(
            num_scalar_prefetch=1,
            grid=(count,),
            in_specs=[pl.BlockSpec((1, length_slots, three), lambda i, n: (i, 0, 0))],
            out_specs=pl.BlockSpec((1, length_slots, width), lambda i, n: (i, 0, 0)),
        ),
        out_shape=jax.ShapeDtypeStruct((count, length_slots, width), BF),
        compiler_params=pltpu.CompilerParams(vmem_limit_bytes=32 * MIB),
        cost_estimate=pl.CostEstimate(
            flops=count * 4 * length_slots * length_slots * width,
            transcendentals=count * length_slots * length_slots * width // HDIM,
            bytes_accessed=count * length_slots * four_of(width),
        ),
    )(lens, block)


def four_of(width):
    return 8 * width


def scatter_kernel(width, entries_pad, codes, lens, column, coef, emb, tops, out, spots_out, squares, acc, pacc, stage, sem):
    step = pl.program_id(0)
    length_slots = emb.shape[1]
    clear = 512

    @pl.when(step == 0)
    def first():
        @pl.loop(0, entries_pad // clear)
        def wipe(i):
            acc[pl.ds(pl.multiple_of(i * clear, clear), clear), :] = jnp.zeros((clear, LANES), F32)

        pacc[...] = jnp.zeros_like(pacc)
        stage[...] = jnp.zeros_like(stage)

    live = lens[step]
    mine = column[step]
    top = tops[0]
    top_high = top.astype(BF)
    top_low = (top - top_high.astype(F32)).astype(BF)
    chunk = 128
    unroll = 8
    for part in range(length_slots // chunk):

        @pl.when(part * chunk < live)
        def work():
            span = slice(part * chunk, (part + 1) * chunk)
            mix = coef[0, span, :]
            wide = mix.astype(F32)
            scale = wide[:, 25:26] + wide[:, 26:27]
            shift = wide[:, 27:28] + wide[:, 28:29]
            slope = wide[:, 29:30] + wide[:, 30:31]
            back = jnp.dot(mix, top_high, preferred_element_type=F32) + jnp.dot(
                mix, top_low, preferred_element_type=F32
            )
            stage[:, 0:width] = back * scale + shift - emb[0, span, :].astype(F32) * slope

            def some(index, carry):
                for k in range(unroll):
                    slot = index * unroll + k
                    code = codes[step, part * chunk + slot]
                    word = lax.shift_right_logical(code, 9)
                    acc[pl.ds(word, 1), :] += stage[pl.ds(slot, 1), :]
                return carry

            def place(index, carry):
                for k in range(unroll):
                    slot = index * unroll + k
                    code = codes[step, part * chunk + slot]
                    spot = jnp.bitwise_and(code, CODE - 1)
                    pacc[pl.ds(spot, 1), :] += stage[pl.ds(slot, 1), :]
                return carry

            rounds = pl.cdiv(jnp.minimum(live - part * chunk, chunk), unroll)
            lax.fori_loop(0, rounds, some, 0)
            lax.fori_loop(0, rounds * mine, place, 0)

    @pl.when(step == pl.num_programs(0) - 1)
    def last():
        copy = pltpu.make_async_copy(acc, out, sem)
        copy.start()
        spots_out[...] = pacc[...]

        def add(i, total):
            part = acc[pl.ds(pl.multiple_of(i * clear, clear), clear), :]
            return total + jnp.sum((part * part).reshape(clear // 8, 8, LANES), 0)

        squares[...] = lax.fori_loop(0, entries_pad // clear, add, jnp.zeros((8, LANES), F32))
        copy.wait()


def scatter(codes, lens, column, coef, emb, tops, entries, places):
    import functools

    count, length_slots, width = emb.shape
    entries_pad = pl.cdiv(entries, 512) * 512
    return pl.pallas_call(
        functools.partial(scatter_kernel, width, entries_pad),
        name="scatter_rows",
        grid_spec=pltpu.PrefetchScalarGridSpec(
            num_scalar_prefetch=3,
            grid=(count,),
            in_specs=[
                pl.BlockSpec((1, length_slots, COEF), lambda i, c, n, m: (i, 0, 0)),
                pl.BlockSpec((1, length_slots, width), lambda i, c, n, m: (i, 0, 0)),
                pl.BlockSpec((1, COEF, width), lambda i, c, n, m: (i, 0, 0)),
            ],
            out_specs=[
                pl.BlockSpec(memory_space=pl.ANY),
                pl.BlockSpec((places, LANES), lambda i, c, n, m: (0, 0)),
                pl.BlockSpec((8, LANES), lambda i, c, n, m: (0, 0)),
            ],
            scratch_shapes=[
                pltpu.VMEM((entries_pad, LANES), F32),
                pltpu.VMEM((places, LANES), F32),
                pltpu.VMEM((128, LANES), F32),
                pltpu.SemaphoreType.DMA,
            ],
        ),
        out_shape=[
            jax.ShapeDtypeStruct((entries_pad, LANES), F32),
            jax.ShapeDtypeStruct((places, LANES), F32),
            jax.ShapeDtypeStruct((8, LANES), F32),
        ],
        compiler_params=pltpu.CompilerParams(vmem_limit_bytes=40 * MIB),
        cost_estimate=pl.CostEstimate(flops=0, transcendentals=0, bytes_accessed=100 * MIB),
    )(codes, lens, column, coef, emb, tops)


def teacher_forward(embedded, attention, feedforward, pooler, vectors, lens, group_index, group_count):
    count, length_slots, model_width = embedded.shape
    local_width = attention.shape[-1]
    local_units = feedforward.shape[-1]
    spread_rows = local_units * group_count // model_width
    block_rows = 8 + spread_rows

    def side(layer):
        return attention[layer].transpose(1, 0, 2).reshape(model_width, 4 * local_width)

    sides = [group_shards(side(0), group_count)]
    wide = group_shards(feedforward[0, 0], group_count)
    narrow = group_shards(feedforward[0, 1], group_count)
    sides.append(group_shards(side(1), group_count))

    def part(row, shard, width):
        return lax.dynamic_slice_in_dim(row, jnp.bitwise_xor(group_index, shard) * width, width)

    state = layer_norm(embedded.astype(F32), vectors[0], vectors[1])
    block = vectors[2 : 2 + block_rows]
    state_low = state.astype(BF)
    joined = state + block[2]
    for shard in range(group_count):
        weight = sides[0][shard]
        bias = jnp.concatenate(
            [part(block[0], shard, local_width), jnp.zeros((local_width,), F32), part(block[1], shard, local_width)]
        )
        heads = (ein("sld,de->sle", state_low, weight[:, : 3 * local_width]) + bias).astype(BF)
        context = attend_full(heads, lens)
        joined = joined + ein("slc,dc->sld", context, weight[:, 3 * local_width :])
    hidden = layer_norm(joined, block[3], block[4])
    hidden_low = hidden.astype(BF)
    unit_bias = block[5 : 5 + spread_rows].reshape(-1)
    summed = hidden + block[5 + spread_rows]
    for shard in range(group_count):
        before = ein("sld,df->slf", hidden_low, wide[shard]) + part(unit_bias, shard, local_units)
        active = jax.nn.gelu(before, approximate=False).astype(BF)
        summed = summed + ein("slf,df->sld", active, narrow[shard])
    state = layer_norm(summed, block[6 + spread_rows], block[7 + spread_rows])
    block = vectors[2 + block_rows : 2 + 2 * block_rows]
    state_low = state.astype(BF)
    first = state[:, 0]
    first_low = state_low[:, 0]
    tops, querys = [], []
    for shard in range(group_count):
        weight = sides[1][shard]
        query = (ein("sd,de->se", first_low, weight[:, :local_width]) + part(block[0], shard, local_width)).astype(BF)
        key_weight = weight[:, local_width : 2 * local_width].reshape(model_width, -1, HDIM)
        tops.append(ein("shd,ehd->she", query.reshape(count, -1, HDIM), key_weight))
    weights = cls_weights(state_low, jnp.concatenate(tops, 1), lens)
    weights_low = weights.astype(BF)
    mass = jnp.sum(weights_low.astype(F32), -1)
    bars = ein("shl,sle->she", weights_low, state_low).reshape(count, group_count, -1, model_width)
    mass = mass.reshape(count, group_count, -1)
    joined = first + block[2]
    for shard in range(group_count):
        weight = sides[1][shard]
        val_weight = weight[:, 2 * local_width : 3 * local_width].reshape(model_width, -1, HDIM)
        context = ein_split("she,ehd->shd", bars[:, shard], val_weight)
        context = context + mass[:, shard, :, None] * part(block[1], shard, local_width).reshape(-1, HDIM)
        context = context.reshape(count, -1).astype(BF)
        joined = joined + ein("sc,dc->sd", context, weight[:, 3 * local_width :])
    hidden = layer_norm(joined, block[3], block[4])
    everyone = spread_to(hidden.astype(BF), "grp", group_count).reshape(-1, model_width)
    unit_bias = block[5 : 5 + spread_rows].reshape(-1)
    before = ein("sd,df->sf", everyone, feedforward[1, 0]) + part(unit_bias, 0, local_units)
    active = jax.nn.gelu(before, approximate=False).astype(BF)
    partial_rows = ein("sf,df->sd", active, feedforward[1, 1]).reshape(group_count, count, model_width)
    total = jnp.sum(exchange(partial_rows, "grp"), 0)
    summed = hidden + total + block[5 + spread_rows]
    cls = layer_norm(summed, block[6 + spread_rows], block[7 + spread_rows])
    pool = jnp.tanh(ein("sd,de->se", cls.astype(BF), pooler) + vectors[2 + 2 * block_rows])
    logits = ein("sd,cd->sc", pool.astype(BF), vectors[3 + 2 * block_rows :].astype(BF))
    return cls, logits


def cls_weights(state_low, tops, lens):
    scores = ein_split_right("sle,she->shl", state_low, tops) * HDIM ** (-0.5)
    valid = jnp.arange(state_low.shape[1])[None, None, :] < lens[:, None, None]
    scores = jnp.where(valid, scores, -1e30)
    shifted = jnp.exp(scores - jnp.max(scores, -1, keepdims=True))
    return shifted / jnp.sum(shifted, -1, keepdims=True)


class Halves:
    def __init__(self, swapped):
        self.swapped = swapped

    def order(self, pair, axis=-1):
        straight = jnp.concatenate(pair, axis)
        crossed = jnp.concatenate(pair[::-1], axis)
        return jnp.where(self.swapped, crossed, straight)

    def parts(self, values, axis=-1):
        first, second = jnp.split(values, 2, axis)
        return (
            jnp.where(self.swapped, second, first),
            jnp.where(self.swapped, first, second),
        )

    def forward(self, values, weight):
        return self.order([ein("sd,de->se", values, half) for half in weight])

    def backward(self, values, weight):
        pieces = self.parts(values)
        return sum(ein("se,de->sd", piece, half) for piece, half in zip(pieces, weight))

    def raise_heads(self, values, weight):
        count = values.shape[0]
        out = [
            ein("shd,ehd->she", piece.reshape(count, -1, HDIM), half.reshape(half.shape[0], -1, HDIM))
            for piece, half in zip(self.parts(values), weight)
        ]
        return self.order(out, 1)

    def lower_heads(self, values, weight):
        out = [
            ein_split("she,ehd->shd", piece, half.reshape(half.shape[0], -1, HDIM))
            for piece, half in zip(self.parts(values, 1), weight)
        ]
        return self.order(out, 1)


def student_forward(embedded, blocks, widen, narrow, small_rows, lens, halves):
    count, length_slots, model_width = embedded.shape
    spread_rows = 2 * widen[0].shape[1] // model_width
    query_weight, key_weight, val_weight, out_weight, pool_weight = blocks
    rows_in = embedded.astype(F32)
    mean = jnp.mean(rows_in, -1, keepdims=True)
    center = rows_in - mean
    rstd = lax.rsqrt(jnp.mean(center * center, -1, keepdims=True) + layer_eps)
    normal = center * rstd
    rows = normal * small_rows[0] + small_rows[1]
    rows_low = rows.astype(BF)
    query = (halves.forward(rows_low[:, 0], query_weight) + small_rows[2]).astype(BF)
    tops = halves.raise_heads(query, key_weight)
    weights = cls_weights(rows_low, tops, lens)
    weights_low = weights.astype(BF)
    mass = jnp.sum(weights_low.astype(F32), -1)
    bars = ein("shl,sle->she", weights_low, rows_low)
    context = halves.lower_heads(bars, val_weight) + mass[:, :, None] * small_rows[3].reshape(-1, HDIM)
    context_low = context.reshape(count, model_width).astype(BF)
    joined = rows[:, 0] + halves.forward(context_low, out_weight) + small_rows[4]
    hidden = layer_norm(joined, small_rows[5], small_rows[6])
    hidden_low = hidden.astype(BF)
    before = halves.forward(hidden_low, widen) + small_rows[7 : 7 + spread_rows].reshape(-1)
    active = jax.nn.gelu(before, approximate=False).astype(BF)
    summed = hidden + halves.forward(active, narrow) + small_rows[7 + spread_rows]
    vector = layer_norm(summed, small_rows[8 + spread_rows], small_rows[9 + spread_rows])
    return {
        "embedded": embedded,
        "normal_low": normal.astype(BF),
        "mean": mean[..., 0],
        "rstd": rstd[..., 0],
        "rows_low": rows_low,
        "query": query,
        "tops": tops,
        "weights": weights,
        "weights_low": weights_low,
        "mass": mass,
        "bars": bars,
        "context_low": context_low,
        "joined": joined,
        "hidden_low": hidden_low,
        "before": before,
        "active": active,
        "summed": summed,
        "vector": vector,
    }


def student_backward(state, blocks, widen, narrow, small_rows, lens, d_vector, halves):
    query_weight, key_weight, val_weight, out_weight, pool_weight = blocks
    count, length_slots, model_width = state["embedded"].shape
    spread_rows = 2 * widen[0].shape[1] // model_width
    head_count = model_width // HDIM
    scale = HDIM ** (-0.5)
    d_summed, d_gain_two, d_shift_two = norm_back(
        state["summed"], small_rows[8 + spread_rows], small_rows[9 + spread_rows], d_vector
    )
    d_output = d_summed.astype(BF)
    d_active = halves.backward(d_output, narrow)
    unused, gelu_pull = jax.vjp(lambda v: jax.nn.gelu(v, approximate=False), state["before"])
    d_before = gelu_pull(d_active)[0].astype(BF)
    d_hidden = d_summed + halves.backward(d_before, widen)
    d_joined, d_gain_one, d_shift_one = norm_back(state["joined"], small_rows[5], small_rows[6], d_hidden)
    d_branch = d_joined.astype(BF)
    d_context = halves.backward(d_branch, out_weight).astype(BF)
    val_tops = halves.raise_heads(d_context, val_weight)
    rows_low = state["rows_low"]
    weights, weights_low = state["weights"], state["weights_low"]
    d_heads = d_context.reshape(count, head_count, HDIM).astype(F32)
    constant = jnp.sum(d_heads * small_rows[3].reshape(head_count, HDIM), -1)
    d_weights = ein_split_right("sle,she->shl", rows_low, val_tops) + constant[..., None]
    d_scores = (weights * (d_weights - jnp.sum(weights * d_weights, -1, keepdims=True))).astype(BF)
    d_bars = ein("shl,sle->she", d_scores, rows_low)
    d_query = (halves.lower_heads(d_bars, key_weight) * scale).reshape(count, model_width).astype(BF)
    d_first = d_joined + halves.backward(d_query, query_weight)
    key_tops = state["tops"] * scale
    tops = jnp.concatenate([val_tops, key_tops, d_first[:, None]], 1)
    start = (jnp.arange(length_slots) == 0).astype(BF)
    coef = jnp.concatenate(
        [weights_low, d_scores, jnp.broadcast_to(start, (count, 1, length_slots))], 1
    )
    d_shift = jnp.einsum("sj,sje->e", jnp.sum(coef.astype(F32), -1), tops, precision=highest)
    normal_bars = ein("sjl,sle->sje", coef, state["normal_low"])
    d_gain = jnp.sum(normal_bars * tops, (0, 1))
    scaled = tops * small_rows[0]
    scaled_sum = jnp.sum(scaled, -1)
    along = ein_split_right("sle,sje->sjl", state["embedded"], scaled)
    mean, rstd = state["mean"], state["rstd"]
    wide = coef.astype(F32)
    slope = rstd * rstd * rstd / model_width * jnp.sum(wide * (along - mean[:, None] * scaled_sum[..., None]), 1)
    shift = mean * slope - rstd / model_width * jnp.sum(wide * scaled_sum[..., None], 1)
    extras = []
    for values in (rstd, shift, slope):
        extras.extend(split_two(values))
    extras.append(jnp.zeros_like(extras[0]))
    packed = jnp.concatenate([coef, jnp.stack(extras, 1)], 1)
    valid = jnp.arange(length_slots)[None, None, :] < lens[:, None, None]
    packed = jnp.where(valid, packed, jnp.zeros_like(packed)).transpose(0, 2, 1)
    d_val_bias = jnp.sum(d_heads * state["mass"][..., None], 0).reshape(model_width)
    head_rows = jnp.stack(
        [
            d_gain,
            d_shift,
            jnp.sum(d_query.astype(F32), 0),
            d_val_bias,
            jnp.sum(d_branch.astype(F32), 0),
            d_gain_one,
            d_shift_one,
        ]
    )
    unit_rows = jnp.sum(d_before.astype(F32), 0).reshape(spread_rows, model_width)
    tail_rows = jnp.stack([jnp.sum(d_output.astype(F32), 0), d_gain_two, d_shift_two])
    return {
        "packed": packed,
        "scaled": scaled,
        "d_bars": d_bars,
        "d_query": d_query,
        "d_context": d_context,
        "d_branch": d_branch,
        "d_before": d_before,
        "d_output": d_output,
        "layer_rows": jnp.concatenate([head_rows, unit_rows, tail_rows], 0),
    }


def sequence_loss(logits, first_vector, teacher_cls, teacher_logits, labels, total_count):
    log_probs = jax.nn.log_softmax(logits, -1)
    hard_loss = -jnp.sum(jnp.where(jnp.arange(logits.shape[1]) == labels[:, None], log_probs, 0.0), -1)
    teacher_soft = jax.nn.log_softmax(teacher_logits / temper, -1)
    student_soft = jax.nn.log_softmax(logits / temper, -1)
    divergence = jnp.sum(jnp.exp(teacher_soft) * (teacher_soft - student_soft), -1)
    student_unit = first_vector * lax.rsqrt(jnp.sum(first_vector * first_vector, -1, keepdims=True) + dist_eps)
    teacher_unit = teacher_cls * lax.rsqrt(jnp.sum(teacher_cls * teacher_cls, -1, keepdims=True) + dist_eps)
    distance = jnp.sum((student_unit - teacher_unit) ** 2, -1)
    return jnp.sum(hard_loss + temper * temper * divergence + 100.0 * distance) / total_count


def adam_update(weight, moment_one, moment_two, gradient, factor):
    gradient = gradient * factor
    first_new = beta_one * moment_one + (1.0 - beta_one) * gradient
    second_new = beta_two * moment_two + (1.0 - beta_two) * gradient * gradient
    first_hat = first_new / (1.0 - beta_one**adam_steps)
    second_hat = second_new / (1.0 - beta_two**adam_steps)
    weight_new = weight - learn_rate * (first_hat / (jnp.sqrt(second_hat) + adam_eps) + decay_rate * weight)
    return (weight_new, first_new, second_new)


def on_device(
    tokens,
    positions,
    lengths,
    labels,
    word_table,
    word_first,
    word_second,
    place_table,
    place_first,
    place_second,
    square_weights,
    square_first,
    square_second,
    widen_weights,
    widen_first,
    widen_second,
    narrow_weights,
    narrow_first,
    narrow_second,
    small_params,
    small_first,
    small_second,
    class_bias,
    class_first,
    class_second,
    teacher_word,
    teacher_place,
    teacher_attention,
    teacher_feedforward,
    teacher_pooler,
    teacher_vectors,
):
    shards = lax.axis_size("fsdp")
    groups = lax.axis_size("grp")
    shard_index = lax.axis_index("fsdp")
    group_index = lax.axis_index("grp")
    count, length_slots = tokens.shape
    model_width = small_params.shape[1]
    own_rows = word_table.shape[0]
    entries = word_table.shape[1]
    places = place_table.shape[1]
    spread_rows = widen_weights.shape[1] // model_width
    classes = class_bias.shape[0]
    head_count = model_width // HDIM
    total_count = count * shards * groups

    message = jnp.concatenate(
        [tokens * CODE + positions, lengths[:, None], jnp.zeros((count, LANES - 1), jnp.int32)], 1
    )
    everyone = spread_to(message, ALL, shards * groups).reshape(shards, groups, count, -1)
    grid_codes, grid_lens = everyone[..., :length_slots], everyone[..., length_slots]
    row_codes = lax.dynamic_index_in_dim(grid_codes, shard_index, 0, False).reshape(-1, length_slots)
    row_lens = lax.dynamic_index_in_dim(grid_lens, shard_index, 0, False).reshape(-1)
    column_codes = lax.dynamic_index_in_dim(grid_codes, group_index, 1, False).reshape(-1, length_slots)
    column_lens = lax.dynamic_index_in_dim(grid_lens, group_index, 1, False).reshape(-1)

    core = jnp.bitwise_and(group_index, 1)
    halves = Halves(core == 1)
    half = model_width // 2

    def my_half(values):
        return lax.dynamic_index_in_dim(values.reshape(values.shape[0], -1, 2, half), core, 2, False)

    unit_half = spread_rows * half
    widen_half = lax.dynamic_index_in_dim(widen_weights.reshape(own_rows, 2, unit_half), core, 1, False)
    side = jnp.concatenate([my_half(square_weights).reshape(own_rows, -1), widen_half], 1).astype(BF)
    side_own = lax.all_gather(side, "fsdp", axis=0, tiled=True)
    narrow_own = lax.all_gather(my_half(narrow_weights)[:, 0].astype(BF), "fsdp", axis=0, tiled=True)
    side_pair = [side_own, group_swap(side_own, 1, groups)]
    narrow = [narrow_own, group_swap(narrow_own, 1, groups)]
    blocks = [[piece[:, i * half : (i + 1) * half] for piece in side_pair] for i in range(5)]
    widen = [piece[:, 5 * half :] for piece in side_pair]

    teacher_slices = lookup(row_codes, row_lens, teacher_word, teacher_place)
    teacher_embedded = lax.all_to_all(teacher_slices, "grp", split_axis=0, concat_axis=2, tiled=True)
    student_slices = lookup(column_codes, column_lens, word_table, place_table)
    embedded = lax.all_to_all(student_slices, "fsdp", split_axis=0, concat_axis=2, tiled=True)
    group_slices = lax.all_gather(student_slices.reshape(-1, length_slots * own_rows), "grp", axis=0, tiled=True)
    group_slices = group_slices.reshape(-1, length_slots, own_rows)

    teacher_cls, teacher_logits = teacher_forward(
        teacher_embedded,
        teacher_attention,
        teacher_feedforward,
        teacher_pooler,
        teacher_vectors,
        lengths,
        group_index,
        groups,
    )
    state = student_forward(embedded, blocks, widen, narrow, small_params, lengths, halves)
    vector = state["vector"]
    vector_low = vector.astype(BF)
    pooled = jnp.tanh(halves.forward(vector_low, blocks[4]) + small_params[10 + spread_rows])
    pooled_low = pooled.astype(BF)
    class_rows = small_params[11 + spread_rows :].astype(BF)
    logits = ein("sd,cd->sc", pooled_low, class_rows) + class_bias
    loss_part, loss_pull = jax.vjp(
        lambda logit_rows, vector_rows: sequence_loss(
            logit_rows, vector_rows, teacher_cls, teacher_logits, labels, total_count
        ),
        logits,
        vector,
    )
    d_logits, d_vector = loss_pull(jnp.ones_like(loss_part))
    d_class_rows = jnp.einsum("sc,sd->cd", d_logits, pooled_low.astype(F32), precision=highest)
    d_class_bias = jnp.sum(d_logits, 0)
    d_pooled = jnp.einsum("sc,cd->sd", d_logits, class_rows.astype(F32), precision=highest)
    d_pre_pool = d_pooled * (1.0 - pooled * pooled)
    pool_high, pool_rest = low(d_pre_pool), d_pre_pool - low(d_pre_pool)
    pool_mid = low(pool_rest)
    pool_terms = jnp.concatenate([pool_high, pool_mid, pool_rest - pool_mid], 0).astype(BF)
    back_terms = halves.backward(pool_terms, blocks[4]).reshape(3, count, model_width)
    d_vector = d_vector + jnp.sum(back_terms, 0)
    grads = student_backward(state, blocks, widen, narrow, small_params, lengths, d_vector, halves)

    def to_rows(values):
        return jnp.moveaxis(values.reshape(values.shape[:-1] + (shards, -1)), -2, 0)

    left = jnp.concatenate(
        [
            state["rows_low"][:, :1].astype(F32),
            state["bars"],
            grads["d_bars"],
            state["context_low"][:, None].astype(F32),
            state["hidden_low"][:, None].astype(F32),
            vector_low[:, None].astype(F32),
            grads["scaled"],
        ],
        1,
    )
    left = to_rows(left)
    active = to_rows(state["active"].astype(F32)[:, None]).reshape(shards, count, spread_rows, own_rows)
    right = jnp.concatenate(
        [
            grads["d_query"].astype(F32),
            state["query"].astype(F32),
            grads["d_context"].astype(F32),
            grads["d_branch"].astype(F32),
            d_pre_pool,
            grads["d_before"].astype(F32),
            grads["d_output"].astype(F32),
        ],
        1,
    )
    small_grad = jnp.concatenate([grads["layer_rows"], jnp.sum(d_pre_pool, 0)[None], d_class_rows], 0)
    scalars = jnp.concatenate([d_class_bias, loss_part[None], jnp.zeros((own_rows - classes - 1,), F32)])
    small_part = jnp.concatenate(
        [to_rows(small_grad), jnp.broadcast_to(scalars, (shards, 1, own_rows))], 1
    )
    left_count = left.shape[2]
    payload = jnp.concatenate(
        [
            left.reshape(shards, -1),
            active.reshape(shards, -1),
            small_part.reshape(shards, -1),
            jnp.broadcast_to(right.reshape(-1), (shards, right.size)),
        ],
        1,
    )
    payload = exchange(payload, "fsdp")
    packed = spread_to(grads["packed"].reshape(count * length_slots // 4, 4 * COEF), "fsdp", shards)

    def group_gather(values):
        pieces = group_shards(values, groups)
        return jnp.stack(pieces)

    payload = group_gather(payload)
    packed = group_gather(packed)
    sizes = [
        count * left_count * own_rows,
        count * spread_rows * own_rows,
        small_part[0].size,
        right.size,
    ]
    pieces, start = [], 0
    for size in sizes:
        pieces.append(payload[..., start : start + size])
        start += size
    seqs = groups * shards * count
    left = pieces[0].reshape(seqs, left_count, own_rows)
    active = pieces[1].reshape(seqs, spread_rows * own_rows)
    order = jnp.bitwise_xor(jnp.arange(groups), group_index)
    small_parts = pieces[2].reshape(groups, shards, -1, own_rows)
    small_parts = jnp.take(small_parts, order, axis=0)
    small_slice = jnp.sum(small_parts, (0, 1))
    right = pieces[3].reshape(seqs, -1)
    names = ["d_query", "query", "d_context", "d_branch", "d_pool"]
    rights = {name: right[:, i * model_width : (i + 1) * model_width] for i, name in enumerate(names)}
    d_before = right[:, 5 * model_width : (5 + spread_rows) * model_width]
    d_output = right[:, (5 + spread_rows) * model_width :]
    h = head_count
    first_rows, bars, d_bars = left[:, 0], left[:, 1 : 1 + h], left[:, 1 + h : 1 + 2 * h]
    context_rows, hidden_rows, vector_rows = (left[:, 1 + 2 * h + i] for i in range(3))
    tops = left[:, 4 + 2 * h :]

    seq_order = (order[:, None] * (shards * count) + jnp.arange(shards * count)[None]).reshape(-1)

    def sort_seqs(values):
        return jnp.take(values, seq_order, axis=0)

    def outer(left_rows, right_rows):
        return ein("sf,sd->fd", sort_seqs(left_rows).astype(BF), sort_seqs(right_rows).astype(BF))

    def outer_heads(left_rows, right_rows):
        right_rows = sort_seqs(right_rows).reshape(seqs, h, HDIM).astype(BF)
        return ein_split("shf,shd->fhd", sort_seqs(left_rows), right_rows).reshape(own_rows, -1)

    square_grad = jnp.concatenate(
        [
            outer(first_rows, rights["d_query"]),
            outer_heads(d_bars, rights["query"]) * HDIM ** (-0.5),
            outer_heads(bars, rights["d_context"]),
            outer(context_rows, rights["d_branch"]),
            jnp.einsum("sf,sd->fd", sort_seqs(vector_rows), sort_seqs(rights["d_pool"]), precision=highest),
        ],
        1,
    )
    widen_grad = outer(hidden_rows, d_before)
    narrow_grad = outer(active, d_output)

    grid_order = grid_codes.transpose(1, 0, 2, 3).reshape(seqs, length_slots)
    grid_order_lens = grid_lens.transpose(1, 0, 2).reshape(seqs)
    packed = packed.reshape(seqs, length_slots, COEF)
    packed = sort_seqs(packed)
    tops = jnp.concatenate([tops, jnp.zeros((seqs, COEF - tops.shape[1], own_rows), F32)], 1)
    tops = sort_seqs(tops)
    column = (jnp.arange(seqs) // (shards * count) == group_index).astype(jnp.int32)
    word_grad, place_part, word_squares = scatter(
        grid_order, grid_order_lens, column, packed, group_slices, tops, entries, places
    )
    word_grad = word_grad[:entries, :own_rows].T
    place_grad = jnp.sum(spread_to(place_part, "grp", groups), 0)[:, :own_rows].T

    local_square = (
        jnp.sum(square_grad * square_grad)
        + jnp.sum(widen_grad * widen_grad)
        + jnp.sum(narrow_grad * narrow_grad)
        + jnp.sum(word_squares)
        + jnp.sum(place_grad * place_grad)
    )
    last = jnp.concatenate([small_slice, jnp.broadcast_to(local_square, (1, own_rows))], 0)
    last = spread_to(last, "fsdp", shards)
    rows_all = small_params.shape[0]
    small_grad = jnp.moveaxis(last[:, :rows_all], 0, 1).reshape(rows_all, model_width)
    bias_grad = last[0, rows_all, :classes]
    total_loss = last[0, rows_all, classes]
    total_square = jnp.sum(last[:, rows_all + 1, 0])
    total_square = total_square + jnp.sum(small_grad * small_grad) + jnp.sum(bias_grad * bias_grad)
    gradient_norm = jnp.sqrt(total_square)
    factor = jnp.minimum(1.0, clip_bound / gradient_norm)
    results = [total_loss, gradient_norm]
    for weight, moment_one, moment_two, gradient in (
        (word_table, word_first, word_second, word_grad),
        (place_table, place_first, place_second, place_grad),
        (square_weights, square_first, square_second, square_grad),
        (widen_weights, widen_first, widen_second, widen_grad),
        (narrow_weights, narrow_first, narrow_second, narrow_grad),
        (small_params, small_first, small_second, small_grad),
        (class_bias, class_first, class_second, bias_grad),
    ):
        results.extend(adam_update(weight, moment_one, moment_two, gradient, factor))
    return tuple(results)


def solution(mesh):
    rows = P("fsdp", None)
    seqs = P(("fsdp", "grp"))
    table = [rows] * 15
    placed = (
        [P(("fsdp", "grp"), None)] * 2
        + [seqs] * 2
        + table
        + [P()] * 6
        + [P("grp", None)] * 2
        + [P(None, None, None, "grp")] * 2
        + [P()] * 2
    )
    return jax.shard_map(
        on_device,
        mesh=mesh,
        in_specs=tuple(placed),
        out_specs=tuple([P(), P()] + table + [P()] * 6),
        check_vma=False,
    )
```

```python
import functools

import jax
import jax.numpy as jnp
from jax import lax
from jax.experimental import pallas as pl
from jax.experimental.pallas import tpu as pltpu
from jax.sharding import PartitionSpec as P

HDIM = 64
BF = jnp.bfloat16
F32 = jnp.float32
ALL = ("fsdp", "grp")
MIB = 2**20

highest = lax.Precision.HIGHEST
layer_eps = 1e-06
dist_eps = 1e-06
temper = 10.0
beta_one = 0.9
beta_two = 0.999
learn_rate = 0.05
decay_rate = 0.01
adam_eps = 1e-08
adam_steps = 10
clip_bound = 1.0
LANES = 128
CODE = 512
COEF = 32
LAST_KEY = 2**30


def layer_norm(values, scale_row, shift_row):
    center = values - jnp.mean(values, -1, keepdims=True)
    spread = jnp.mean(center * center, -1, keepdims=True)
    return center * lax.rsqrt(spread + layer_eps) * scale_row + shift_row


def norm_back(values, scale_row, shift_row, cotangent):
    outputs, pullback = jax.vjp(layer_norm, values, scale_row, shift_row)
    return pullback(cotangent)


def low(values):
    return lax.reduce_precision(values, exponent_bits=8, mantissa_bits=7)


def ein(spec, left, right):
    return jnp.einsum(spec, left, right, preferred_element_type=F32)


def split_two(values):
    high_part = low(values)
    return high_part.astype(BF), (values - high_part).astype(BF)


def ein_split(spec, left, right):
    high_part, low_part = split_two(left)
    return ein(spec, high_part, right) + ein(spec, low_part, right)


def ein_split_right(spec, left, right):
    high_part, low_part = split_two(right)
    return ein(spec, left, high_part) + ein(spec, left, low_part)


def half_of(entries):
    return pl.cdiv(entries, 4096) * 2048


def small_cost():
    return pl.CostEstimate(flops=0, transcendentals=0, bytes_accessed=MIB)


def exchange(values, axes):
    return lax.all_to_all(values, axes, split_axis=0, concat_axis=0, tiled=True)


def spread_to(values, axes, count):
    return exchange(jnp.broadcast_to(values[None], (count,) + values.shape), axes)


def group_swap(values, distance, count):
    return lax.ppermute(values, "grp", [(i, i ^ distance) for i in range(count)])


def group_shards(own, count):
    shards = [own]
    if count > 2:
        assert count == 4
        far = group_swap(own, 2, count)
        return [own, group_swap(own, 1, count), far, group_swap(far, 1, count)]
    if count == 2:
        shards.append(group_swap(own, 1, count))
    return shards


def lookup_kernel(width, table_block, table_steps, length_slots, codes, lens, table, place, out, rows, spots, stage):
    step = pl.program_id(0)

    @pl.when(step == 0)
    def first():
        spots[:, 0:width] = place[...].astype(BF).astype(F32).T

    @pl.when(step < table_steps)
    def turn():
        start = pl.multiple_of(step * table_block, table_block)
        rows[pl.ds(start, table_block), 0:width] = table[...].astype(BF).astype(F32).T

    @pl.when(step >= table_steps)
    def fetch():
        item = step - table_steps
        live = lens[item]
        unroll = 16

        def some(index, carry):
            for k in range(unroll):
                slot = index * unroll + k
                code = codes[item, slot]
                word = lax.shift_right_logical(code, 9)
                spot = jnp.bitwise_and(code, CODE - 1)
                stage[pl.ds(slot, 1), :] = rows[pl.ds(word, 1), :] + spots[pl.ds(spot, 1), :]
            return carry

        lax.fori_loop(0, pl.cdiv(live, unroll), some, 0)
        slots = lax.broadcasted_iota(jnp.int32, stage.shape, 0)
        out[0] = jnp.where(slots < live, stage[...], 0.0).T[0:width].astype(BF)


def lookup(codes, lens, table, place):
    count, length_slots = codes.shape
    width, entries = table.shape
    table_block = 2048
    table_steps = pl.cdiv(entries, table_block)
    wide = pl.cdiv(width, LANES) * LANES
    return pl.pallas_call(
        functools.partial(lookup_kernel, width, table_block, table_steps, length_slots),
        name="lookup",
        grid_spec=pltpu.PrefetchScalarGridSpec(
            num_scalar_prefetch=2,
            grid=(table_steps + count,),
            in_specs=[
                pl.BlockSpec((width, table_block), lambda i, c, n: (0, jnp.minimum(i, table_steps - 1))),
                pl.BlockSpec(place.shape, lambda i, c, n: (0, 0)),
            ],
            out_specs=pl.BlockSpec((1, width, length_slots), lambda i, c, n: (jnp.maximum(i - table_steps, 0), 0, 0)),
            scratch_shapes=[
                pltpu.VMEM((table_steps * table_block, wide), F32),
                pltpu.VMEM((place.shape[1], wide), F32),
                pltpu.VMEM((length_slots, wide), F32),
            ],
        ),
        out_shape=jax.ShapeDtypeStruct((count, width, length_slots), BF),
        compiler_params=pltpu.CompilerParams(vmem_limit_bytes=58 * MIB),
        cost_estimate=small_cost(),
    )(codes, lens, table, place)


def two_terms(values):
    high_part = values.astype(BF)
    return high_part, (values - high_part.astype(F32)).astype(BF)


def row_gradients(b, message, emb, stage):
    own_rows = emb.shape[1]
    mix = message[0, b]
    extra = mix.astype(F32)
    tops = message[0, message.shape[1] - 1]
    both = tops[:, b * 2 * LANES : (b + 1) * 2 * LANES]
    back = lax.dot_general(both, mix, (((0,), (0,)), ((), ())), preferred_element_type=F32)
    back = back[:LANES] + back[LANES:]
    scale = extra[13:14] + extra[14:15]
    shift = extra[28:29] + extra[29:30]
    slope = extra[30:31] + extra[31:32]
    rows = back[:own_rows] * scale + shift - emb[b].astype(F32) * slope
    if own_rows < LANES:
        rows = jnp.concatenate([rows, jnp.zeros((LANES - own_rows, rows.shape[1]), F32)], 0)
    stage[...] = rows.T


def add_rows(live, base, row_of, codes, stage, acc):
    unroll = 16

    def some(index, carry):
        for k in range(unroll):
            slot = index * unroll + k
            acc[pl.ds(row_of(codes[base + slot]), 1), :] += stage[pl.ds(slot, 1), :]
        return carry

    lax.fori_loop(0, pl.cdiv(live, unroll), some, 0)


def scatter_kernel(half_entries, codes, facts, core, message, emb, out, squares, acc, stage, sem):
    step = pl.program_id(0)
    count, own_rows, length_slots = emb.shape
    clear = 512
    unroll = 16

    @pl.when(step == 0)
    def first():
        @pl.loop(0, half_entries // clear)
        def wipe(i):
            acc[pl.ds(pl.multiple_of(i * clear, clear), clear), :] = jnp.zeros((clear, LANES), F32)

    low_word = core[0] * half_entries

    def add_row(base, slot):
        word = lax.shift_right_logical(codes[base + slot], 9) - low_word
        acc[pl.ds(word, 1), :] += stage[pl.ds(slot, 1), :]

    for b in range(count):
        item = step * count + b
        base = item * length_slots
        row_gradients(b, message, emb, stage)
        middle = 1 + facts[1, item]
        start = jnp.where(core[0] == 0, 1, middle)
        end = jnp.where(core[0] == 0, middle, facts[0, item])
        word = lax.shift_right_logical(codes[base], 9)

        @pl.when((word >= low_word) & (word < low_word + half_entries))
        def first_slot():
            add_row(base, 0)

        def some(index, carry):
            for k in range(unroll):
                add_row(base, start + index * unroll + k)
            return carry

        def one(slot, carry):
            add_row(base, slot)
            return carry

        whole = (end - start) // unroll
        lax.fori_loop(0, whole, some, 0)
        lax.fori_loop(start + whole * unroll, end, one, 0)

    @pl.when(step == pl.num_programs(0) - 1)
    def last():
        copy = pltpu.make_async_copy(acc, out, sem)
        copy.start()

        def add(i, total):
            part = acc[pl.ds(pl.multiple_of(i * clear, clear), clear), :]
            return total + jnp.sum((part * part).reshape(clear // 8, 8, LANES), 0)

        squares[...] = lax.fori_loop(0, half_entries // clear, add, jnp.zeros((8, LANES), F32))
        copy.wait()


def place_kernel(codes, lens, message, emb, out, stage):
    step = pl.program_id(0)
    count, own_rows, length_slots = emb.shape

    @pl.when(step == 0)
    def first():
        out[...] = jnp.zeros_like(out)

    for b in range(count):
        item = step * count + b
        row_gradients(b, message, emb, stage)
        add_rows(lens[item], item * length_slots, lambda code: jnp.bitwise_and(code, CODE - 1), codes, stage, out)


def row_specs(message, emb, count):
    return [
        pl.BlockSpec((1,) + message.shape[1:], lambda i, *scalars: (i, 0, 0, 0)),
        pl.BlockSpec((count,) + emb.shape[1:], lambda i, *scalars: (i, 0, 0)),
    ]


def scatter(codes, facts, core, message, emb, half_entries):
    count = message.shape[1] - 1
    length_slots = emb.shape[2]
    return pl.pallas_call(
        functools.partial(scatter_kernel, half_entries),
        name="scatter_rows",
        grid_spec=pltpu.PrefetchScalarGridSpec(
            num_scalar_prefetch=3,
            grid=(message.shape[0],),
            in_specs=row_specs(message, emb, count),
            out_specs=[
                pl.BlockSpec(memory_space=pl.ANY),
                pl.BlockSpec((8, LANES), lambda i, *scalars: (0, 0)),
            ],
            scratch_shapes=[
                pltpu.VMEM((half_entries, LANES), F32),
                pltpu.VMEM((length_slots, LANES), F32),
                pltpu.SemaphoreType.DMA,
            ],
        ),
        out_shape=[
            jax.ShapeDtypeStruct((half_entries, LANES), F32),
            jax.ShapeDtypeStruct((8, LANES), F32),
        ],
        compiler_params=pltpu.CompilerParams(vmem_limit_bytes=40 * MIB),
        cost_estimate=small_cost(),
    )(codes, facts, core.reshape(1), message, emb)


def place_sums(codes, lens, message, emb, places):
    count = message.shape[1] - 1
    length_slots = emb.shape[2]
    return pl.pallas_call(
        place_kernel,
        name="place_rows",
        grid_spec=pltpu.PrefetchScalarGridSpec(
            num_scalar_prefetch=2,
            grid=(message.shape[0],),
            in_specs=row_specs(message, emb, count),
            out_specs=pl.BlockSpec((places, LANES), lambda i, *scalars: (0, 0)),
            scratch_shapes=[pltpu.VMEM((length_slots, LANES), F32)],
        ),
        out_shape=jax.ShapeDtypeStruct((places, LANES), F32),
        compiler_params=pltpu.CompilerParams(vmem_limit_bytes=16 * MIB),
        cost_estimate=small_cost(),
    )(codes, lens, message, emb)


def adam_kernel(width, half_steps, factor, core, own, other, weight, first, second, new_weight, new_first, new_second):
    mine = (pl.program_id(0) // half_steps) == core[0]
    rows = jnp.where(mine, own[...], other[...]).T[0:width]
    out = adam_update(weight[...], first[...], second[...], rows, factor[0])
    new_weight[...], new_first[...], new_second[...] = out


def adam_table(factor, core, own, other, weight, first, second):
    width, entries = weight.shape
    block = 2048
    half_steps = own.shape[0] // block
    spec = pl.BlockSpec((width, block), lambda i, f, c: (0, i))

    def half_spec(flip):
        def index(i, f, c):
            start = jnp.bitwise_xor(c[0], flip) * half_steps
            return (jnp.clip(i - start, 0, half_steps - 1), 0)

        return pl.BlockSpec((block, LANES), index)

    return pl.pallas_call(
        functools.partial(adam_kernel, width, half_steps),
        name="adam_table",
        grid_spec=pltpu.PrefetchScalarGridSpec(
            num_scalar_prefetch=2,
            grid=(pl.cdiv(entries, block),),
            in_specs=[half_spec(0), half_spec(1), spec, spec, spec],
            out_specs=[spec, spec, spec],
        ),
        out_shape=[jax.ShapeDtypeStruct(weight.shape, F32)] * 3,
        compiler_params=pltpu.CompilerParams(vmem_limit_bytes=40 * MIB),
        cost_estimate=small_cost(),
    )(factor.reshape(1), core.reshape(1), own, other, weight, first, second)


def attention_kernel(lens, embedded, shard_bias, vectors, *rest):
    groups, _, width, length_slots = embedded.shape
    weights, (hidden_out, rows, rows_low, heads, context) = rest[:groups], rest[groups:]
    live = lens[pl.program_id(0)]
    big, small = 256, 128

    def over_blocks(block, work, blank):
        @pl.loop(0, length_slots // block)
        def one(index):
            span = pl.ds(pl.multiple_of(index * block, block), block)
            pl.when(index * block < live)(lambda: work(span))
            pl.when(index * block >= live)(lambda: blank(span))

    def norm_in(span):
        values = jnp.concatenate([embedded[g, 0, :, span].astype(F32) for g in range(groups)], 0).T
        state = normalise(values)[0] * vectors[0:1, :] + vectors[1:2, :]
        rows[span, :] = state
        rows_low[span, :] = state.astype(BF)

    def no_rows(span):
        rows_low[span, :] = jnp.zeros((small, groups * width), BF)

    over_blocks(small, norm_in, no_rows)
    for shard in range(groups):
        weight = weights[shard]

        def project(span):
            values = rows_low[span, :]
            heads[0, span, :] = (mm_t(values, weight[0]) + shard_bias[shard, 0:1, 0:width]).astype(BF)
            heads[1, span, :] = mm_t(values, weight[1]).astype(BF)
            heads[2, span, :] = (mm_t(values, weight[2]) + shard_bias[shard, 1:2, 0:width]).astype(BF)

        def no_heads(span):
            for i in range(3):
                heads[i, span, :] = jnp.zeros((big, width), BF)

        over_blocks(big, project, no_heads)

        def attend(span):
            pieces = []
            for head in range(width // HDIM):
                part = slice(head * HDIM, (head + 1) * HDIM)
                scores = mm_t(heads[0, span, part], heads[1, :, part]) * HDIM ** (-0.5)
                spots = lax.broadcasted_iota(jnp.int32, scores.shape, 1)
                scores = jnp.where(spots < live, scores, -1e30)
                shifted = jnp.exp(scores - jnp.max(scores, -1, keepdims=True))
                prob = shifted * (1.0 / jnp.sum(shifted, -1, keepdims=True))
                pieces.append(mm(prob.astype(BF), heads[2, :, part]))
            context[shard, span, :] = jnp.concatenate(pieces, 1).astype(BF)

        def no_context(span):
            context[shard, span, :] = jnp.zeros((small, width), BF)

        over_blocks(small, attend, no_context)

    def join(span):
        joined = rows[span, :] + vectors[4:5, :]
        for shard in range(groups):
            joined = joined + mm(context[shard, span, :], weights[shard][3])
        hidden_out[0, span, :] = normalise(joined)[0] * vectors[5:6, :] + vectors[6:7, :]

    def no_hidden(span):
        hidden_out[0, span, :] = jnp.zeros((big, groups * width), F32)

    over_blocks(big, join, no_hidden)


def feed_kernel(spread_rows, block, lens, hidden, shard_bias, vectors, *rest):
    groups = (len(rest) - 2) // 2
    wides, narrows, (state_low, first) = rest[:groups], rest[groups : 2 * groups], rest[2 * groups :]
    _, length_slots, model_width = hidden.shape
    live = lens[pl.program_id(0)]
    tail = 2 + 5 + spread_rows

    @pl.loop(0, length_slots // block)
    def one(index):
        span = pl.ds(pl.multiple_of(index * block, block), block)

        @pl.when(index * block < live)
        def work():
            rows = hidden[0, span, :]
            rows_low = rows.astype(BF)
            summed = rows + vectors[tail : tail + 1, :]
            for shard in range(groups):
                before = mm(rows_low, wides[shard][...]) + shard_bias[shard, 4:5, :]
                active = (before * phi(before)).astype(BF)
                summed = summed + mm_t(active, narrows[shard][...])
            state = normalise(summed)[0] * vectors[tail + 1 : tail + 2, :] + vectors[tail + 2 : tail + 3, :]
            state_low[0, span, :] = state.astype(BF)

            @pl.when(index == 0)
            def keep():
                first[0] = state[0:8, :]

        @pl.when(index * block >= live)
        def blank():
            state_low[0, span, :] = jnp.zeros((block, model_width), BF)


def cls_kernel(spread_rows, lens, state_low, first, shard_bias, vectors, *rest):
    groups = len(rest) - 1
    weights, hidden_out = rest[:groups], rest[groups]
    count, length_slots, model_width = state_low.shape
    width = model_width // groups
    shard_heads = width // HDIM
    base = 2 + 8 + spread_rows
    head_rows = 8
    head_mask = (
        lax.broadcasted_iota(jnp.int32, (head_rows, width), 0)
        == lax.broadcasted_iota(jnp.int32, (head_rows, width), 1) // HDIM
    ).astype(F32)
    starts = jnp.concatenate([first[b, 0:1, :] for b in range(count)], 0)
    starts_low = starts.astype(BF)
    tops = []
    for shard in range(groups):
        query = (mm_t(starts_low, weights[shard][0]) + shard_bias[shard, 2:3, 0:width]).astype(BF).astype(F32)
        spread = jnp.concatenate(
            [jnp.broadcast_to(query[b : b + 1], head_mask.shape) * head_mask for b in range(count)], 0
        )
        tops.append(mm(spread.astype(BF), weights[shard][1]))
    bars, masses = [], []
    all_rows = groups * head_rows
    slot_index = lax.broadcasted_iota(jnp.int32, (all_rows, length_slots), 1)
    for b in range(count):
        own = jnp.concatenate([top[b * head_rows : (b + 1) * head_rows] for top in tops], 0)
        high_part, low_part = two_terms(own)
        scores = mm_t(jnp.concatenate([high_part, low_part], 0), state_low[b])
        scores = (scores[:all_rows] + scores[all_rows:]) * HDIM ** (-0.5)
        scores = jnp.where(slot_index < lens[b], scores, -1e30)
        shifted = jnp.exp(scores - jnp.max(scores, -1, keepdims=True))
        prob_low = (shifted / jnp.sum(shifted, -1, keepdims=True)).astype(BF)
        bars.append(mm(prob_low, state_low[b]))
        masses.append(jnp.sum(prob_low.astype(F32), -1, keepdims=True))
    joined = starts + vectors[base + 2 : base + 3, :]
    for shard in range(groups):
        part = slice(shard * head_rows, (shard + 1) * head_rows)
        own = jnp.concatenate([bar[part] for bar in bars], 0)
        mass = jnp.concatenate([mass[part] for mass in masses], 0)
        high_part, low_part = two_terms(own)
        full = mm_t(jnp.concatenate([high_part, low_part], 0), weights[shard][2])
        full = full[: count * head_rows] + full[count * head_rows :] + mass * shard_bias[shard, 3:4, 0:width]
        context = jnp.concatenate(
            [
                jnp.sum(full[b * head_rows : (b + 1) * head_rows] * head_mask, 0, keepdims=True)
                for b in range(count)
            ],
            0,
        )
        joined = joined + mm(context.astype(BF), weights[shard][3])
    hidden_out[...] = normalise(joined)[0] * vectors[base + 3 : base + 4, :] + vectors[base + 4 : base + 5, :]


def teacher_forward(embedded, shard_pieces, cls_pieces, student_embedded, feedforward, pooler, vectors, lens, group_index):
    groups, count, width, length_slots = embedded.shape
    model_width = groups * width
    first_attention, wides, narrows = shard_pieces
    local_units = feedforward.shape[-1]
    spread_rows = local_units * groups // model_width
    block_rows = 8 + spread_rows
    one, two = vectors[2 : 2 + block_rows], vectors[2 + block_rows : 2 + 2 * block_rows]
    biases = [one[0], one[1], two[0], two[1]]
    biases = [jnp.pad(row.reshape(groups, width), ((0, 0), (0, local_units - width))) for row in biases]
    unit_rows = one[5 : 5 + spread_rows].reshape(groups, local_units)
    shard_bias = jnp.stack(biases + [unit_rows] + [jnp.zeros_like(unit_rows)] * 3, 1)
    order = jnp.bitwise_xor(jnp.arange(groups), group_index)
    shard_bias = jnp.take(shard_bias, order, axis=0)

    def whole(values):
        return pl.BlockSpec(values.shape, lambda i, n: (0,) * values.ndim, pipeline_mode=pl.Buffered(1))

    each = pl.BlockSpec((1, length_slots, model_width), lambda i, n: (i, 0, 0))
    hidden = pl.pallas_call(
        attention_kernel,
        name="teacher_attention",
        grid_spec=pltpu.PrefetchScalarGridSpec(
            num_scalar_prefetch=1,
            grid=(count,),
            in_specs=[
                pl.BlockSpec((groups, 1, width, length_slots), lambda i, n: (0, i, 0, 0)),
                whole(shard_bias),
                whole(vectors),
            ]
            + [whole(piece) for piece in first_attention],
            out_specs=each,
            scratch_shapes=[
                pltpu.VMEM((length_slots, model_width), F32),
                pltpu.VMEM((length_slots, model_width), BF),
                pltpu.VMEM((3, length_slots, width), BF),
                pltpu.VMEM((groups, length_slots, width), BF),
            ],
        ),
        out_shape=jax.ShapeDtypeStruct((count, length_slots, model_width), F32),
        compiler_params=pltpu.CompilerParams(vmem_limit_bytes=40 * MIB),
        cost_estimate=small_cost(),
    )(lens, embedded, shard_bias, vectors, *first_attention)
    own, near, far = cls_pieces
    hidden, far, student_embedded = lax.optimization_barrier((hidden, far, student_embedded))
    second_attention = [own, near, far, group_swap(far, 1, groups)]
    state_low, first = pl.pallas_call(
        functools.partial(feed_kernel, spread_rows, 256),
        name="teacher_feed",
        grid_spec=pltpu.PrefetchScalarGridSpec(
            num_scalar_prefetch=1,
            grid=(count,),
            in_specs=[each, whole(shard_bias), whole(vectors)] + [whole(piece) for piece in wides + narrows],
            out_specs=[each, pl.BlockSpec((1, 8, model_width), lambda i, n: (i, 0, 0))],
        ),
        out_shape=[
            jax.ShapeDtypeStruct((count, length_slots, model_width), BF),
            jax.ShapeDtypeStruct((count, 8, model_width), F32),
        ],
        compiler_params=pltpu.CompilerParams(vmem_limit_bytes=50 * MIB),
        cost_estimate=small_cost(),
    )(lens, hidden, shard_bias, vectors, *wides, *narrows)
    smem = pl.BlockSpec(memory_space=pltpu.SMEM)
    vmem = pl.BlockSpec(memory_space=pltpu.VMEM)
    hidden = pl.pallas_call(
        functools.partial(cls_kernel, spread_rows),
        name="teacher_cls",
        in_specs=[smem] + [vmem] * (4 + groups),
        out_specs=vmem,
        out_shape=jax.ShapeDtypeStruct((count, model_width), F32),
        compiler_params=pltpu.CompilerParams(vmem_limit_bytes=40 * MIB),
        cost_estimate=small_cost(),
    )(lens, state_low, first, shard_bias, vectors, *second_attention)
    everyone = spread_to(hidden.astype(BF), "grp", groups).reshape(-1, model_width)
    unit_bias = lax.dynamic_slice_in_dim(two[5 : 5 + spread_rows].reshape(-1), group_index * local_units, local_units)
    before = ein("sd,df->sf", everyone, feedforward[1, 0]) + unit_bias
    active = jax.nn.gelu(before, approximate=False).astype(BF)
    partial_rows = ein("sf,df->sd", active, feedforward[1, 1]).reshape(groups, count, model_width)
    total = jnp.sum(exchange(partial_rows, "grp"), 0)
    summed = hidden + total + two[5 + spread_rows]
    cls = layer_norm(summed, two[6 + spread_rows], two[7 + spread_rows])
    pool = jnp.tanh(ein("sd,de->se", cls.astype(BF), pooler) + vectors[2 + 2 * block_rows])
    logits = ein("sd,cd->sc", pool.astype(BF), vectors[3 + 2 * block_rows :].astype(BF))
    return cls, logits, student_embedded


NT = (((1,), (1,)), ((), ()))
HEAD_ROWS = 16
MISC_ROWS = 8
SEQ_ROWS = MISC_ROWS + 2 * HEAD_ROWS
SMALL_ROWS = 24


def mm(left, right):
    return jnp.dot(left, right, preferred_element_type=F32)


def mm_t(left, right):
    return lax.dot_general(left, right, NT, preferred_element_type=F32)


def row_mean(values):
    return jnp.mean(values, -1, keepdims=True)


def normalise(values):
    center = values - row_mean(values)
    rstd = lax.rsqrt(row_mean(center * center) + layer_eps)
    return center * rstd, rstd


def normal_back(normal, rstd, cotangent):
    return rstd * (cotangent - row_mean(cotangent) - normal * row_mean(cotangent * normal))


def phi(values):
    return 0.5 * (1.0 + lax.erf(values * 0.5**0.5))


def log_soft(values, live):
    shifted = jnp.where(live, values, -1e30)
    shifted = shifted - jnp.max(shifted, -1, keepdims=True)
    return shifted - jnp.log(jnp.sum(jnp.where(live, jnp.exp(shifted), 0.0), -1, keepdims=True))


def student_kernel(
    total_count,
    classes,
    lens,
    labels,
    swapped,
    emb,
    side_own,
    side_far,
    narrow_own,
    narrow_far,
    small,
    bias,
    teacher_cls,
    teacher_logits,
    message,
    left,
    right,
    rows_in,
    rows_low,
    normal_low,
    stats,
):
    shards, count, own_rows, length_slots = emb.shape
    model_width = shards * own_rows
    half = model_width // 2
    unit_half = side_own.shape[1] - 5 * half
    spread_rows = 2 * unit_half // model_width
    far = swapped[0] == 1
    scale = HDIM ** (-0.5)
    block = 128

    def small_row(index, rows=1):
        return small[index : index + rows, :]

    def weight(index):
        span = slice(index * half, (index + 1) * half)
        return side_own[:, span], side_far[:, span]

    def units():
        return side_own[:, 5 * half :], side_far[:, 5 * half :]

    def narrow():
        return narrow_own[...], narrow_far[...]

    def forward(values, pair):
        one, two = mm(values, pair[0]), mm(values, pair[1])
        return jnp.where(far, jnp.concatenate([two, one], 1), jnp.concatenate([one, two], 1))

    def backward(values, pair):
        middle = values.shape[1] // 2
        low_part, high_part = values[:, :middle].astype(F32), values[:, middle:].astype(F32)
        one = jnp.where(far, high_part, low_part).astype(BF)
        two = jnp.where(far, low_part, high_part).astype(BF)
        return mm_t(one, pair[0]) + mm_t(two, pair[1])

    def both(values):
        return jnp.concatenate(two_terms(values), 0)

    def fold(values):
        middle = values.shape[0] // 2
        return values[:middle] + values[middle:]

    head_mask = (
        lax.broadcasted_iota(jnp.int32, (HEAD_ROWS, model_width), 0)
        == lax.broadcasted_iota(jnp.int32, (HEAD_ROWS, model_width), 1) // HDIM
    ).astype(F32)
    heads = model_width // HDIM

    def by_head(values):
        return jnp.concatenate(
            [jnp.broadcast_to(values[b : b + 1], head_mask.shape) * head_mask for b in range(count)], 0
        )

    def from_head(values):
        return jnp.concatenate(
            [
                jnp.sum(values[b * HEAD_ROWS : (b + 1) * HEAD_ROWS] * head_mask, 0, keepdims=True)
                for b in range(count)
            ],
            0,
        )

    def head_rows(values, b):
        return values[b * HEAD_ROWS : (b + 1) * HEAD_ROWS]

    firsts = []
    for b in range(count):

        def norm_rows(index, carry):
            start = pl.multiple_of(index * block, block)
            span = pl.ds(start, block)
            values = jnp.concatenate([emb[f, b, :, span].astype(F32) for f in range(shards)], 0).T
            mean = row_mean(values)
            center = values - mean
            rstd = lax.rsqrt(row_mean(center * center) + layer_eps)
            normal = center * rstd
            rows_in[b, span, :] = values.astype(BF)
            normal_low[b, span, :] = normal.astype(BF)
            rows_low[b, span, :] = (normal * small_row(0) + small_row(1)).astype(BF)
            stats[b, 0:8, span] = jnp.broadcast_to(mean, (block, LANES)).T[0:8]
            stats[b, 8:16, span] = jnp.broadcast_to(rstd, (block, LANES)).T[0:8]
            return carry

        lax.fori_loop(0, length_slots // block, norm_rows, 0)
        start_row = rows_in[b, 0:16, :].astype(F32)
        firsts.append((normalise(start_row)[0] * small_row(0) + small_row(1))[0:1])
    first = jnp.concatenate(firsts, 0)
    first_low = first.astype(BF)

    query = (forward(first_low, weight(0)) + small_row(2)).astype(BF)
    key_tops = backward(by_head(query.astype(F32)).astype(BF), weight(1))
    row_index = lax.broadcasted_iota(jnp.int32, (HEAD_ROWS, length_slots), 0)
    slot_index = lax.broadcasted_iota(jnp.int32, (HEAD_ROWS, length_slots), 1)
    probs, bars, masses = [], [], []
    for b in range(count):
        scores = fold(mm_t(both(head_rows(key_tops, b)), rows_low[b])) * scale
        scores = jnp.where(slot_index < lens[b], scores, -1e30)
        shifted = jnp.exp(scores - jnp.max(scores, -1, keepdims=True))
        prob = shifted / jnp.sum(shifted, -1, keepdims=True)
        prob = jnp.where(row_index < heads, prob, 0.0)
        prob_low = prob.astype(BF)
        probs.append(prob)
        bars.append(mm(prob_low, rows_low[b]))
        masses.append(jnp.sum(prob_low.astype(F32), -1, keepdims=True))
    bars = jnp.concatenate(bars, 0)
    masses = jnp.concatenate(masses, 0)
    context = from_head(fold(forward(both(bars), weight(2))) + masses * small_row(3))
    context_low = context.astype(BF)
    joined = first + forward(context_low, weight(3)) + small_row(4)
    normal_one, rstd_one = normalise(joined)
    hidden = normal_one * small_row(5) + small_row(6)
    hidden_low = hidden.astype(BF)
    unit_bias = jnp.concatenate([small_row(7 + i) for i in range(spread_rows)], 1)
    before = forward(hidden_low, units()) + unit_bias
    gate = phi(before)
    active = (before * gate).astype(BF)
    s = 7 + spread_rows
    summed = hidden + forward(active, narrow()) + small_row(s)
    normal_two, rstd_two = normalise(summed)
    vector = normal_two * small_row(s + 1) + small_row(s + 2)
    vector_low = vector.astype(BF)
    pooled = jnp.tanh(forward(vector_low, weight(4)) + small_row(s + 3))
    pooled_low = pooled.astype(BF)
    class_rows = jnp.concatenate(
        [small_row(s + 4, classes), jnp.zeros((LANES - classes, model_width), F32)], 0
    ).astype(BF)
    lane = lax.broadcasted_iota(jnp.int32, (count, LANES), 1)
    live = lane < classes
    logits = mm_t(pooled_low, class_rows) + bias[...]

    label = jnp.concatenate([jnp.full((1, LANES), labels[b], jnp.int32) for b in range(count)], 0)
    hit = (lane == label).astype(F32)
    log_prob = log_soft(logits, live)
    teacher_soft = log_soft(teacher_logits[...] / temper, live)
    student_soft = log_soft(logits / temper, live)
    teacher_prob = jnp.where(live, jnp.exp(teacher_soft), 0.0)
    loss = jnp.sum(jnp.where(hit > 0, -log_prob, 0.0), -1, keepdims=True)
    gap = jnp.where(live, teacher_soft - student_soft, 0.0)
    loss = loss + temper * temper * jnp.sum(teacher_prob * gap, -1, keepdims=True)
    inverse = lax.rsqrt(jnp.sum(vector * vector, -1, keepdims=True) + dist_eps)
    student_unit = vector * inverse
    teacher_rows = teacher_cls[...]
    teacher_unit = teacher_rows * lax.rsqrt(jnp.sum(teacher_rows * teacher_rows, -1, keepdims=True) + dist_eps)
    apart = student_unit - teacher_unit
    loss = loss + 100.0 * jnp.sum(apart * apart, -1, keepdims=True)
    d_logits = jnp.where(live, jnp.exp(log_prob), 0.0) - hit
    soft_mass = jnp.sum(teacher_prob, -1, keepdims=True)
    d_logits = d_logits + temper * (jnp.where(live, jnp.exp(student_soft), 0.0) * soft_mass - teacher_prob)
    d_logits = d_logits / total_count
    d_unit = 200.0 / total_count * apart
    d_vector = inverse * (d_unit - student_unit * jnp.sum(student_unit * d_unit, -1, keepdims=True))

    pooled_wide = pooled_low.astype(F32)
    class_wide = class_rows.astype(F32)
    d_pooled = jnp.zeros((count, model_width), F32)
    class_grads = []
    for c in range(classes):
        part = d_logits[:, c : c + 1]
        d_pooled = d_pooled + part * class_wide[c : c + 1]
        class_grads.append(jnp.sum(part * pooled_wide, 0, keepdims=True))
    d_pool = d_pooled * (1.0 - pooled * pooled)
    pool_high, pool_rest = two_terms(d_pool)
    pool_mid, pool_last = two_terms(d_pool - pool_high.astype(F32))
    pool_back = backward(jnp.concatenate([pool_high, pool_mid, pool_last], 0), weight(4))
    d_vector = d_vector + pool_back[:count] + pool_back[count : 2 * count] + pool_back[2 * count :]
    d_summed = normal_back(normal_two, rstd_two, d_vector * small_row(s + 1))
    d_output = d_summed.astype(BF)
    d_active = backward(d_output, narrow())
    slope_gate = gate + before * jnp.exp(-0.5 * before * before) * (2.0 * 3.141592653589793) ** -0.5
    d_before = (slope_gate * d_active).astype(BF)
    d_hidden = d_summed + backward(d_before, units())
    d_joined = normal_back(normal_one, rstd_one, d_hidden * small_row(5))
    d_branch = d_joined.astype(BF)
    d_context = backward(d_branch, weight(3)).astype(BF)
    context_heads = by_head(d_context.astype(F32))
    val_tops = backward(context_heads.astype(BF), weight(2))
    constant = jnp.sum(context_heads * small_row(3), -1, keepdims=True)
    d_scores, d_bars = [], []
    for b in range(count):
        d_prob = fold(mm_t(both(head_rows(val_tops, b)), rows_low[b])) + head_rows(constant, b)
        prob = probs[b]
        d_score = (prob * (d_prob - jnp.sum(prob * d_prob, -1, keepdims=True))).astype(BF)
        d_scores.append(d_score)
        d_bars.append(mm(d_score, rows_low[b]))
    d_bars = jnp.concatenate(d_bars, 0)
    d_query = (from_head(fold(forward(both(d_bars), weight(1)))) * scale).astype(BF)
    d_first = d_joined + backward(d_query, weight(0))

    d_gain = jnp.zeros((1, model_width), F32)
    d_shift = jnp.zeros((1, model_width), F32)
    top_row = lax.broadcasted_iota(jnp.int32, (HEAD_ROWS, model_width), 0)
    for b in range(count):
        tops = jnp.concatenate(
            [
                jnp.where(top_row == 12, d_first[b : b + 1], head_rows(val_tops, b)),
                head_rows(key_tops, b) * scale,
            ],
            0,
        )
        start_slot = jnp.where(slot_index == 0, 1.0, 0.0)
        value_side = jnp.where(row_index == 12, start_slot, probs[b].astype(BF).astype(F32))
        score_side = d_scores[b].astype(F32)
        coef = jnp.concatenate([value_side, score_side], 0)
        d_shift = d_shift + jnp.sum(jnp.sum(coef, -1, keepdims=True) * tops, 0, keepdims=True)
        d_gain = d_gain + jnp.sum(mm(coef.astype(BF), normal_low[b]) * tops, 0, keepdims=True)
        scaled = tops * small_row(0)
        scaled_sum = jnp.sum(scaled, -1, keepdims=True)
        along = fold(mm_t(both(scaled), rows_in[b]))
        mean, rstd = stats[b, 0:1, :], stats[b, 8:9, :]
        live_slot = slot_index[0:1] < lens[b]
        slope = rstd * rstd * rstd * (1.0 / model_width) * jnp.sum(coef * (along - mean * scaled_sum), 0, keepdims=True)
        shift = mean * slope - rstd * (1.0 / model_width) * jnp.sum(coef * scaled_sum, 0, keepdims=True)

        def insert(values, first_row, extra):
            for term in two_terms(jnp.where(live_slot, extra, 0.0)):
                values = jnp.where(row_index == first_row, term.astype(F32), values)
                first_row += 1
            return values

        value_side = insert(value_side, 13, rstd)
        score_side = insert(insert(score_side, 12, shift), 14, slope)
        packed = jnp.concatenate([value_side, score_side], 0).astype(BF)
        top_terms = two_terms(scaled)
        for f in range(shards):
            message[f, b] = packed
            for i, term in enumerate(top_terms):
                start = (2 * b + i) * LANES
                part = term[:, f * own_rows : (f + 1) * own_rows].astype(F32)
                part = jnp.concatenate([part, jnp.zeros((COEF, LANES - own_rows), F32)], 1)
                message[f, count, :, start : start + LANES] = part.astype(BF)

    def sum_rows(values):
        return jnp.sum(values.astype(F32), 0, keepdims=True)

    small_grads = jnp.concatenate(
        [
            d_gain,
            d_shift,
            sum_rows(d_query),
            sum_rows(context_heads * masses),
            sum_rows(d_branch),
            sum_rows(d_hidden * normal_one),
            sum_rows(d_hidden),
        ]
        + [sum_rows(d_before[:, i * model_width : (i + 1) * model_width]) for i in range(spread_rows)]
        + [sum_rows(d_output), sum_rows(d_vector * normal_two), sum_rows(d_vector), sum_rows(d_pool)]
        + class_grads
        + [jnp.zeros((SMALL_ROWS - small.shape[0], model_width), F32)],
        0,
    )
    scalars = jnp.where(
        lane[0:1] == classes, jnp.sum(loss, 0, keepdims=True) / total_count, jnp.sum(d_logits, 0, keepdims=True)
    )
    scalars = jnp.where(lane[0:1] <= classes, scalars, 0.0)
    unit_rows = spread_rows * own_rows
    for f in range(shards):
        span = slice(f * own_rows, (f + 1) * own_rows)
        for b in range(count):
            one = slice(b, b + 1)
            base = b * SEQ_ROWS
            misc = [values[one, span].astype(F32) for values in (first_low, context_low, hidden_low, vector_low)]
            misc += [
                active[one, f * unit_rows + j * own_rows : f * unit_rows + (j + 1) * own_rows].astype(F32)
                for j in range(spread_rows)
            ]
            left[f, base : base + MISC_ROWS, :] = jnp.concatenate(misc, 0)
            left[f, base + MISC_ROWS : base + MISC_ROWS + HEAD_ROWS, :] = head_rows(bars, b)[:, span]
            left[f, base + MISC_ROWS + HEAD_ROWS : base + SEQ_ROWS, :] = head_rows(d_bars, b)[:, span]
        base = count * SEQ_ROWS
        left[f, base : base + SMALL_ROWS, :] = small_grads[:, span]
        left[f, base + small.shape[0] : base + small.shape[0] + 1, :] = scalars[:, 0:own_rows]
    for b in range(count):
        one = slice(b, b + 1)
        rows = [values[one].astype(F32) for values in (d_query, query, d_context, d_branch, pool_high, pool_mid)]
        rows += [d_before[one, i * model_width : (i + 1) * model_width].astype(F32) for i in range(spread_rows)]
        rows += [d_output[one].astype(F32), jnp.zeros((right.shape[1] - 7 - spread_rows, model_width), F32)]
        right[b] = jnp.concatenate(rows, 0).astype(BF)


def student_step(emb, sides, narrows, small, bias, lens, labels, swapped, teacher_cls, teacher_logits, total_count):
    shards, count, own_rows, length_slots = emb.shape
    assert 2 * count * LANES <= length_slots
    model_width = small.shape[1]
    classes = bias.shape[0]

    def wide(values):
        return jnp.pad(values, ((0, 0), (0, LANES - values.shape[1])))

    smem = pl.BlockSpec(memory_space=pltpu.SMEM)
    vmem = pl.BlockSpec(memory_space=pltpu.VMEM)
    return pl.pallas_call(
        functools.partial(student_kernel, total_count, classes),
        name="student",
        in_specs=[smem] * 3 + [vmem] * 9,
        out_specs=[vmem] * 3,
        out_shape=[
            jax.ShapeDtypeStruct((shards, count + 1, COEF, length_slots), BF),
            jax.ShapeDtypeStruct((shards, count * SEQ_ROWS + SMALL_ROWS, own_rows), F32),
            jax.ShapeDtypeStruct((count, 16, model_width), BF),
        ],
        scratch_shapes=[pltpu.VMEM((count, length_slots, model_width), BF)] * 3
        + [pltpu.VMEM((count, 16, length_slots), F32)],
        compiler_params=pltpu.CompilerParams(vmem_limit_bytes=52 * MIB),
        cost_estimate=small_cost(),
    )(
        lens,
        labels,
        swapped.reshape(1),
        emb,
        *sides,
        *narrows,
        small,
        wide(bias[None]),
        teacher_cls,
        wide(teacher_logits),
    )


def adam_update(weight, moment_one, moment_two, gradient, factor):
    gradient = gradient * factor
    first_new = beta_one * moment_one + (1.0 - beta_one) * gradient
    second_new = beta_two * moment_two + (1.0 - beta_two) * gradient * gradient
    first_hat = first_new / (1.0 - beta_one**adam_steps)
    second_hat = second_new / (1.0 - beta_two**adam_steps)
    weight_new = weight - learn_rate * (first_hat / (jnp.sqrt(second_hat) + adam_eps) + decay_rate * weight)
    return (weight_new, first_new, second_new)


def on_device(
    tokens,
    positions,
    lengths,
    labels,
    word_table,
    word_first,
    word_second,
    place_table,
    place_first,
    place_second,
    square_weights,
    square_first,
    square_second,
    widen_weights,
    widen_first,
    widen_second,
    narrow_weights,
    narrow_first,
    narrow_second,
    small_params,
    small_first,
    small_second,
    class_bias,
    class_first,
    class_second,
    teacher_word,
    teacher_place,
    teacher_attention,
    teacher_feedforward,
    teacher_pooler,
    teacher_vectors,
):
    shards = lax.axis_size("fsdp")
    groups = lax.axis_size("grp")
    shard_index = lax.axis_index("fsdp")
    group_index = lax.axis_index("grp")
    count, length_slots = tokens.shape
    model_width = small_params.shape[1]
    own_rows = word_table.shape[0]
    entries = word_table.shape[1]
    places = place_table.shape[1]
    spread_rows = widen_weights.shape[1] // model_width
    classes = class_bias.shape[0]
    head_count = model_width // HDIM
    total_count = count * shards * groups
    core = jnp.bitwise_and(group_index, 1)

    half_entries = half_of(entries)
    codes = tokens * CODE + positions
    slots = jnp.arange(length_slots, dtype=jnp.int32)[None]
    keys = jnp.where(slots < lengths[:, None], codes, LAST_KEY)
    keys = jnp.where(slots == 0, -1, keys)
    ahead = (keys[:, :, None] < keys[:, None, :]) | (
        (keys[:, :, None] == keys[:, None, :]) & (slots[:, :, None] < slots[:, None, :])
    )
    rank = jnp.sum(ahead.astype(jnp.int32), 1)
    codes = jnp.sum(jnp.where(rank[:, :, None] == slots[:, None, :], codes[:, :, None], 0), 1)
    early = jnp.sum(((keys >= 0) & (keys < half_entries * CODE)).astype(jnp.int32), 1)

    facts = jnp.stack([lengths, labels, early], 1)
    message = jnp.concatenate([codes, facts, jnp.zeros((count, LANES - facts.shape[1]), jnp.int32)], 1)
    everyone = spread_to(message, ALL, shards * groups).reshape(total_count, -1)
    all_lens = everyone[:, length_slots]
    index = jnp.arange(total_count, dtype=jnp.int32)
    longer = (all_lens[None] > all_lens[:, None]) | ((all_lens[None] == all_lens[:, None]) & (index[None] < index[:, None]))
    rank = jnp.sum(longer.astype(jnp.int32), 1)
    turn, seat = rank // (shards * groups), rank % (shards * groups)
    seat = jnp.where(turn % 2 == 0, seat, shards * groups - 1 - seat)
    target = seat * count + turn
    everyone = jnp.sum(jnp.where(target[:, None, None] == index[None, :, None], everyone[:, None], 0), 0)
    everyone = everyone.reshape(shards, groups, count, -1)
    grid_codes, grid_lens = everyone[..., :length_slots], everyone[..., length_slots]
    grid_early = everyone[..., length_slots + 2]
    row = lax.dynamic_index_in_dim(everyone, shard_index, 0, False)
    own = lax.dynamic_index_in_dim(row, group_index, 0, False)
    lengths, labels = own[:, length_slots], own[:, length_slots + 1]
    row = row.reshape(groups * count, -1)
    row_codes, row_lens = row[:, :length_slots], row[:, length_slots]
    column = lax.dynamic_index_in_dim(everyone, group_index, 1, False).reshape(shards * count, -1)
    column_codes, column_lens = column[:, :length_slots], column[:, length_slots]
    later = (square_weights, widen_weights, narrow_weights, teacher_attention, teacher_feedforward)
    later, grid_codes, grid_lens = lax.optimization_barrier((later, grid_codes, grid_lens))
    square_source, widen_source, narrow_source, teacher_attention_own, teacher_feedforward_own = later

    attention_source = jnp.swapaxes(teacher_attention_own, 2, 3)
    sources = (
        attention_source[0],
        teacher_feedforward_own[0, 0],
        teacher_feedforward_own[0, 1],
        attention_source[1],
    )
    sources, row_codes, row_lens = lax.optimization_barrier((sources, row_codes, row_lens))
    near = [group_swap(piece, 1, groups) for piece in sources]
    far = [group_swap(piece, 2, groups) for piece in sources]

    half = model_width // 2

    def my_half(values):
        return lax.dynamic_index_in_dim(values.reshape(values.shape[0], -1, 2, half), core, 2, False)

    unit_half = spread_rows * half
    widen_half = lax.dynamic_index_in_dim(widen_source.reshape(own_rows, 2, unit_half), core, 1, False)
    side = jnp.concatenate([my_half(square_source).reshape(own_rows, -1), widen_half], 1).astype(BF)
    side_own = lax.all_gather(side, "fsdp", axis=0, tiled=True)
    narrow_half = my_half(narrow_source)[:, 0].astype(BF)
    narrow_own = lax.all_gather(narrow_half, "fsdp", axis=0, tiled=True)
    side_pair = [side_own, group_swap(side_own, 1, groups)]
    narrow = [narrow_own, group_swap(narrow_own, 1, groups)]

    teacher_slices = lookup(row_codes, row_lens, teacher_word, teacher_place)
    teacher_slices, far[0], column_codes, column_lens = lax.optimization_barrier(
        (teacher_slices, far[0], column_codes, column_lens)
    )
    teacher_embedded = exchange(teacher_slices, "grp").reshape(groups, count, -1, length_slots)
    student_slices = lookup(column_codes, column_lens, word_table, place_table)
    student_slices, far[1], far[2] = lax.optimization_barrier((student_slices, far[1], far[2]))
    embedded = exchange(student_slices, "fsdp").reshape(shards, count, own_rows, length_slots)
    group_slices = lax.all_gather(student_slices, "grp", axis=0, tiled=True)
    last = [group_swap(piece, 1, groups) for piece in far[:3]]
    teacher_embedded, student_slices, last[1], last[2] = lax.optimization_barrier(
        (teacher_embedded, student_slices, last[1], last[2])
    )
    shard_pieces = [list(pieces) for pieces in zip(sources[:3], near[:3], far[:3], last)]

    teacher_cls, teacher_logits, embedded = teacher_forward(
        teacher_embedded,
        shard_pieces,
        (sources[3], near[3], far[3]),
        embedded,
        teacher_feedforward,
        teacher_pooler,
        teacher_vectors,
        lengths,
        group_index,
    )
    message, left, right = student_step(
        embedded,
        side_pair,
        narrow,
        small_params,
        class_bias,
        lengths,
        labels,
        core,
        teacher_cls,
        teacher_logits,
        total_count,
    )

    message = exchange(message, "fsdp")
    message, left, right = lax.optimization_barrier((message, left, right))
    left = exchange(left, "fsdp")
    right = spread_to(right, "fsdp", shards)
    far_message = group_swap(message, 2, groups)
    place_part = place_sums(column_codes.reshape(-1), column_lens, message, student_slices, places)
    left, right, far_message, place_part = lax.optimization_barrier((left, right, far_message, place_part))
    place_part = spread_to(place_part, "grp", groups)

    def in_order(pieces):
        buffer = jnp.zeros((groups,) + pieces[0].shape, pieces[0].dtype)
        for distance, piece in enumerate(pieces):
            place = jnp.bitwise_xor(group_index, distance)
            buffer = lax.dynamic_update_index_in_dim(buffer, piece, place, 0)
        return buffer.reshape((-1,) + pieces[0].shape[1:])

    all_messages = in_order(
        [message, group_swap(message, 1, groups), far_message, group_swap(far_message, 1, groups)]
    )
    left = spread_to(left, "grp", groups)
    right = spread_to(right, "grp", groups)
    seqs = groups * shards * count
    seq_codes = grid_codes.transpose(1, 0, 2, 3).reshape(-1)
    seq_facts = jnp.stack([grid_lens.transpose(1, 0, 2).reshape(seqs), grid_early.transpose(1, 0, 2).reshape(seqs)])
    half_rows, word_squares = scatter(seq_codes, seq_facts, core, all_messages, group_slices, half_entries)
    left, right, place_part, half_rows, word_squares = lax.optimization_barrier(
        (left, right, place_part, half_rows, word_squares)
    )
    other_rows = group_swap(half_rows, 1, groups)
    place_grad = jnp.sum(place_part, 0)[:, :own_rows].T
    small_slice = jnp.sum(left[:, :, count * SEQ_ROWS : count * SEQ_ROWS + small_params.shape[0] + 1], (0, 1))
    left = left[:, :, : count * SEQ_ROWS].reshape(seqs, SEQ_ROWS, own_rows)
    right = right.reshape(seqs, -1, model_width)
    names = ["d_query", "query", "d_context", "d_branch", "pool_high", "pool_low"]
    rights = {name: right[:, i] for i, name in enumerate(names)}
    d_before = right[:, 6 : 6 + spread_rows].reshape(seqs, -1)
    d_output = right[:, 6 + spread_rows]
    h = head_count
    bars = left[:, MISC_ROWS : MISC_ROWS + h]
    d_bars = left[:, MISC_ROWS + HEAD_ROWS : MISC_ROWS + HEAD_ROWS + h]
    active = left[:, 4 : 4 + spread_rows].reshape(seqs, -1)

    def outer(left_side, right_side):
        return ein("sf,sd->fd", left_side.astype(BF), right_side)

    def outer_heads(left_side, right_side):
        return ein_split("shf,shd->fhd", left_side, right_side.reshape(seqs, h, HDIM)).reshape(own_rows, -1)

    square_grad = jnp.concatenate(
        [
            outer(left[:, 0], rights["d_query"]),
            outer_heads(d_bars, rights["query"]) * HDIM ** (-0.5),
            outer_heads(bars, rights["d_context"]),
            outer(left[:, 1], rights["d_branch"]),
            outer(left[:, 3], rights["pool_high"]) + outer(left[:, 3], rights["pool_low"]),
        ],
        1,
    )
    widen_grad = outer(left[:, 2], d_before)
    narrow_grad = outer(active, d_output)

    local_square = (
        jnp.sum(square_grad * square_grad)
        + jnp.sum(widen_grad * widen_grad)
        + jnp.sum(narrow_grad * narrow_grad)
        + jnp.sum(place_grad * place_grad)
    )
    squares = jnp.stack([local_square, jnp.sum(word_squares)])
    squares = jnp.concatenate([squares, jnp.zeros((own_rows - 2,), F32)])[None]
    last = jnp.concatenate([small_slice, squares], 0)
    last = spread_to(last, ALL, shards * groups)
    word_square = jnp.sum(last[:, -1, 1]) * (2.0 / groups)
    last = last.reshape((shards, groups) + last.shape[1:])[:, 0]
    rows_all = small_params.shape[0]
    small_grad = jnp.moveaxis(last[:, :rows_all], 0, 1).reshape(rows_all, model_width)
    bias_grad = last[0, rows_all, :classes]
    total_loss = last[0, rows_all, classes]
    total_square = jnp.sum(last[:, rows_all + 1, 0]) + word_square
    total_square = total_square + jnp.sum(small_grad * small_grad) + jnp.sum(bias_grad * bias_grad)
    gradient_norm = jnp.sqrt(total_square)
    factor = jnp.minimum(1.0, clip_bound / gradient_norm)
    results = [total_loss, gradient_norm]
    results.extend(adam_table(factor, core, half_rows, other_rows, word_table, word_first, word_second))
    for weight, moment_one, moment_two, gradient in (
        (place_table, place_first, place_second, place_grad),
        (square_weights, square_first, square_second, square_grad),
        (widen_weights, widen_first, widen_second, widen_grad),
        (narrow_weights, narrow_first, narrow_second, narrow_grad),
        (small_params, small_first, small_second, small_grad),
        (class_bias, class_first, class_second, bias_grad),
    ):
        results.extend(adam_update(weight, moment_one, moment_two, gradient, factor))
    return tuple(results)


def solution(mesh):
    rows = P("fsdp", None)
    seqs = P(("fsdp", "grp"))
    table = [rows] * 15
    placed = (
        [P(("fsdp", "grp"), None)] * 2
        + [seqs] * 2
        + table
        + [P()] * 6
        + [P("grp", None)] * 2
        + [P(None, None, None, "grp")] * 2
        + [P()] * 2
    )
    return jax.shard_map(
        on_device,
        mesh=mesh,
        in_specs=tuple(placed),
        out_specs=tuple([P(), P()] + table + [P()] * 6),
        check_vma=False,
    )
```

```python
import functools

import jax
import jax.numpy as jnp
from jax import lax
from jax.experimental import pallas as pl
from jax.experimental.pallas import tpu as pltpu
from jax.sharding import PartitionSpec as P

HDIM = 64
BF = jnp.bfloat16
F32 = jnp.float32
ALL = ("fsdp", "grp")
MIB = 2**20

highest = lax.Precision.HIGHEST
layer_eps = 1e-06
dist_eps = 1e-06
temper = 10.0
beta_one = 0.9
beta_two = 0.999
learn_rate = 0.05
decay_rate = 0.01
adam_eps = 1e-08
adam_steps = 10
clip_bound = 1.0
LANES = 128
CODE = 512
COEF = 32
LAST_KEY = 2**30
DEAL = 15


def layer_norm(values, scale_row, shift_row):
    center = values - jnp.mean(values, -1, keepdims=True)
    spread = jnp.mean(center * center, -1, keepdims=True)
    return center * lax.rsqrt(spread + layer_eps) * scale_row + shift_row


def norm_back(values, scale_row, shift_row, cotangent):
    outputs, pullback = jax.vjp(layer_norm, values, scale_row, shift_row)
    return pullback(cotangent)


def low(values):
    return lax.reduce_precision(values, exponent_bits=8, mantissa_bits=7)


def ein(spec, left, right):
    return jnp.einsum(spec, left, right, preferred_element_type=F32)


def split_two(values):
    high_part = low(values)
    return high_part.astype(BF), (values - high_part).astype(BF)


def ein_split(spec, left, right):
    high_part, low_part = split_two(left)
    return ein(spec, high_part, right) + ein(spec, low_part, right)


def ein_split_right(spec, left, right):
    high_part, low_part = split_two(right)
    return ein(spec, left, high_part) + ein(spec, left, low_part)


def half_of(entries):
    return pl.cdiv(entries, 4096) * 2048


def small_cost():
    return pl.CostEstimate(flops=0, transcendentals=0, bytes_accessed=MIB)


def large_cost():
    return pl.CostEstimate(flops=0, transcendentals=0, bytes_accessed=200 * MIB)


def exchange(values, axes):
    return lax.all_to_all(values, axes, split_axis=0, concat_axis=0, tiled=True)


def spread_to(values, axes, count):
    return exchange(jnp.broadcast_to(values[None], (count,) + values.shape), axes)


def group_swap(values, distance, count):
    return lax.ppermute(values, "grp", [(i, i ^ distance) for i in range(count)])


def group_direct(own, count):
    return [own] + [group_swap(own, r, count) for r in range(1, count)]


def half_kernel(core, square, widen, narrow, side):
    own_rows = square.shape[0]
    half = narrow.shape[1] // 2
    second = core[0] == 1
    for i in range(5):
        start = 2 * i * half
        pair = square[:, start : start + half], square[:, start + half : start + 2 * half]
        side[:, i * half : (i + 1) * half] = jnp.where(second, pair[1], pair[0]).astype(BF)
    middle = widen.shape[1] // 2
    side[:, 5 * half : 5 * half + middle] = jnp.where(second, widen[:, middle:], widen[:, :middle]).astype(BF)
    for j in range(narrow.shape[0] // own_rows):
        rows = slice(j * own_rows, (j + 1) * own_rows)
        start = 5 * half + middle + j * half
        side[:, start : start + half] = jnp.where(second, narrow[rows, half:], narrow[rows, :half]).astype(BF)


def half_weights(core, square, widen, narrow):
    vmem = pl.BlockSpec(memory_space=pltpu.VMEM)
    return pl.pallas_call(
        half_kernel,
        name="half_weights",
        in_specs=[pl.BlockSpec(memory_space=pltpu.SMEM)] + [vmem] * 3,
        out_specs=vmem,
        out_shape=jax.ShapeDtypeStruct((square.shape[0], (square.shape[1] + 2 * widen.shape[1]) // 2), BF),
        compiler_params=pltpu.CompilerParams(vmem_limit_bytes=16 * MIB),
        cost_estimate=small_cost(),
    )(core.reshape(1), square, widen, narrow)


def lookup_kernel(width, streams, table_steps, count, codes, info, where, *refs):
    tables, (place, out), scratch = refs[:streams], refs[streams : streams + 2], refs[streams + 2 :]
    groups = len(scratch) // 3
    rows, spots, stages = scratch[:groups], scratch[groups : 2 * groups], scratch[2 * groups :]
    step = pl.program_id(0)
    length_slots = out.shape[2]
    block = tables[0].shape[1]
    piece = block // 2

    def turned(values):
        values = values.astype(BF).astype(F32)
        return [values[g * LANES : min((g + 1) * LANES, width)].T for g in range(groups)]

    @pl.when(step == 0)
    def first():
        for spot, value in zip(spots, turned(place[...])):
            spot[:, 0 : value.shape[1]] = value

    @pl.when(step < table_steps)
    def turn():
        for stream, table in enumerate(tables):

            @pl.loop(0, block // piece)
            def part(i):
                column = pl.multiple_of(i * piece, piece)
                start = pl.multiple_of((stream * table_steps + step) * block + i * piece, piece)
                for row, value in zip(rows, turned(table[:, pl.ds(column, piece)])):
                    row[pl.ds(start, piece), 0 : value.shape[1]] = value

    @pl.when(step >= table_steps)
    def fetch():
        unroll = 16
        for b in range(count):
            seq = info[where[0] + (step - table_steps) * where[1] + b, DEAL]
            base = seq * length_slots
            live = info[seq, 0]

            def some(index, carry):
                for k in range(unroll):
                    slot = index * unroll + k
                    code = codes[base + slot]
                    word = lax.shift_right_logical(code, 9)
                    spot = jnp.bitwise_and(code, CODE - 1)
                    for stage, row, place_row in zip(stages, rows, spots):
                        stage[pl.ds(slot, 1), :] = row[pl.ds(word, 1), :] + place_row[pl.ds(spot, 1), :]
                return carry

            lax.fori_loop(0, pl.cdiv(live, unroll), some, 0)
            slots = lax.broadcasted_iota(jnp.int32, (length_slots, LANES), 0)
            for g, stage in enumerate(stages):
                start, end = g * LANES, min((g + 1) * LANES, width)
                out[b, start:end] = jnp.where(slots < live, stage[...], 0.0).T[0 : end - start].astype(BF)


def lookup(codes, info, where, table, place, steps, count, length_slots):
    width, entries = table.shape
    streams, table_steps = 4, 4
    block = pl.cdiv(entries, streams * table_steps * 4 * LANES) * 4 * LANES
    groups = pl.cdiv(width, LANES)
    last = pl.cdiv(entries, block) - 1

    def stream_spec(stream):
        def index(i, *scalars):
            return (0, jnp.minimum(stream * table_steps + jnp.minimum(i, table_steps - 1), last))

        return pl.BlockSpec((width, block), index)

    return pl.pallas_call(
        functools.partial(lookup_kernel, width, streams, table_steps, count),
        name="lookup",
        grid_spec=pltpu.PrefetchScalarGridSpec(
            num_scalar_prefetch=3,
            grid=(table_steps + steps,),
            in_specs=[stream_spec(stream) for stream in range(streams)]
            + [pl.BlockSpec(place.shape, lambda i, *scalars: (0, 0))],
            out_specs=pl.BlockSpec(
                (count, width, length_slots), lambda i, *scalars: (jnp.maximum(i - table_steps, 0), 0, 0)
            ),
            scratch_shapes=[pltpu.VMEM((streams * table_steps * block, LANES), F32)] * groups
            + [pltpu.VMEM((place.shape[1], LANES), F32)] * groups
            + [pltpu.VMEM((length_slots, LANES), F32)] * groups,
        ),
        out_shape=jax.ShapeDtypeStruct((steps * count, width, length_slots), BF),
        compiler_params=pltpu.CompilerParams(vmem_limit_bytes=58 * MIB),
        cost_estimate=small_cost(),
    )(codes, info, where, *[table] * streams, place)


def two_terms(values):
    high_part = values.astype(BF)
    return high_part, (values - high_part.astype(F32)).astype(BF)


def slot_gradients(b, message, emb, span):
    own_rows = emb.shape[1]
    both = message[0, message.shape[1] - 1, :, b * 2 * LANES : (b + 1) * 2 * LANES]
    mix = message[0, b, :, span]
    extra = mix.astype(F32)
    back = lax.dot_general(both, mix, (((0,), (0,)), ((), ())), preferred_element_type=F32)
    back = back[:LANES] + back[LANES:]
    scale = extra[13:14] + extra[14:15]
    shift = extra[28:29] + extra[29:30]
    slope = extra[30:31] + extra[31:32]
    rows = back[:own_rows] * scale + shift - emb[b, :, span].astype(F32) * slope
    if own_rows < LANES:
        rows = jnp.concatenate([rows, jnp.zeros((LANES - own_rows, rows.shape[1]), F32)], 0)
    return rows


def row_gradients(b, message, emb, stage, low, high, begin, finish):
    length_slots = emb.shape[2]
    rows = slot_gradients(b, message, emb, slice(0, length_slots))
    slots = lax.broadcasted_iota(jnp.int32, (1, length_slots), 1)
    keep = (slots < high) & ((slots >= low) | (slots == 0))
    rows = jnp.where(keep, rows, 0.0).T
    slots = lax.broadcasted_iota(jnp.int32, rows.shape, 0)
    inside = (slots >= begin) & (slots < finish)
    stage[0:length_slots, :] = jnp.where(inside, 0.0, rows)
    return jnp.sum(jnp.sum(jnp.where(inside, rows, 0.0).reshape(length_slots // 8, 8, LANES), 0), 0, keepdims=True)


def scatter_kernel(half_entries, groups, codes, info, core, *refs):
    pieces, (emb, out, squares, acc, stages, messages, sem) = refs[:groups], refs[groups:]
    step = pl.program_id(0)
    count, own_rows, length_slots = emb.shape
    clear = 512
    batch = 8

    @pl.when(step == 0)
    def first():
        stages[...] = jnp.zeros_like(stages)
        for distance, piece in enumerate(pieces):
            messages[jnp.bitwise_xor(core[1], distance)] = piece[...]

        @pl.loop(0, half_entries // clear)
        def wipe(i):
            acc[pl.ds(pl.multiple_of(i * clear, clear), clear), :] = jnp.zeros((clear, LANES), F32)

    shards = pl.num_programs(0) // groups
    group, shard = step // shards, step % shards
    def add_many(stage, base, slots, last_word=None):
        words = [codes[base + slot] for slot in slots]
        if last_word is None:
            sums = [acc[pl.ds(w, 1), :] + stage[pl.ds(s, 1), :] for w, s in zip(words, slots)]
            for w, total in zip(words, sums):
                acc[pl.ds(w, 1), :] = total
        else:
            for w, s in zip(words, slots):
                w = jnp.clip(w, 0, last_word)
                acc[pl.ds(w, 1), :] += stage[pl.ds(s, 1), :]

    plans = []
    for b in range(count):
        seq = info[(shard * groups + group) * count + b, DEAL]
        base = seq * length_slots
        middle = 1 + info[seq, 2]
        start = jnp.where(core[0] == 0, 1, middle)
        end = jnp.where(core[0] == 0, middle, info[seq, 0])
        begin = info[seq, 3 + 3 * core[0]]
        finish = begin + info[seq, 4 + 3 * core[0]]
        most = info[seq, 5 + 3 * core[0]]
        total = row_gradients(b, messages.at[group, pl.ds(shard, 1)], emb, stages.at[b], start, end, begin, finish)
        plans.append((base, start, end, begin, finish, most, total))

    for b, (base, start, end, begin, finish, most, total) in enumerate(plans):
        stage = stages.at[b]
        word = codes[base]

        @pl.when(finish > begin)
        def run():
            acc[pl.ds(codes[base + begin], 1), :] += total

        @pl.when((word >= 0) & (word < half_entries))
        def first_slot():
            add_many(stage, base, [0])

        stride = (end - start) // batch

        @pl.when(most <= stride)
        def apart():
            def some(index, carry):
                for u in range(2):
                    slots = [start + 2 * index + u + k * stride for k in range(batch)]
                    add_many(stage, base, slots)
                return carry

            lax.fori_loop(0, stride // 2, some, 0)

            @pl.when(stride % 2 == 1)
            def odd():
                add_many(stage, base, [start + stride - 1 + k * stride for k in range(batch)])

        @pl.when(most > stride)
        def repeated():
            def some(index, carry):
                for k in range(batch):
                    slot = start + index * batch + k
                    acc[pl.ds(codes[base + slot], 1), :] += stage[pl.ds(slot, 1), :]
                return carry

            lax.fori_loop(0, stride, some, 0)

        add_many(stage, base, [start + stride * batch + k for k in range(batch)], half_entries - 1)

    @pl.when(step == pl.num_programs(0) - 1)
    def last():
        copy = pltpu.make_async_copy(acc, out, sem)
        copy.start()

        def add(i, total):
            part = acc[pl.ds(pl.multiple_of(i * clear, clear), clear), :]
            return total + jnp.sum((part * part).reshape(clear // 8, 8, LANES), 0)

        squares[...] = lax.fori_loop(0, half_entries // clear, add, jnp.zeros((8, LANES), F32))
        copy.wait()


def place_kernel(info, where, message, emb, spots, out):
    step = pl.program_id(0)
    count, own_rows, length_slots = emb.shape
    places = out.shape[1]
    block = LANES

    @pl.when(step == 0)
    def first():
        out[...] = jnp.zeros_like(out)

    for b in range(count):
        live = info[info[where[0] + step * where[1] + b, DEAL], 0]

        @pl.loop(0, pl.cdiv(live, block))
        def part(index):
            span = pl.ds(pl.multiple_of(index * block, block), block)
            rows = slot_gradients(b, message, emb, span)
            spot = jnp.broadcast_to(spots[b, 0:1, span], (block, block)).T
            spot = jnp.concatenate([spot] * (places // block), 1)
            hit = (spot == lax.broadcasted_iota(jnp.int32, (block, places), 1).astype(F32)).astype(F32).astype(BF)
            high_part, low_part = two_terms(rows)
            sums = jnp.dot(jnp.concatenate([high_part, low_part], 0), hit, preferred_element_type=F32)
            out[...] += sums[:LANES] + sums[LANES:]


def row_specs(message, emb, count):
    return [
        pl.BlockSpec((1,) + message.shape[1:], lambda i, *scalars: (i, 0, 0, 0)),
        pl.BlockSpec((count,) + emb.shape[1:], lambda i, *scalars: (i, 0, 0)),
    ]


def scatter(codes, info, core, group_index, pieces, emb, half_entries):
    groups = len(pieces)
    shards, count = pieces[0].shape[0], pieces[0].shape[1] - 1
    length_slots = emb.shape[2]
    whole = pl.BlockSpec(pieces[0].shape, lambda i, *scalars: (0, 0, 0, 0), pipeline_mode=pl.Buffered(1))
    return pl.pallas_call(
        functools.partial(scatter_kernel, half_entries, groups),
        name="scatter_rows",
        grid_spec=pltpu.PrefetchScalarGridSpec(
            num_scalar_prefetch=3,
            grid=(groups * shards,),
            in_specs=[whole] * groups + [pl.BlockSpec((count,) + emb.shape[1:], lambda i, *scalars: (i, 0, 0))],
            out_specs=[
                pl.BlockSpec(memory_space=pl.ANY),
                pl.BlockSpec((8, LANES), lambda i, *scalars: (0, 0)),
            ],
            scratch_shapes=[
                pltpu.VMEM((half_entries, LANES), F32),
                pltpu.VMEM((count, length_slots + LANES, LANES), F32),
                pltpu.VMEM((groups,) + pieces[0].shape, BF),
                pltpu.SemaphoreType.DMA,
            ],
        ),
        out_shape=[
            jax.ShapeDtypeStruct((half_entries, LANES), F32),
            jax.ShapeDtypeStruct((8, LANES), F32),
        ],
        compiler_params=pltpu.CompilerParams(vmem_limit_bytes=48 * MIB),
        cost_estimate=large_cost(),
    )(codes, info, jnp.stack([core, group_index]), *pieces, emb)


def place_sums(info, where, message, emb, spots, places):
    count = message.shape[1] - 1
    return pl.pallas_call(
        place_kernel,
        name="place_rows",
        grid_spec=pltpu.PrefetchScalarGridSpec(
            num_scalar_prefetch=2,
            grid=(message.shape[0],),
            in_specs=row_specs(message, emb, count)
            + [pl.BlockSpec((count,) + spots.shape[1:], lambda i, *scalars: (i, 0, 0))],
            out_specs=pl.BlockSpec((LANES, places), lambda i, *scalars: (0, 0)),
        ),
        out_shape=jax.ShapeDtypeStruct((LANES, places), F32),
        compiler_params=pltpu.CompilerParams(vmem_limit_bytes=16 * MIB),
        cost_estimate=large_cost(),
    )(info, where, message, emb, spots)


def adam_kernel(width, half_steps, factor, core, own, other, weight, first, second, new_weight, new_first, new_second):
    mine = (pl.program_id(0) // half_steps) == core[0]
    rows = jnp.where(mine, own[...], other[...]).T[0:width]
    out = adam_update(weight[...], first[...], second[...], rows, factor[0])
    new_weight[...], new_first[...], new_second[...] = out


def adam_table(factor, core, own, other, weight, first, second):
    width, entries = weight.shape
    block = 2048
    half_steps = own.shape[0] // block
    spec = pl.BlockSpec((width, block), lambda i, f, c: (0, i))

    def half_spec(flip):
        def index(i, f, c):
            start = jnp.bitwise_xor(c[0], flip) * half_steps
            return (jnp.clip(i - start, 0, half_steps - 1), 0)

        return pl.BlockSpec((block, LANES), index)

    return pl.pallas_call(
        functools.partial(adam_kernel, width, half_steps),
        name="adam_table",
        grid_spec=pltpu.PrefetchScalarGridSpec(
            num_scalar_prefetch=2,
            grid=(pl.cdiv(entries, block),),
            in_specs=[half_spec(0), half_spec(1), spec, spec, spec],
            out_specs=[spec, spec, spec],
        ),
        out_shape=[jax.ShapeDtypeStruct(weight.shape, F32)] * 3,
        compiler_params=pltpu.CompilerParams(vmem_limit_bytes=40 * MIB),
        cost_estimate=small_cost(),
    )(factor.reshape(1), core.reshape(1), own, other, weight, first, second)


def attention_kernel(lens, me, embedded, shard_bias, vectors, *rest):
    groups, _, width, length_slots = embedded.shape
    weights, (hidden_out, rows, rows_low, heads, context) = rest[:groups], rest[groups:]
    live = lens[pl.program_id(0)]
    big, small = 256, 128

    def over_blocks(block, work, blank):
        @pl.loop(0, length_slots // block)
        def one(index):
            span = pl.ds(pl.multiple_of(index * block, block), block)
            pl.when(index * block < live)(lambda: work(span))
            pl.when(index * block >= live)(lambda: blank(span))

    def norm_in(span):
        values = jnp.concatenate([embedded[g, 0, :, span].astype(F32) for g in range(groups)], 0).T
        state = normalise(values)[0] * vectors[0:1, :] + vectors[1:2, :]
        rows[span, :] = state
        rows_low[span, :] = state.astype(BF)

    def no_rows(span):
        rows_low[span, :] = jnp.zeros((small, groups * width), BF)

    over_blocks(small, norm_in, no_rows)

    def project(shard, span):
        weight, values = weights[shard], rows_low[span, :]
        place = jnp.bitwise_xor(me[0], shard)
        query = (mm_t(values, weight[0]) + shard_bias[pl.ds(place, 1), :]).astype(BF)
        heads[shard % 2, 0, span, :] = query * jnp.asarray(HDIM ** (-0.5), BF)
        heads[shard % 2, 1, span, :] = mm_t(values, weight[1]).astype(BF)
        heads[shard % 2, 2, span, :] = (mm_t(values, weight[2]) + shard_bias[pl.ds(groups + place, 1), :]).astype(BF)

    def no_heads(span):
        for i in range(6):
            heads[i // 3, i % 3, span, :] = jnp.zeros((big, width), BF)

    over_blocks(big, functools.partial(project, 0), no_heads)

    def attend(shard, reach, span):
        mask = jnp.where(lax.broadcasted_iota(jnp.int32, (1, reach), 1) < live, 0.0, -1e30)
        pieces = []
        for head in range(width // HDIM):
            part = slice(head * HDIM, (head + 1) * HDIM)
            scores = mm_t(heads[shard % 2, 0, span, part], heads[shard % 2, 1, 0:reach, part]) + mask
            shifted = jnp.exp(scores - jnp.max(scores, -1, keepdims=True))
            prob = shifted * (1.0 / jnp.sum(shifted, -1, keepdims=True))
            pieces.append(mm(prob.astype(BF), heads[shard % 2, 2, 0:reach, part]))
        context[shard, span, :] = jnp.concatenate(pieces, 1).astype(BF)
        if shard + 1 < groups:
            project(shard + 1, span)

    for shard in range(groups):

        @pl.when(live <= big)
        def short():
            attend(shard, big, pl.ds(0, big))

        @pl.when(live > big)
        def long():
            @pl.loop(0, length_slots // big)
            def one(index):
                span = pl.ds(pl.multiple_of(index * big, big), big)
                pl.when(index * big < live)(lambda: attend(shard, length_slots, span))

    def join(span):
        joined = rows[span, :] + vectors[4:5, :]
        for shard in range(groups):
            joined = joined + mm(context[shard, span, :], weights[shard][3])
        hidden_out[0, span, :] = normalise(joined)[0] * vectors[5:6, :] + vectors[6:7, :]

    def no_hidden(span):
        hidden_out[0, span, :] = jnp.zeros((big, groups * width), F32)

    over_blocks(big, join, no_hidden)


def feed_kernel(spread_rows, block, lens, me, hidden, vectors, *rest):
    groups = (len(rest) - 2) // 2
    wides, narrows, (state_low, first) = rest[:groups], rest[groups : 2 * groups], rest[2 * groups :]
    _, length_slots, model_width = hidden.shape
    live = lens[pl.program_id(0)]
    tail = 2 + 5 + spread_rows

    @pl.loop(0, length_slots // block)
    def one(index):
        span = pl.ds(pl.multiple_of(index * block, block), block)

        @pl.when(index * block < live)
        def work():
            rows = hidden[0, span, :]
            rows_low = rows.astype(BF)
            summed = rows + vectors[tail : tail + 1, :]
            for shard in range(groups):
                before = mm(rows_low, wides[shard][...]) + vectors[pl.ds(7 + jnp.bitwise_xor(me[0], shard), 1), :]
                active = (before * phi(before)).astype(BF)
                summed = summed + mm_t(active, narrows[shard][...])
            state = normalise(summed)[0] * vectors[tail + 1 : tail + 2, :] + vectors[tail + 2 : tail + 3, :]
            state_low[0, span, :] = state.astype(BF)

            @pl.when(index == 0)
            def keep():
                first[0] = state[0:8, :]

        @pl.when(index * block >= live)
        def blank():
            state_low[0, span, :] = jnp.zeros((block, model_width), BF)


def cls_kernel(spread_rows, lens, me, state_low, first, shard_bias, vectors, *rest):
    groups = (len(rest) - 1) // 2
    hidden_out = rest[-1]
    weights = [[rest[2 * i + j // 2].at[j % 2] for j in range(4)] for i in range(groups)]
    count, length_slots, model_width = state_low.shape
    width = model_width // groups
    shard_heads = width // HDIM
    base = 2 + 8 + spread_rows
    head_rows = 8
    head_mask = (
        lax.broadcasted_iota(jnp.int32, (head_rows, width), 0)
        == lax.broadcasted_iota(jnp.int32, (head_rows, width), 1) // HDIM
    ).astype(F32)
    starts = jnp.concatenate([first[b, 0:1, :] for b in range(count)], 0)
    starts_low = starts.astype(BF)
    tops = []
    places = [jnp.bitwise_xor(me[0], shard) for shard in range(groups)]
    for shard in range(groups):
        query = mm_t(starts_low, weights[shard][0][...]) + shard_bias[pl.ds(2 * groups + places[shard], 1), :]
        query = query.astype(BF).astype(F32)
        spread = jnp.concatenate(
            [jnp.broadcast_to(query[b : b + 1], head_mask.shape) * head_mask for b in range(count)], 0
        )
        tops.append(mm(spread.astype(BF), weights[shard][1][...]))
    bars, masses = [], []
    all_rows = groups * head_rows
    slot_index = lax.broadcasted_iota(jnp.int32, (all_rows, length_slots), 1)
    for b in range(count):
        own = jnp.concatenate([top[b * head_rows : (b + 1) * head_rows] for top in tops], 0)
        high_part, low_part = two_terms(own)
        scores = mm_t(jnp.concatenate([high_part, low_part], 0), state_low[b])
        scores = (scores[:all_rows] + scores[all_rows:]) * HDIM ** (-0.5)
        scores = jnp.where(slot_index < lens[b], scores, -1e30)
        shifted = jnp.exp(scores - jnp.max(scores, -1, keepdims=True))
        prob_low = (shifted / jnp.sum(shifted, -1, keepdims=True)).astype(BF)
        bars.append(mm(prob_low, state_low[b]))
        masses.append(jnp.sum(prob_low.astype(F32), -1, keepdims=True))
    joined = starts + vectors[base + 2 : base + 3, :]
    for shard in range(groups):
        part = slice(shard * head_rows, (shard + 1) * head_rows)
        own = jnp.concatenate([bar[part] for bar in bars], 0)
        mass = jnp.concatenate([mass[part] for mass in masses], 0)
        high_part, low_part = two_terms(own)
        full = mm_t(jnp.concatenate([high_part, low_part], 0), weights[shard][2][...])
        full = full[: count * head_rows] + full[count * head_rows :] + mass * shard_bias[pl.ds(3 * groups + places[shard], 1), :]
        context = jnp.concatenate(
            [
                jnp.sum(full[b * head_rows : (b + 1) * head_rows] * head_mask, 0, keepdims=True)
                for b in range(count)
            ],
            0,
        )
        joined = joined + mm(context.astype(BF), weights[shard][3][...])
    hidden_out[...] = normalise(joined)[0] * vectors[base + 3 : base + 4, :] + vectors[base + 4 : base + 5, :]


def teacher_forward(embedded, shard_bias, shard_pieces, narrow_pieces, cls_pieces, student_parts, feedforward, pooler, vectors, lens, group_index):
    groups, count, width, length_slots = embedded.shape
    model_width = groups * width
    first_attention, wides = shard_pieces
    student_embedded, side_own = student_parts
    local_units = feedforward.shape[-1]
    spread_rows = local_units * groups // model_width
    block_rows = 8 + spread_rows
    one, two = vectors[2 : 2 + block_rows], vectors[2 + block_rows : 2 + 2 * block_rows]
    assert local_units == model_width
    me = group_index.reshape(1)

    def whole(values):
        return pl.BlockSpec(values.shape, lambda i, *scalars: (0,) * values.ndim, pipeline_mode=pl.Buffered(1))

    each = pl.BlockSpec((1, length_slots, model_width), lambda i, *scalars: (i, 0, 0))
    hidden = pl.pallas_call(
        attention_kernel,
        name="teacher_attention",
        grid_spec=pltpu.PrefetchScalarGridSpec(
            num_scalar_prefetch=2,
            grid=(count,),
            in_specs=[
                pl.BlockSpec((groups, 1, width, length_slots), lambda i, *scalars: (0, i, 0, 0)),
                whole(shard_bias),
                whole(vectors),
            ]
            + [whole(piece) for piece in first_attention],
            out_specs=each,
            scratch_shapes=[
                pltpu.VMEM((length_slots, model_width), F32),
                pltpu.VMEM((length_slots, model_width), BF),
                pltpu.VMEM((2, 3, length_slots, width), BF),
                pltpu.VMEM((groups, length_slots, width), BF),
            ],
        ),
        out_shape=jax.ShapeDtypeStruct((count, length_slots, model_width), F32),
        compiler_params=pltpu.CompilerParams(vmem_limit_bytes=40 * MIB),
        cost_estimate=small_cost(),
    )(lens, me, embedded, shard_bias, vectors, *first_attention)
    own, near, far = narrow_pieces
    cls_own, cls_near, cls_far = cls_pieces
    hidden, near, far, cls_far[0] = lax.optimization_barrier((hidden, near, far, cls_far[0]))
    narrows = [own, near, far, group_swap(far, 1, groups)]
    state_low, first = pl.pallas_call(
        functools.partial(feed_kernel, spread_rows, 256),
        name="teacher_feed",
        grid_spec=pltpu.PrefetchScalarGridSpec(
            num_scalar_prefetch=2,
            grid=(count,),
            in_specs=[each, whole(vectors)] + [whole(piece) for piece in wides + narrows],
            out_specs=[each, pl.BlockSpec((1, 8, model_width), lambda i, *scalars: (i, 0, 0))],
        ),
        out_shape=[
            jax.ShapeDtypeStruct((count, length_slots, model_width), BF),
            jax.ShapeDtypeStruct((count, 8, model_width), F32),
        ],
        compiler_params=pltpu.CompilerParams(vmem_limit_bytes=50 * MIB),
        cost_estimate=small_cost(),
    )(lens, me, hidden, vectors, *wides, *narrows)
    state_low, cls_near, cls_far, student_embedded = lax.optimization_barrier(
        (state_low, cls_near, cls_far, student_embedded)
    )
    cls_last, side_own = lax.optimization_barrier(([group_swap(part, 1, groups) for part in cls_far], side_own))
    second_attention = [*cls_own, *cls_near, *cls_far, *cls_last]
    side_far = group_swap(side_own, 1, groups)
    hidden = pl.pallas_call(
        functools.partial(cls_kernel, spread_rows),
        name="teacher_cls",
        grid_spec=pltpu.PrefetchScalarGridSpec(
            num_scalar_prefetch=2,
            grid=(1,),
            in_specs=[whole(array) for array in (state_low, first, shard_bias, vectors, *second_attention)],
            out_specs=pl.BlockSpec((count, model_width), lambda i, *scalars: (0, 0)),
        ),
        out_shape=jax.ShapeDtypeStruct((count, model_width), F32),
        compiler_params=pltpu.CompilerParams(vmem_limit_bytes=58 * MIB),
        cost_estimate=small_cost(),
    )(lens, me, state_low, first, shard_bias, vectors, *second_attention)
    everyone = spread_to(hidden.astype(BF), "grp", groups).reshape(-1, model_width)
    unit_bias = lax.dynamic_slice_in_dim(two[5 : 5 + spread_rows].reshape(-1), group_index * local_units, local_units)
    before = ein("sd,df->sf", everyone, feedforward[1, 0]) + unit_bias
    active = jax.nn.gelu(before, approximate=False).astype(BF)
    partial_rows = ein("sf,df->sd", active, feedforward[1, 1]).reshape(groups, count, model_width)
    total = jnp.sum(exchange(partial_rows, "grp"), 0)
    summed = hidden + total + two[5 + spread_rows]
    cls = layer_norm(summed, two[6 + spread_rows], two[7 + spread_rows])
    pool = jnp.tanh(ein("sd,de->se", cls.astype(BF), pooler) + vectors[2 + 2 * block_rows])
    logits = ein("sd,cd->sc", pool.astype(BF), vectors[3 + 2 * block_rows :].astype(BF))
    return cls, logits, (student_embedded, side_own, side_far)


NT = (((1,), (1,)), ((), ()))
HEAD_ROWS = 16
MISC_ROWS = 8
SEQ_ROWS = MISC_ROWS + 2 * HEAD_ROWS
SMALL_ROWS = 24


def mm(left, right):
    return jnp.dot(left, right, preferred_element_type=F32)


def mm_t(left, right):
    return lax.dot_general(left, right, NT, preferred_element_type=F32)


def row_mean(values):
    return jnp.mean(values, -1, keepdims=True)


def normalise(values):
    center = values - row_mean(values)
    rstd = lax.rsqrt(row_mean(center * center) + layer_eps)
    return center * rstd, rstd


def normal_back(normal, rstd, cotangent):
    return rstd * (cotangent - row_mean(cotangent) - normal * row_mean(cotangent * normal))


def phi(values):
    return 0.5 * (1.0 + lax.erf(values * 0.5**0.5))


def log_soft(values, live):
    shifted = jnp.where(live, values, -1e30)
    shifted = shifted - jnp.max(shifted, -1, keepdims=True)
    return shifted - jnp.log(jnp.sum(jnp.where(live, jnp.exp(shifted), 0.0), -1, keepdims=True))


def student_kernel(
    total_count,
    classes,
    lens,
    labels,
    swapped,
    emb,
    side_own,
    side_far,
    small,
    bias,
    teacher_cls,
    teacher_logits,
    message,
    shares,
    rows_in,
    rows_low,
    normal_low,
    stats,
):
    shards, count, own_rows, length_slots = emb.shape
    model_width = shards * own_rows
    half = model_width // 2
    spread_rows = (side_own.shape[1] // half - 5) // 2
    unit_half = spread_rows * half
    far = swapped[0] == 1
    scale = HDIM ** (-0.5)
    block = 128

    def small_row(index, rows=1):
        return small[index : index + rows, :]

    def weight(index):
        span = slice(index * half, (index + 1) * half)
        return side_own[:, span], side_far[:, span]

    def units():
        span = slice(5 * half, 5 * half + unit_half)
        return side_own[:, span], side_far[:, span]

    def narrow(index):
        return weight(5 + spread_rows + index)

    def narrow_parts(values):
        return [
            jnp.concatenate(
                [
                    values[:, (f * spread_rows + j) * own_rows : (f * spread_rows + j + 1) * own_rows]
                    for f in range(shards)
                ],
                1,
            )
            for j in range(spread_rows)
        ]

    def in_units(parts):
        return jnp.concatenate(
            [part[:, f * own_rows : (f + 1) * own_rows] for f in range(shards) for part in parts], 1
        )

    def forward(values, pair):
        one, two = mm(values, pair[0]), mm(values, pair[1])
        return jnp.where(far, jnp.concatenate([two, one], 1), jnp.concatenate([one, two], 1))

    def backward(values, pair):
        middle = values.shape[1] // 2
        low_part, high_part = values[:, :middle].astype(F32), values[:, middle:].astype(F32)
        one = jnp.where(far, high_part, low_part).astype(BF)
        two = jnp.where(far, low_part, high_part).astype(BF)
        return mm_t(one, pair[0]) + mm_t(two, pair[1])

    def both(values):
        return jnp.concatenate(two_terms(values), 0)

    def fold(values):
        middle = values.shape[0] // 2
        return values[:middle] + values[middle:]

    head_mask = (
        lax.broadcasted_iota(jnp.int32, (HEAD_ROWS, model_width), 0)
        == lax.broadcasted_iota(jnp.int32, (HEAD_ROWS, model_width), 1) // HDIM
    ).astype(F32)
    heads = model_width // HDIM

    def by_head(values):
        return jnp.concatenate(
            [jnp.broadcast_to(values[b : b + 1], head_mask.shape) * head_mask for b in range(count)], 0
        )

    def from_head(values):
        return jnp.concatenate(
            [
                jnp.sum(values[b * HEAD_ROWS : (b + 1) * HEAD_ROWS] * head_mask, 0, keepdims=True)
                for b in range(count)
            ],
            0,
        )

    def head_rows(values, b):
        return values[b * HEAD_ROWS : (b + 1) * HEAD_ROWS]

    firsts = []
    for b in range(count):

        def norm_rows(index, carry):
            start = pl.multiple_of(index * block, block)
            span = pl.ds(start, block)
            values = jnp.concatenate([emb[f, b, :, span].astype(F32) for f in range(shards)], 0).T
            mean = row_mean(values)
            center = values - mean
            rstd = lax.rsqrt(row_mean(center * center) + layer_eps)
            normal = center * rstd
            rows_in[b, span, :] = values.astype(BF)
            normal_low[b, span, :] = normal.astype(BF)
            rows_low[b, span, :] = (normal * small_row(0) + small_row(1)).astype(BF)
            stats[b, 0:8, span] = jnp.broadcast_to(mean, (block, LANES)).T[0:8]
            stats[b, 8:16, span] = jnp.broadcast_to(rstd, (block, LANES)).T[0:8]
            return carry

        def no_rows(index, carry):
            span = pl.ds(pl.multiple_of(index * block, block), block)
            for rows in (rows_in, normal_low, rows_low):
                rows[b, span, :] = jnp.zeros((block, model_width), BF)
            stats[b, :, span] = jnp.zeros((16, block), F32)
            return carry

        used = pl.cdiv(lens[b], block)
        lax.fori_loop(0, used, norm_rows, 0)
        lax.fori_loop(used, length_slots // block, no_rows, 0)
        start_row = rows_in[b, 0:16, :].astype(F32)
        firsts.append((normalise(start_row)[0] * small_row(0) + small_row(1))[0:1])
    first = jnp.concatenate(firsts, 0)
    first_low = first.astype(BF)

    query = (forward(first_low, weight(0)) + small_row(2)).astype(BF)
    key_tops = backward(by_head(query.astype(F32)).astype(BF), weight(1))
    row_index = lax.broadcasted_iota(jnp.int32, (HEAD_ROWS, length_slots), 0)
    slot_index = lax.broadcasted_iota(jnp.int32, (HEAD_ROWS, length_slots), 1)
    probs, bars, masses = [], [], []
    for b in range(count):
        scores = fold(mm_t(both(head_rows(key_tops, b)), rows_low[b])) * scale
        scores = jnp.where(slot_index < lens[b], scores, -1e30)
        shifted = jnp.exp(scores - jnp.max(scores, -1, keepdims=True))
        prob = shifted / jnp.sum(shifted, -1, keepdims=True)
        prob = jnp.where(row_index < heads, prob, 0.0)
        prob_low = prob.astype(BF)
        probs.append(prob)
        bars.append(mm(prob_low, rows_low[b]))
        masses.append(jnp.sum(prob_low.astype(F32), -1, keepdims=True))
    bars = jnp.concatenate(bars, 0)
    masses = jnp.concatenate(masses, 0)
    context = from_head(fold(forward(both(bars), weight(2))) + masses * small_row(3))
    context_low = context.astype(BF)
    joined = first + forward(context_low, weight(3)) + small_row(4)
    normal_one, rstd_one = normalise(joined)
    hidden = normal_one * small_row(5) + small_row(6)
    hidden_low = hidden.astype(BF)
    unit_bias = jnp.concatenate([small_row(7 + i) for i in range(spread_rows)], 1)
    before = forward(hidden_low, units()) + unit_bias
    gate = phi(before)
    active = (before * gate).astype(BF)
    s = 7 + spread_rows
    active_parts = [part.astype(BF) for part in narrow_parts(active.astype(F32))]
    summed = hidden + small_row(s)
    for j in range(spread_rows):
        summed = summed + forward(active_parts[j], narrow(j))
    normal_two, rstd_two = normalise(summed)
    vector = normal_two * small_row(s + 1) + small_row(s + 2)
    vector_low = vector.astype(BF)
    pooled = jnp.tanh(forward(vector_low, weight(4)) + small_row(s + 3))
    pooled_low = pooled.astype(BF)
    class_rows = jnp.concatenate(
        [small_row(s + 4, classes), jnp.zeros((LANES - classes, model_width), F32)], 0
    ).astype(BF)
    lane = lax.broadcasted_iota(jnp.int32, (count, LANES), 1)
    live = lane < classes
    logits = mm_t(pooled_low, class_rows) + bias[...]

    label = jnp.concatenate([jnp.full((1, LANES), labels[b], jnp.int32) for b in range(count)], 0)
    hit = (lane == label).astype(F32)
    log_prob = log_soft(logits, live)
    teacher_soft = log_soft(teacher_logits[...] / temper, live)
    student_soft = log_soft(logits / temper, live)
    teacher_prob = jnp.where(live, jnp.exp(teacher_soft), 0.0)
    loss = jnp.sum(jnp.where(hit > 0, -log_prob, 0.0), -1, keepdims=True)
    gap = jnp.where(live, teacher_soft - student_soft, 0.0)
    loss = loss + temper * temper * jnp.sum(teacher_prob * gap, -1, keepdims=True)
    inverse = lax.rsqrt(jnp.sum(vector * vector, -1, keepdims=True) + dist_eps)
    student_unit = vector * inverse
    teacher_rows = teacher_cls[...]
    teacher_unit = teacher_rows * lax.rsqrt(jnp.sum(teacher_rows * teacher_rows, -1, keepdims=True) + dist_eps)
    apart = student_unit - teacher_unit
    loss = loss + 100.0 * jnp.sum(apart * apart, -1, keepdims=True)
    d_logits = jnp.where(live, jnp.exp(log_prob), 0.0) - hit
    soft_mass = jnp.sum(teacher_prob, -1, keepdims=True)
    d_logits = d_logits + temper * (jnp.where(live, jnp.exp(student_soft), 0.0) * soft_mass - teacher_prob)
    d_logits = d_logits / total_count
    d_unit = 200.0 / total_count * apart
    d_vector = inverse * (d_unit - student_unit * jnp.sum(student_unit * d_unit, -1, keepdims=True))

    pooled_wide = pooled_low.astype(F32)
    class_wide = class_rows.astype(F32)
    d_pooled = jnp.zeros((count, model_width), F32)
    class_grads = []
    for c in range(classes):
        part = d_logits[:, c : c + 1]
        d_pooled = d_pooled + part * class_wide[c : c + 1]
        class_grads.append(jnp.sum(part * pooled_wide, 0, keepdims=True))
    d_pool = d_pooled * (1.0 - pooled * pooled)
    pool_high, pool_rest = two_terms(d_pool)
    pool_mid, pool_last = two_terms(d_pool - pool_high.astype(F32))
    pool_back = backward(jnp.concatenate([pool_high, pool_mid, pool_last], 0), weight(4))
    d_vector = d_vector + pool_back[:count] + pool_back[count : 2 * count] + pool_back[2 * count :]
    d_summed = normal_back(normal_two, rstd_two, d_vector * small_row(s + 1))
    d_output = d_summed.astype(BF)
    d_active = in_units([backward(d_output, narrow(j)) for j in range(spread_rows)])
    slope_gate = gate + before * jnp.exp(-0.5 * before * before) * (2.0 * 3.141592653589793) ** -0.5
    d_before = (slope_gate * d_active).astype(BF)
    d_hidden = d_summed + backward(d_before, units())
    d_joined = normal_back(normal_one, rstd_one, d_hidden * small_row(5))
    d_branch = d_joined.astype(BF)
    d_context = backward(d_branch, weight(3)).astype(BF)
    context_heads = by_head(d_context.astype(F32))
    val_tops = backward(context_heads.astype(BF), weight(2))
    constant = jnp.sum(context_heads * small_row(3), -1, keepdims=True)
    d_scores, d_bars = [], []
    for b in range(count):
        d_prob = fold(mm_t(both(head_rows(val_tops, b)), rows_low[b])) + head_rows(constant, b)
        prob = probs[b]
        d_score = (prob * (d_prob - jnp.sum(prob * d_prob, -1, keepdims=True))).astype(BF)
        d_scores.append(d_score)
        d_bars.append(mm(d_score, rows_low[b]))
    d_bars = jnp.concatenate(d_bars, 0)
    d_query = (from_head(fold(forward(both(d_bars), weight(1)))) * scale).astype(BF)
    d_first = d_joined + backward(d_query, weight(0))

    d_gain = jnp.zeros((1, model_width), F32)
    d_shift = jnp.zeros((1, model_width), F32)
    top_row = lax.broadcasted_iota(jnp.int32, (HEAD_ROWS, model_width), 0)
    for b in range(count):
        tops = jnp.concatenate(
            [
                jnp.where(top_row == 12, d_first[b : b + 1], head_rows(val_tops, b)),
                head_rows(key_tops, b) * scale,
            ],
            0,
        )
        start_slot = jnp.where(slot_index == 0, 1.0, 0.0)
        value_side = jnp.where(row_index == 12, start_slot, probs[b].astype(BF).astype(F32))
        score_side = d_scores[b].astype(F32)
        coef = jnp.concatenate([value_side, score_side], 0)
        d_shift = d_shift + jnp.sum(jnp.sum(coef, -1, keepdims=True) * tops, 0, keepdims=True)
        d_gain = d_gain + jnp.sum(mm(coef.astype(BF), normal_low[b]) * tops, 0, keepdims=True)
        scaled = tops * small_row(0)
        scaled_sum = jnp.sum(scaled, -1, keepdims=True)
        along = fold(mm_t(both(scaled), rows_in[b]))
        mean, rstd = stats[b, 0:1, :], stats[b, 8:9, :]
        live_slot = slot_index[0:1] < lens[b]
        slope = rstd * rstd * rstd * (1.0 / model_width) * jnp.sum(coef * (along - mean * scaled_sum), 0, keepdims=True)
        shift = mean * slope - rstd * (1.0 / model_width) * jnp.sum(coef * scaled_sum, 0, keepdims=True)

        def insert(values, first_row, extra):
            for term in two_terms(jnp.where(live_slot, extra, 0.0)):
                values = jnp.where(row_index == first_row, term.astype(F32), values)
                first_row += 1
            return values

        value_side = insert(value_side, 13, rstd)
        score_side = insert(insert(score_side, 12, shift), 14, slope)
        packed = jnp.concatenate([value_side, score_side], 0).astype(BF)
        top_terms = two_terms(scaled)
        for f in range(shards):
            message[f, b] = packed
            for i, term in enumerate(top_terms):
                start = (2 * b + i) * LANES
                part = term[:, f * own_rows : (f + 1) * own_rows].astype(F32)
                part = jnp.concatenate([part, jnp.zeros((COEF, LANES - own_rows), F32)], 1)
                message[f, count, :, start : start + LANES] = part.astype(BF)

    def sum_rows(values):
        return jnp.sum(values.astype(F32), 0, keepdims=True)

    small_grads = jnp.concatenate(
        [
            d_gain,
            d_shift,
            sum_rows(d_query),
            sum_rows(context_heads * masses),
            sum_rows(d_branch),
            sum_rows(d_hidden * normal_one),
            sum_rows(d_hidden),
        ]
        + [sum_rows(d_before[:, i * model_width : (i + 1) * model_width]) for i in range(spread_rows)]
        + [sum_rows(d_output), sum_rows(d_vector * normal_two), sum_rows(d_vector), sum_rows(d_pool)]
        + class_grads
        + [jnp.zeros((SMALL_ROWS - small.shape[0], model_width), F32)],
        0,
    )
    scalars = jnp.where(
        lane[0:1] == classes, jnp.sum(loss, 0, keepdims=True) / total_count, jnp.sum(d_logits, 0, keepdims=True)
    )
    scalars = jnp.where(lane[0:1] <= classes, scalars, 0.0)
    third = own_rows // 3
    small_index = lax.broadcasted_iota(jnp.int32, (SMALL_ROWS, own_rows), 0)
    for f in range(shards):
        span = slice(f * own_rows, (f + 1) * own_rows)
        rows = []
        for b in range(count):
            one = slice(b, b + 1)
            rows += [values[one, span].astype(F32) for values in (first_low, context_low, hidden_low, vector_low)]
            rows += [part[one, span].astype(F32) for part in active_parts]
            rows += [head_rows(bars, b)[:, span], head_rows(d_bars, b)[:, span]]
        rows.append(jnp.where(small_index == small.shape[0], scalars[:, 0:own_rows], small_grads[:, span]))
        rows.append(jnp.zeros((LANES - count * SEQ_ROWS - SMALL_ROWS, own_rows), F32))
        for i, term in enumerate(two_terms(jnp.concatenate(rows, 0).T)):
            for q in range(3):
                start = 2 * q * LANES + i * LANES
                shares[f, count * HEAD_ROWS :, start : start + LANES] = term[q * third : (q + 1) * third]
    for b in range(count):
        one = slice(b, b + 1)
        rows = [values[one].astype(F32) for values in (d_query, query, d_context, d_branch, pool_high, pool_mid)]
        rows += [d_before[one, i * model_width : (i + 1) * model_width].astype(F32) for i in range(spread_rows)]
        rows += [d_output[one].astype(F32), jnp.zeros((HEAD_ROWS - 7 - spread_rows, model_width), F32)]
        rows = jnp.concatenate(rows, 0).astype(BF)
        for f in range(shards):
            shares[f, b * HEAD_ROWS : (b + 1) * HEAD_ROWS, :] = rows


def student_step(emb, sides, small, bias, lens, labels, swapped, teacher_cls, teacher_logits, total_count):
    shards, count, own_rows, length_slots = emb.shape
    assert 2 * count * LANES <= length_slots and count * SEQ_ROWS + SMALL_ROWS <= LANES
    model_width = small.shape[1]
    classes = bias.shape[0]

    def wide(values):
        return jnp.pad(values, ((0, 0), (0, LANES - values.shape[1])))

    smem = pl.BlockSpec(memory_space=pltpu.SMEM)
    vmem = pl.BlockSpec(memory_space=pltpu.VMEM)
    return pl.pallas_call(
        functools.partial(student_kernel, total_count, classes),
        name="student",
        in_specs=[smem] * 3 + [vmem] * 7,
        out_specs=[vmem] * 2,
        out_shape=[
            jax.ShapeDtypeStruct((shards, count + 1, COEF, length_slots), BF),
            jax.ShapeDtypeStruct((shards, count * HEAD_ROWS + own_rows // 3, model_width), BF),
        ],
        scratch_shapes=[pltpu.VMEM((count, length_slots, model_width), BF)] * 3
        + [pltpu.VMEM((count, 16, length_slots), F32)],
        compiler_params=pltpu.CompilerParams(vmem_limit_bytes=52 * MIB),
        cost_estimate=small_cost(),
    )(
        lens,
        labels,
        swapped.reshape(1),
        emb,
        *sides,
        small,
        wide(bias[None]),
        teacher_cls,
        wide(teacher_logits),
    )


def adam_update(weight, moment_one, moment_two, gradient, factor):
    gradient = gradient * factor
    first_new = beta_one * moment_one + (1.0 - beta_one) * gradient
    second_new = beta_two * moment_two + (1.0 - beta_two) * gradient * gradient
    first_hat = first_new / (1.0 - beta_one**adam_steps)
    second_hat = second_new / (1.0 - beta_two**adam_steps)
    weight_new = weight - learn_rate * (first_hat / (jnp.sqrt(second_hat) + adam_eps) + decay_rate * weight)
    return (weight_new, first_new, second_new)


TN = (((0,), (0,)), ((), ()))


def tm(left, right):
    return lax.dot_general(left, right, TN, preferred_element_type=F32)


def grads_kernel(groups, group_index, *refs):
    shares, parts = refs[:groups], refs[groups : 2 * groups]
    word_squares, square, widen, narrow, place, payload = refs[2 * groups : 2 * groups + 6]
    factors, wide, bars, d_bars, masked, place_parts, smalls = refs[2 * groups + 6 :]
    shards, _, model_width = shares[0].shape
    own_rows = square.shape[0]
    third = own_rows // 3
    count = factors.shape[0] // (groups * shards)
    spread_rows = narrow.shape[0] // own_rows
    pairs = groups * shards
    base = count * SEQ_ROWS
    head_mask = (
        lax.broadcasted_iota(jnp.int32, (HEAD_ROWS, model_width), 0)
        == lax.broadcasted_iota(jnp.int32, (HEAD_ROWS, model_width), 1) // HDIM
    ).astype(F32)

    for distance in range(groups):
        group = jnp.bitwise_xor(group_index[0], distance)
        share = shares[distance]
        place_parts[group] = parts[distance][...]

        @pl.loop(0, shards)
        def shard(f):
            pair = group * shards + f
            both = jnp.concatenate(
                [
                    share[f, count * HEAD_ROWS :, 2 * q * LANES : 2 * (q + 1) * LANES].astype(F32)
                    for q in range(3)
                ],
                0,
            )
            left = (both[:, :LANES] + both[:, LANES:]).T
            smalls[pair] = left[base : base + SMALL_ROWS]
            for b in range(count):
                seq = pair * count + b
                start = b * SEQ_ROWS
                factors[seq] = left[start : start + MISC_ROWS]
                bars[seq] = left[start + MISC_ROWS : start + MISC_ROWS + HEAD_ROWS]
                d_bars[seq] = left[start + MISC_ROWS + HEAD_ROWS : start + SEQ_ROWS]
                wide[seq] = share[f, b * HEAD_ROWS : (b + 1) * HEAD_ROWS, :].astype(F32)

    def factor(index):
        return factors[:, index, :].astype(BF)

    def side(index):
        return wide[:, index, :].astype(BF)

    def heads(rows, index):
        @pl.loop(0, pairs * count)
        def spread(seq):
            row = wide[seq, index : index + 1, :]
            start = pl.multiple_of(seq * HEAD_ROWS, HEAD_ROWS)
            masked[pl.ds(start, HEAD_ROWS), :] = (jnp.broadcast_to(row, head_mask.shape) * head_mask).astype(BF)

        high_part, low_part = two_terms(rows[...].reshape(pairs * count * HEAD_ROWS, own_rows))
        return tm(high_part, masked[...]) + tm(low_part, masked[...])

    total = jnp.zeros((), F32)
    blocks = [
        tm(factor(0), side(0)),
        heads(d_bars, 1) * HDIM ** (-0.5),
        heads(bars, 2),
        tm(factor(1), side(3)),
        tm(factor(3), side(4)) + tm(factor(3), side(5)),
    ]
    for i, block in enumerate(blocks):
        square[:, i * model_width : (i + 1) * model_width] = block
        total = total + jnp.sum(block * block)
    for i in range(spread_rows):
        block = tm(factor(2), side(6 + i))
        widen[:, i * model_width : (i + 1) * model_width] = block
        total = total + jnp.sum(block * block)
        block = tm(factor(4 + i), side(6 + spread_rows))
        narrow[i * own_rows : (i + 1) * own_rows, :] = block
        total = total + jnp.sum(block * block)
    places = place_parts[0]
    for g in range(1, groups):
        places = places + place_parts[g]
    places = places[0:own_rows]
    place[...] = places
    total = total + jnp.sum(places * places)
    small = smalls[0]
    for p in range(1, pairs):
        small = small + smalls[p]
    rows = lax.broadcasted_iota(jnp.int32, small.shape, 0)
    lanes = lax.broadcasted_iota(jnp.int32, small.shape, 1)
    small = jnp.where(rows == SMALL_ROWS - 1, jnp.where(lanes == 0, total, jnp.sum(word_squares[...])), small)
    for d in range(payload.shape[0]):
        payload[d] = small


def weight_grads(group_index, shares, place_parts, word_squares, devices, own_rows):
    groups = len(shares)
    shards, share_rows, model_width = shares[0].shape
    count = (share_rows - own_rows // 3) // HEAD_ROWS
    places = place_parts[0].shape[1]
    right_rows = HEAD_ROWS
    spread_rows = MISC_ROWS - 4
    smem = pl.BlockSpec(memory_space=pltpu.SMEM)
    vmem = pl.BlockSpec(memory_space=pltpu.VMEM)
    seqs = groups * shards * count
    return pl.pallas_call(
        functools.partial(grads_kernel, groups),
        name="weight_grads",
        in_specs=[smem] + [vmem] * (2 * groups + 1),
        out_specs=[vmem] * 5,
        out_shape=[
            jax.ShapeDtypeStruct((own_rows, 5 * model_width), F32),
            jax.ShapeDtypeStruct((own_rows, spread_rows * model_width), F32),
            jax.ShapeDtypeStruct((spread_rows * own_rows, model_width), F32),
            jax.ShapeDtypeStruct((own_rows, places), F32),
            jax.ShapeDtypeStruct((devices, SMALL_ROWS, own_rows), F32),
        ],
        scratch_shapes=[
            pltpu.VMEM((seqs, MISC_ROWS, own_rows), F32),
            pltpu.VMEM((seqs, right_rows, model_width), F32),
            pltpu.VMEM((seqs, HEAD_ROWS, own_rows), F32),
            pltpu.VMEM((seqs, HEAD_ROWS, own_rows), F32),
            pltpu.VMEM((seqs * HEAD_ROWS, model_width), BF),
            pltpu.VMEM((groups,) + place_parts[0].shape, F32),
            pltpu.VMEM((groups * shards, SMALL_ROWS, own_rows), F32),
        ],
        compiler_params=pltpu.CompilerParams(vmem_limit_bytes=58 * MIB),
        cost_estimate=small_cost(),
    )(group_index.reshape(1), *shares, *place_parts, word_squares)


def norm_kernel(classes, core, parts, others, *refs):
    grads, refs = refs[:4], refs[4:]
    states, (factor_out, scalars), outs = refs[:18], refs[18:20], refs[20:]
    devices, _, own_rows = parts.shape
    rows_all = states[12].shape[0]
    joined = jnp.concatenate([parts[d] for d in range(devices)], 1)
    last = SMALL_ROWS - 1
    total = jnp.zeros((1, 1), F32)
    mine = jnp.zeros((1, 1), F32)
    other = jnp.zeros((1, 1), F32)
    for d in range(devices):
        total = total + parts[d, last : last + 1, 0:1]
        mine = mine + parts[d, last : last + 1, 1:2]
        other = other + others[d, last : last + 1, 1:2]
    first = jnp.where(core[0] == 0, mine, other)
    second = jnp.where(core[0] == 0, other, mine)
    small_grad = joined[0:rows_all]
    extra = parts[0, rows_all : rows_all + 1, :]
    lane = lax.broadcasted_iota(jnp.int32, extra.shape, 1)
    bias_grad = extra[:, 0:classes]
    total = total + first + second
    total = total + jnp.sum(jnp.sum(small_grad * small_grad, 1, keepdims=True), 0, keepdims=True)
    total = total + jnp.sum(bias_grad * bias_grad, 1, keepdims=True)
    norm = jnp.sqrt(total)
    factor = jnp.minimum(1.0, clip_bound / norm)
    factor_out[...] = jnp.broadcast_to(factor, factor_out.shape)
    loss = jnp.sum(jnp.where(lane == classes, extra, 0.0), 1, keepdims=True)
    lanes = lax.broadcasted_iota(jnp.int32, scalars.shape, 1)
    scalars[...] = jnp.where(lanes == 0, jnp.broadcast_to(loss, scalars.shape), jnp.broadcast_to(norm, scalars.shape))

    def update(index, gradient):
        weight, moment_one, moment_two = (states[3 * index + j][...] for j in range(3))
        new = adam_update(weight, moment_one, moment_two, gradient, factor)
        for j in range(3):
            outs[3 * index + j][...] = new[j]

    for index, grad in enumerate(grads):
        update(index, grad[...])
    update(4, small_grad)
    update(5, bias_grad)


def norm_step(core, parts, others, grads, states):
    classes = states[5][0].shape[0]
    steps = 3

    def whole(array):
        return pl.BlockSpec(array.shape, lambda i, *scalars: (0,) * array.ndim)

    def block(array):
        return pl.BlockSpec((array.shape[0] // steps, array.shape[1]), lambda i, *scalars: (i, 0))

    flat = [array[None] if array.ndim == 1 else array for state in states for array in state]
    flat_specs = [block(array) for array in flat[:12]] + [whole(array) for array in flat[12:]]
    row = jax.ShapeDtypeStruct((1, LANES), F32)
    outs = pl.pallas_call(
        functools.partial(norm_kernel, classes),
        name="norm",
        grid_spec=pltpu.PrefetchScalarGridSpec(
            num_scalar_prefetch=1,
            grid=(steps,),
            in_specs=[whole(parts), whole(others)] + [block(grad) for grad in grads] + flat_specs,
            out_specs=[whole(row), whole(row)] + flat_specs,
        ),
        out_shape=[row, row] + [jax.ShapeDtypeStruct(array.shape, F32) for array in flat],
        compiler_params=pltpu.CompilerParams(vmem_limit_bytes=48 * MIB),
        cost_estimate=small_cost(),
    )(core.reshape(1), parts, others, *grads, *flat)
    rest = [out[0] if out.shape[0] == 1 else out for out in outs[2:]]
    return outs[0], outs[1], rest


def on_device(
    tokens,
    positions,
    lengths,
    labels,
    word_table,
    word_first,
    word_second,
    place_table,
    place_first,
    place_second,
    square_weights,
    square_first,
    square_second,
    widen_weights,
    widen_first,
    widen_second,
    narrow_weights,
    narrow_first,
    narrow_second,
    small_params,
    small_first,
    small_second,
    class_bias,
    class_first,
    class_second,
    teacher_word,
    teacher_place,
    teacher_attention,
    teacher_feedforward,
    teacher_pooler,
    teacher_vectors,
):
    shards = lax.axis_size("fsdp")
    groups = lax.axis_size("grp")
    shard_index = lax.axis_index("fsdp")
    group_index = lax.axis_index("grp")
    count, length_slots = tokens.shape
    model_width = small_params.shape[1]
    own_rows = word_table.shape[0]
    entries = word_table.shape[1]
    places = place_table.shape[1]
    spread_rows = widen_weights.shape[1] // model_width
    classes = class_bias.shape[0]
    head_count = model_width // HDIM
    total_count = count * shards * groups
    core = jnp.bitwise_and(group_index, 1)

    half_entries = half_of(entries)
    codes = tokens * CODE + positions
    slots = jnp.arange(length_slots, dtype=jnp.int32)[None]
    keys = jnp.where(slots < lengths[:, None], codes, LAST_KEY)
    keys = jnp.where(slots == 0, -1, keys)
    ahead = (keys[:, :, None] < keys[:, None, :]) | (
        (keys[:, :, None] == keys[:, None, :]) & (slots[:, :, None] < slots[:, None, :])
    )
    rank = jnp.sum(ahead.astype(jnp.int32), 1)
    codes = jnp.sum(jnp.where(rank[:, :, None] == slots[:, None, :], codes[:, :, None], 0), 1)
    early = jnp.sum(((keys >= 0) & (keys < half_entries * CODE)).astype(jnp.int32), 1)
    words = lax.shift_right_arithmetic(keys, 9)
    same = (words[:, :, None] == words[:, None, :]) & (keys[:, :, None] >= 0) & (keys[:, :, None] < LAST_KEY)
    repeats = jnp.sum(same.astype(jnp.int32), 1)
    runs = []
    for low_half in (True, False):
        there = jnp.where((keys >= 0) & (keys < LAST_KEY) & ((words < half_entries) == low_half), repeats, 0)
        top = jnp.max(there, 1)
        begin = jnp.min(jnp.where((there == top[:, None]) & (there > 0), rank, length_slots), 1)
        inside = (rank >= begin[:, None]) & (rank < (begin + top)[:, None])
        runs += [begin, top, jnp.max(jnp.where(inside, 0, there), 1)]
    facts = jnp.stack([lengths, labels, early] + runs, 1)
    message = jnp.concatenate([codes, facts, jnp.zeros((count, LANES - facts.shape[1]), jnp.int32)], 1)
    everyone = spread_to(message, ALL, shards * groups).reshape(total_count, -1)

    attention_source = jnp.swapaxes(teacher_attention, 2, 3)
    sources = [
        attention_source[0],
        teacher_feedforward[0, 0],
        teacher_feedforward[0, 1],
        (attention_source[1, 0:2], attention_source[1, 2:4]),
    ]

    side = half_weights(core, square_weights, widen_weights, narrow_weights)
    everyone, sources, side = lax.optimization_barrier((everyone, sources, side))

    all_codes = everyone[:, :length_slots].reshape(-1)
    all_words = jnp.pad(lax.shift_right_logical(all_codes, 9) - core * half_entries, (0, LANES))
    all_facts = everyone[:, length_slots:]
    all_lens = all_facts[:, 0]
    index = jnp.arange(total_count, dtype=jnp.int32)
    longer = (all_lens[None] > all_lens[:, None]) | ((all_lens[None] == all_lens[:, None]) & (index[None] < index[:, None]))
    rank = jnp.sum(longer.astype(jnp.int32), 1)
    turn, seat = rank // (shards * groups), rank % (shards * groups)
    seat = jnp.where(turn % 2 == 0, seat, shards * groups - 1 - seat)
    target = seat * count + turn
    deal = jnp.sum(jnp.where(target[None] == index[:, None], index[None], 0), 1, keepdims=True)
    info = jnp.where(jnp.arange(LANES)[None] == DEAL, deal, all_facts)
    mine = (shard_index * groups + group_index) * count + jnp.arange(count, dtype=jnp.int32)
    own = jnp.sum(jnp.where(target[None, :, None] == mine[:, None, None], all_facts[None, :, :2], 0), 1)
    lengths, labels = own[:, 0], own[:, 1]
    row_where = jnp.stack([shard_index * groups * count, jnp.full((), count, jnp.int32)])
    column_where = jnp.stack([group_index * count, jnp.full((), groups * count, jnp.int32)])
    column = column_where[0] + jnp.arange(shards)[:, None] * column_where[1] + jnp.arange(count)[None]
    all_spots = jnp.bitwise_and(everyone[:, :length_slots], CODE - 1)
    column_hits = target[None] == column.reshape(-1)[:, None]
    column_spots = jnp.sum(jnp.where(column_hits[:, :, None], all_spots[None], 0), 1).astype(F32)[:, None]

    shard_bias = [teacher_vectors[row : row + 2] for row in (2, 2 + 8 + spread_rows)]
    shard_bias = jnp.concatenate(shard_bias).reshape(4 * groups, -1)
    side, info, all_words, column_spots, row_where, column_where, lengths, labels, shard_bias = lax.optimization_barrier(
        (side, info, all_words, column_spots, row_where, column_where, lengths, labels, shard_bias)
    )

    near = [group_swap(piece, 1, groups) for piece in sources[:3]]
    near.append([group_swap(piece, 1, groups) for piece in sources[3]])
    far = [group_swap(piece, 2, groups) for piece in sources[:2]]
    side_own = lax.all_gather(side, "fsdp", axis=0, tiled=True)

    teacher_slices = lookup(
        all_codes, info, row_where, teacher_word, teacher_place, groups, count, length_slots
    )
    teacher_slices, far[0], column_where, sources[2] = lax.optimization_barrier(
        (teacher_slices, far[0], column_where, sources[2])
    )
    teacher_embedded = exchange(teacher_slices, "grp").reshape(groups, count, -1, length_slots)
    far.append(group_swap(sources[2], 2, groups))
    student_slices = lookup(
        all_codes, info, column_where, word_table, place_table, shards, count, length_slots
    )
    student_slices, far[1], near[:2] = lax.optimization_barrier((student_slices, far[1], near[:2]))
    embedded = exchange(student_slices, "fsdp").reshape(shards, count, own_rows, length_slots)
    group_slices = lax.all_gather(student_slices, "grp", axis=0, tiled=True)
    last = [group_swap(piece, 1, groups) for piece in far[:2]]
    last[0], sources[3] = lax.optimization_barrier((last[0], sources[3]))
    far.append([group_swap(piece, 2, groups) for piece in sources[3]])
    teacher_embedded, student_slices = lax.optimization_barrier((teacher_embedded, student_slices))
    shard_pieces = [list(pieces) for pieces in zip(sources[:2], near[:2], far[:2], last)]

    teacher_cls, teacher_logits, (embedded, side_own, side_far) = teacher_forward(
        teacher_embedded,
        shard_bias,
        shard_pieces,
        (sources[2], near[2], far[2]),
        (sources[3], near[3], far[3]),
        (embedded, side_own),
        teacher_feedforward,
        teacher_pooler,
        teacher_vectors,
        lengths,
        group_index,
    )
    message, shares = student_step(
        embedded,
        (side_own, side_far),
        small_params,
        class_bias,
        lengths,
        labels,
        core,
        teacher_cls,
        teacher_logits,
        total_count,
    )

    message = exchange(message, "fsdp")
    message, shares = lax.optimization_barrier((message, shares))
    shares = exchange(shares, "fsdp")
    far_message = group_swap(message, 2, groups)
    place_part = place_sums(info, column_where, message, student_slices, column_spots, places)
    shares, far_message, place_part = lax.optimization_barrier((shares, far_message, place_part))
    all_messages = [message, group_swap(message, 1, groups), far_message, group_swap(far_message, 1, groups)]
    shares, place_part, all_messages = lax.optimization_barrier((shares, place_part, all_messages))
    place_parts, shares = (group_direct(v, groups) for v in (place_part, shares))
    half_rows, word_squares = scatter(
        all_words, info, core, group_index, all_messages, group_slices, half_entries
    )
    shares, place_parts, half_rows, word_squares = lax.optimization_barrier(
        (shares, place_parts, half_rows, word_squares)
    )
    square_grad, widen_grad, narrow_grad, place_grad, payload = weight_grads(
        group_index, shares, place_parts, word_squares, shards, own_rows
    )
    payload, half_rows = lax.optimization_barrier((payload, half_rows))
    other_rows = group_swap(half_rows, 1, groups)
    parts = exchange(payload, "fsdp")
    factor, scalars, rest = norm_step(
        core,
        parts,
        group_swap(parts, 1, groups),
        (place_grad, square_grad, widen_grad, narrow_grad),
        (
            (place_table, place_first, place_second),
            (square_weights, square_first, square_second),
            (widen_weights, widen_first, widen_second),
            (narrow_weights, narrow_first, narrow_second),
            (small_params, small_first, small_second),
            (class_bias, class_first, class_second),
        ),
    )
    word = adam_table(factor[0, 0:1], core, half_rows, other_rows, word_table, word_first, word_second)
    results = [scalars[0, 0], scalars[0, 1], *word, *rest]
    return tuple(results)


def solution(mesh):
    rows = P("fsdp", None)
    seqs = P(("fsdp", "grp"))
    table = [rows] * 15
    placed = (
        [P(("fsdp", "grp"), None)] * 2
        + [seqs] * 2
        + table
        + [P()] * 6
        + [P("grp", None)] * 2
        + [P(None, None, None, "grp")] * 2
        + [P()] * 2
    )
    return jax.shard_map(
        on_device,
        mesh=mesh,
        in_specs=tuple(placed),
        out_specs=tuple([P(), P()] + table + [P()] * 6),
        check_vma=False,
    )
```

```python
import functools

import jax
import jax.numpy as jnp
from jax import lax
from jax.experimental import pallas as pl
from jax.experimental.pallas import tpu as pltpu
from jax.sharding import PartitionSpec as P

HDIM = 64
BF = jnp.bfloat16
F32 = jnp.float32
ALL = ("fsdp", "grp")
MIB = 2**20

highest = lax.Precision.HIGHEST
layer_eps = 1e-06
dist_eps = 1e-06
temper = 10.0
beta_one = 0.9
beta_two = 0.999
learn_rate = 0.05
decay_rate = 0.01
adam_eps = 1e-08
adam_steps = 10
clip_bound = 1.0
LANES = 128
CODE = 512
COEF = 32
LAST_KEY = 2**30
DEAL = 15


def layer_norm(values, scale_row, shift_row):
    center = values - jnp.mean(values, -1, keepdims=True)
    spread = jnp.mean(center * center, -1, keepdims=True)
    return center * lax.rsqrt(spread + layer_eps) * scale_row + shift_row


def norm_back(values, scale_row, shift_row, cotangent):
    outputs, pullback = jax.vjp(layer_norm, values, scale_row, shift_row)
    return pullback(cotangent)


def low(values):
    return lax.reduce_precision(values, exponent_bits=8, mantissa_bits=7)


def ein(spec, left, right):
    return jnp.einsum(spec, left, right, preferred_element_type=F32)


def split_two(values):
    high_part = low(values)
    return high_part.astype(BF), (values - high_part).astype(BF)


def ein_split(spec, left, right):
    high_part, low_part = split_two(left)
    return ein(spec, high_part, right) + ein(spec, low_part, right)


def ein_split_right(spec, left, right):
    high_part, low_part = split_two(right)
    return ein(spec, left, high_part) + ein(spec, left, low_part)


def half_of(entries):
    return pl.cdiv(entries, 4096) * 2048


def small_cost():
    return pl.CostEstimate(flops=0, transcendentals=0, bytes_accessed=0)


def large_cost():
    return pl.CostEstimate(flops=0, transcendentals=0, bytes_accessed=200 * MIB)


def exchange(values, axes):
    return lax.all_to_all(values, axes, split_axis=0, concat_axis=0, tiled=True)


def spread_to(values, axes, count):
    return exchange(jnp.broadcast_to(values[None], (count,) + values.shape), axes)


def group_swap(values, distance, count):
    return lax.ppermute(values, "grp", [(i, i ^ distance) for i in range(count)])


def group_direct(own, count):
    return [own] + [group_swap(own, r, count) for r in range(1, count)]


def half_kernel(core, square, widen, narrow, side):
    own_rows = square.shape[0]
    half = narrow.shape[1] // 2
    second = core[0] == 1
    for i in range(5):
        start = 2 * i * half
        pair = square[:, start : start + half], square[:, start + half : start + 2 * half]
        side[:, i * half : (i + 1) * half] = jnp.where(second, pair[1], pair[0]).astype(BF)
    middle = widen.shape[1] // 2
    side[:, 5 * half : 5 * half + middle] = jnp.where(second, widen[:, middle:], widen[:, :middle]).astype(BF)
    for j in range(narrow.shape[0] // own_rows):
        rows = slice(j * own_rows, (j + 1) * own_rows)
        start = 5 * half + middle + j * half
        side[:, start : start + half] = jnp.where(second, narrow[rows, half:], narrow[rows, :half]).astype(BF)


def half_weights(core, square, widen, narrow):
    vmem = pl.BlockSpec(memory_space=pltpu.VMEM)
    return pl.pallas_call(
        half_kernel,
        name="half_weights",
        in_specs=[pl.BlockSpec(memory_space=pltpu.SMEM)] + [vmem] * 3,
        out_specs=vmem,
        out_shape=jax.ShapeDtypeStruct((square.shape[0], (square.shape[1] + 2 * widen.shape[1]) // 2), BF),
        compiler_params=pltpu.CompilerParams(vmem_limit_bytes=16 * MIB),
        cost_estimate=small_cost(),
    )(core.reshape(1), square, widen, narrow)


def lookup_kernel(width, streams, table_steps, count, codes, info, where, *refs):
    tables, (place, out), scratch = refs[:streams], refs[streams : streams + 2], refs[streams + 2 :]
    groups = len(scratch) // 3
    rows, spots, stages = scratch[:groups], scratch[groups : 2 * groups], scratch[2 * groups :]
    step = pl.program_id(0)
    length_slots = out.shape[2]
    block = tables[0].shape[1]
    piece = block // 2

    def turned(values):
        values = values.astype(BF).astype(F32)
        return [values[g * LANES : min((g + 1) * LANES, width)].T for g in range(groups)]

    @pl.when(step == 0)
    def first():
        for spot, value in zip(spots, turned(place[...])):
            spot[:, 0 : value.shape[1]] = value

    @pl.when(step < table_steps)
    def turn():
        for stream, table in enumerate(tables):

            @pl.loop(0, block // piece)
            def part(i):
                column = pl.multiple_of(i * piece, piece)
                start = pl.multiple_of((stream * table_steps + step) * block + i * piece, piece)
                for row, value in zip(rows, turned(table[:, pl.ds(column, piece)])):
                    row[pl.ds(start, piece), 0 : value.shape[1]] = value

    @pl.when(step >= table_steps)
    def fetch():
        unroll = 16
        for b in range(count):
            seq = info[where[0] + (step - table_steps) * where[1] + b, DEAL]
            base = seq * length_slots
            live = info[seq, 0]

            def some(index, carry):
                for k in range(unroll):
                    slot = index * unroll + k
                    code = codes[base + slot]
                    word = lax.shift_right_logical(code, 9)
                    spot = jnp.bitwise_and(code, CODE - 1)
                    for stage, row, place_row in zip(stages, rows, spots):
                        stage[pl.ds(slot, 1), :] = row[pl.ds(word, 1), :] + place_row[pl.ds(spot, 1), :]
                return carry

            lax.fori_loop(0, pl.cdiv(live, unroll), some, 0)
            slots = lax.broadcasted_iota(jnp.int32, (length_slots, LANES), 0)
            for g, stage in enumerate(stages):
                start, end = g * LANES, min((g + 1) * LANES, width)
                out[b, start:end] = jnp.where(slots < live, stage[...], 0.0).T[0 : end - start].astype(BF)


def lookup(codes, info, where, table, place, steps, count, length_slots):
    width, entries = table.shape
    streams, table_steps = 4, 4
    block = pl.cdiv(entries, streams * table_steps * 4 * LANES) * 4 * LANES
    groups = pl.cdiv(width, LANES)
    last = pl.cdiv(entries, block) - 1

    def stream_spec(stream):
        def index(i, *scalars):
            return (0, jnp.minimum(stream * table_steps + jnp.minimum(i, table_steps - 1), last))

        return pl.BlockSpec((width, block), index)

    return pl.pallas_call(
        functools.partial(lookup_kernel, width, streams, table_steps, count),
        name="lookup",
        grid_spec=pltpu.PrefetchScalarGridSpec(
            num_scalar_prefetch=3,
            grid=(table_steps + steps,),
            in_specs=[stream_spec(stream) for stream in range(streams)]
            + [pl.BlockSpec(place.shape, lambda i, *scalars: (0, 0))],
            out_specs=pl.BlockSpec(
                (count, width, length_slots), lambda i, *scalars: (jnp.maximum(i - table_steps, 0), 0, 0)
            ),
            scratch_shapes=[pltpu.VMEM((streams * table_steps * block, LANES), F32)] * groups
            + [pltpu.VMEM((place.shape[1], LANES), F32)] * groups
            + [pltpu.VMEM((length_slots, LANES), F32)] * groups,
        ),
        out_shape=jax.ShapeDtypeStruct((steps * count, width, length_slots), BF),
        compiler_params=pltpu.CompilerParams(vmem_limit_bytes=58 * MIB),
        cost_estimate=small_cost(),
    )(codes, info, where, *[table] * streams, place)


def two_terms(values):
    high_part = values.astype(BF)
    return high_part, (values - high_part.astype(F32)).astype(BF)


def slot_gradients(b, message, emb, span):
    own_rows = emb.shape[1]
    both = message[0, message.shape[1] - 1, :, b * 2 * LANES : (b + 1) * 2 * LANES]
    mix = message[0, b, :, span]
    extra = mix.astype(F32)
    back = lax.dot_general(both, mix, (((0,), (0,)), ((), ())), preferred_element_type=F32)
    back = back[:LANES] + back[LANES:]
    scale = extra[13:14] + extra[14:15]
    shift = extra[28:29] + extra[29:30]
    slope = extra[30:31] + extra[31:32]
    rows = back[:own_rows] * scale + shift - emb[b, :, span].astype(F32) * slope
    if own_rows < LANES:
        rows = jnp.concatenate([rows, jnp.zeros((LANES - own_rows, rows.shape[1]), F32)], 0)
    return rows


def row_gradients(b, message, emb, stage, low, high, begin, finish):
    length_slots = emb.shape[2]
    rows = slot_gradients(b, message, emb, slice(0, length_slots))
    slots = lax.broadcasted_iota(jnp.int32, (1, length_slots), 1)
    keep = (slots < high) & ((slots >= low) | (slots == 0))
    rows = jnp.where(keep, rows, 0.0).T
    slots = lax.broadcasted_iota(jnp.int32, rows.shape, 0)
    inside = (slots >= begin) & (slots < finish)
    stage[0:length_slots, :] = jnp.where(inside, 0.0, rows)
    return jnp.sum(jnp.sum(jnp.where(inside, rows, 0.0).reshape(length_slots // 8, 8, LANES), 0), 0, keepdims=True)


def scatter_kernel(half_entries, groups, codes, info, core, *refs):
    pieces, (emb, out, squares, acc, stages, messages, sem) = refs[:groups], refs[groups:]
    step = pl.program_id(0)
    count, own_rows, length_slots = emb.shape
    clear = 512
    batch = 8

    @pl.when(step == 0)
    def first():
        stages[...] = jnp.zeros_like(stages)
        for distance, piece in enumerate(pieces):
            messages[jnp.bitwise_xor(core[1], distance)] = piece[...]

        @pl.loop(0, half_entries // clear)
        def wipe(i):
            acc[pl.ds(pl.multiple_of(i * clear, clear), clear), :] = jnp.zeros((clear, LANES), F32)

    shards = pl.num_programs(0) // groups
    group, shard = step // shards, step % shards
    def add_many(stage, base, slots, last_word=None):
        words = [codes[base + slot] for slot in slots]
        if last_word is None:
            sums = [acc[pl.ds(w, 1), :] + stage[pl.ds(s, 1), :] for w, s in zip(words, slots)]
            for w, total in zip(words, sums):
                acc[pl.ds(w, 1), :] = total
        else:
            for w, s in zip(words, slots):
                w = jnp.clip(w, 0, last_word)
                acc[pl.ds(w, 1), :] += stage[pl.ds(s, 1), :]

    plans = []
    for b in range(count):
        seq = info[(shard * groups + group) * count + b, DEAL]
        base = seq * length_slots
        middle = 1 + info[seq, 2]
        start = jnp.where(core[0] == 0, 1, middle)
        end = jnp.where(core[0] == 0, middle, info[seq, 0])
        begin = info[seq, 3 + 3 * core[0]]
        finish = begin + info[seq, 4 + 3 * core[0]]
        most = info[seq, 5 + 3 * core[0]]
        total = row_gradients(b, messages.at[group, pl.ds(shard, 1)], emb, stages.at[b], start, end, begin, finish)
        plans.append((base, start, end, begin, finish, most, total))

    for b, (base, start, end, begin, finish, most, total) in enumerate(plans):
        stage = stages.at[b]
        word = codes[base]

        @pl.when(finish > begin)
        def run():
            acc[pl.ds(codes[base + begin], 1), :] += total

        @pl.when((word >= 0) & (word < half_entries))
        def first_slot():
            add_many(stage, base, [0])

        stride = (end - start) // batch

        @pl.when(most <= stride)
        def apart():
            def some(index, carry):
                for u in range(4):
                    add_many(stage, base, [start + 4 * index + u + k * stride for k in range(batch)])
                return carry

            def rest(index, carry):
                add_many(stage, base, [start + index + k * stride for k in range(batch)])
                return carry

            lax.fori_loop(0, stride // 4, some, 0)
            lax.fori_loop(stride // 4 * 4, stride, rest, 0)

        @pl.when(most > stride)
        def repeated():
            def some(index, carry):
                for k in range(batch):
                    slot = start + index * batch + k
                    acc[pl.ds(codes[base + slot], 1), :] += stage[pl.ds(slot, 1), :]
                return carry

            lax.fori_loop(0, stride, some, 0)

        add_many(stage, base, [start + stride * batch + k for k in range(batch)], half_entries - 1)

    @pl.when(step == pl.num_programs(0) - 1)
    def last():
        copy = pltpu.make_async_copy(acc, out, sem)
        copy.start()

        def add(i, total):
            part = acc[pl.ds(pl.multiple_of(i * clear, clear), clear), :]
            return total + jnp.sum((part * part).reshape(clear // 8, 8, LANES), 0)

        squares[...] = lax.fori_loop(0, half_entries // clear, add, jnp.zeros((8, LANES), F32))
        copy.wait()


def place_kernel(info, where, message, emb, spots, out):
    step = pl.program_id(0)
    count, own_rows, length_slots = emb.shape
    places = out.shape[1]
    block = LANES

    @pl.when(step == 0)
    def first():
        out[...] = jnp.zeros_like(out)

    for b in range(count):
        live = info[info[where[0] + step * where[1] + b, DEAL], 0]

        @pl.loop(0, pl.cdiv(live, block))
        def part(index):
            span = pl.ds(pl.multiple_of(index * block, block), block)
            rows = slot_gradients(b, message, emb, span)
            spot = jnp.broadcast_to(spots[b, 0:1, span], (block, block)).T
            spot = jnp.concatenate([spot] * (places // block), 1)
            hit = (spot == lax.broadcasted_iota(jnp.int32, (block, places), 1).astype(F32)).astype(F32).astype(BF)
            high_part, low_part = two_terms(rows)
            sums = jnp.dot(jnp.concatenate([high_part, low_part], 0), hit, preferred_element_type=F32)
            out[...] += sums[:LANES] + sums[LANES:]


def row_specs(message, emb, count):
    return [
        pl.BlockSpec((1,) + message.shape[1:], lambda i, *scalars: (i, 0, 0, 0)),
        pl.BlockSpec((count,) + emb.shape[1:], lambda i, *scalars: (i, 0, 0)),
    ]


def scatter(codes, info, core, group_index, pieces, emb, half_entries):
    groups = len(pieces)
    shards, count = pieces[0].shape[0], pieces[0].shape[1] - 1
    length_slots = emb.shape[2]
    whole = pl.BlockSpec(pieces[0].shape, lambda i, *scalars: (0, 0, 0, 0), pipeline_mode=pl.Buffered(1))
    return pl.pallas_call(
        functools.partial(scatter_kernel, half_entries, groups),
        name="scatter_rows",
        grid_spec=pltpu.PrefetchScalarGridSpec(
            num_scalar_prefetch=3,
            grid=(groups * shards,),
            in_specs=[whole] * groups + [pl.BlockSpec((count,) + emb.shape[1:], lambda i, *scalars: (i, 0, 0))],
            out_specs=[
                pl.BlockSpec(memory_space=pl.ANY),
                pl.BlockSpec((8, LANES), lambda i, *scalars: (0, 0)),
            ],
            scratch_shapes=[
                pltpu.VMEM((half_entries, LANES), F32),
                pltpu.VMEM((count, length_slots + LANES, LANES), F32),
                pltpu.VMEM((groups,) + pieces[0].shape, BF),
                pltpu.SemaphoreType.DMA,
            ],
        ),
        out_shape=[
            jax.ShapeDtypeStruct((half_entries, LANES), F32),
            jax.ShapeDtypeStruct((8, LANES), F32),
        ],
        compiler_params=pltpu.CompilerParams(vmem_limit_bytes=48 * MIB),
        cost_estimate=large_cost(),
    )(codes, info, jnp.stack([core, group_index]), *pieces, emb)


def place_sums(info, where, message, emb, spots, places):
    count = message.shape[1] - 1
    return pl.pallas_call(
        place_kernel,
        name="place_rows",
        grid_spec=pltpu.PrefetchScalarGridSpec(
            num_scalar_prefetch=2,
            grid=(message.shape[0],),
            in_specs=row_specs(message, emb, count)
            + [pl.BlockSpec((count,) + spots.shape[1:], lambda i, *scalars: (i, 0, 0))],
            out_specs=pl.BlockSpec((LANES, places), lambda i, *scalars: (0, 0)),
        ),
        out_shape=jax.ShapeDtypeStruct((LANES, places), F32),
        compiler_params=pltpu.CompilerParams(vmem_limit_bytes=16 * MIB),
        cost_estimate=large_cost(),
    )(info, where, message, emb, spots)


def adam_kernel(width, half_steps, factor, core, own, other, weight, first, second, new_weight, new_first, new_second):
    mine = (pl.program_id(0) // half_steps) == core[0]
    rows = jnp.where(mine, own[...], other[...]).T[0:width]
    out = adam_update(weight[...], first[...], second[...], rows, factor[0])
    new_weight[...], new_first[...], new_second[...] = out


def adam_table(factor, core, own, other, weight, first, second):
    width, entries = weight.shape
    block = 4096
    half_steps = own.shape[0] // block
    spec = pl.BlockSpec((width, block), lambda i, f, c: (0, i))

    def half_spec(flip):
        def index(i, f, c):
            start = jnp.bitwise_xor(c[0], flip) * half_steps
            return (jnp.clip(i - start, 0, half_steps - 1), 0)

        return pl.BlockSpec((block, LANES), index)

    return pl.pallas_call(
        functools.partial(adam_kernel, width, half_steps),
        name="adam_table",
        grid_spec=pltpu.PrefetchScalarGridSpec(
            num_scalar_prefetch=2,
            grid=(pl.cdiv(entries, block),),
            in_specs=[half_spec(0), half_spec(1), spec, spec, spec],
            out_specs=[spec, spec, spec],
        ),
        out_shape=[jax.ShapeDtypeStruct(weight.shape, F32)] * 3,
        compiler_params=pltpu.CompilerParams(vmem_limit_bytes=56 * MIB),
        cost_estimate=small_cost(),
    )(factor.reshape(1), core.reshape(1), own, other, weight, first, second)


def attention_kernel(lens, me, embedded, shard_bias, vectors, *rest):
    groups, _, width, length_slots = embedded.shape
    weights, (hidden_out, rows, rows_low, heads, context) = rest[:groups], rest[groups:]
    live = lens[pl.program_id(0)]
    big, small = 256, 128

    def over_blocks(block, work, blank):
        @pl.loop(0, length_slots // block)
        def one(index):
            span = pl.ds(pl.multiple_of(index * block, block), block)
            pl.when(index * block < live)(lambda: work(span))
            pl.when(index * block >= live)(lambda: blank(span))

    def norm_in(span):
        values = jnp.concatenate([embedded[g, 0, :, span].astype(F32) for g in range(groups)], 0).T
        state = normalise(values)[0] * vectors[0:1, :] + vectors[1:2, :]
        rows[span, :] = state
        rows_low[span, :] = state.astype(BF)

    def no_rows(span):
        rows[span, :] = jnp.zeros((small, groups * width), F32)
        rows_low[span, :] = jnp.zeros((small, groups * width), BF)

    over_blocks(small, norm_in, no_rows)

    def project(shard, span):
        weight, values = weights[shard], rows_low[span, :]
        place = jnp.bitwise_xor(me[0], shard)
        query = (mm_t(values, weight[0]) + shard_bias[pl.ds(place, 1), :]).astype(BF)
        heads[shard % 2, 0, span, :] = query * jnp.asarray(HDIM ** (-0.5), BF)
        heads[shard % 2, 1, span, :] = mm_t(values, weight[1]).astype(BF)
        heads[shard % 2, 2, span, :] = (mm_t(values, weight[2]) + shard_bias[pl.ds(groups + place, 1), :]).astype(BF)

    def no_heads(span):
        for i in range(6):
            heads[i // 3, i % 3, span, :] = jnp.zeros((big, width), BF)

    over_blocks(big, functools.partial(project, 0), no_heads)

    def attend(shard, reach, span):
        mask = jnp.where(lax.broadcasted_iota(jnp.int32, (1, reach), 1) < live, 0.0, -1e30)
        pieces = []
        for head in range(width // HDIM):
            part = slice(head * HDIM, (head + 1) * HDIM)
            scores = mm_t(heads[shard % 2, 0, span, part], heads[shard % 2, 1, 0:reach, part]) + mask
            shifted = jnp.exp(scores - jnp.max(scores, -1, keepdims=True))
            prob = shifted * (1.0 / jnp.sum(shifted, -1, keepdims=True))
            pieces.append(mm(prob.astype(BF), heads[shard % 2, 2, 0:reach, part]))
        context[shard, span, :] = jnp.concatenate(pieces, 1).astype(BF)
        if shard + 1 < groups:
            project(shard + 1, span)

    for shard in range(groups):

        @pl.when(live <= big)
        def short():
            attend(shard, big, pl.ds(0, big))

        @pl.when(live > big)
        def long():
            @pl.loop(0, length_slots // big)
            def one(index):
                span = pl.ds(pl.multiple_of(index * big, big), big)
                pl.when(index * big < live)(lambda: attend(shard, length_slots, span))

    def join(span):
        joined = rows[span, :] + vectors[4:5, :]
        for shard in range(groups):
            joined = joined + mm(context[shard, span, :], weights[shard][3])
        hidden_out[0, span, :] = normalise(joined)[0] * vectors[5:6, :] + vectors[6:7, :]

    def no_hidden(span):
        hidden_out[0, span, :] = jnp.zeros((big, groups * width), F32)

    over_blocks(big, join, no_hidden)


def feed_kernel(spread_rows, block, lens, me, hidden, vectors, *rest):
    groups = (len(rest) - 2) // 2
    wides, narrows, (state_low, first) = rest[:groups], rest[groups : 2 * groups], rest[2 * groups :]
    _, length_slots, model_width = hidden.shape
    live = lens[pl.program_id(0)]
    tail = 2 + 5 + spread_rows

    @pl.loop(0, length_slots // block)
    def one(index):
        span = pl.ds(pl.multiple_of(index * block, block), block)

        @pl.when(index * block < live)
        def work():
            rows = hidden[0, span, :]
            rows_low = rows.astype(BF)
            summed = rows + vectors[tail : tail + 1, :]
            for shard in range(groups):
                before = mm(rows_low, wides[shard][...]) + vectors[pl.ds(7 + jnp.bitwise_xor(me[0], shard), 1), :]
                active = (before * phi(before)).astype(BF)
                summed = summed + mm_t(active, narrows[shard][...])
            state = normalise(summed)[0] * vectors[tail + 1 : tail + 2, :] + vectors[tail + 2 : tail + 3, :]
            state_low[0, span, :] = state.astype(BF)

            @pl.when(index == 0)
            def keep():
                first[0] = state[0:8, :]

        @pl.when(index * block >= live)
        def blank():
            state_low[0, span, :] = jnp.zeros((block, model_width), BF)


def cls_kernel(spread_rows, lens, me, state_low, first, shard_bias, vectors, *rest):
    groups = (len(rest) - 1) // 2
    hidden_out = rest[-1]
    weights = [[rest[2 * i + j // 2].at[j % 2] for j in range(4)] for i in range(groups)]
    count, length_slots, model_width = state_low.shape
    width = model_width // groups
    shard_heads = width // HDIM
    base = 2 + 8 + spread_rows
    head_rows = 8
    head_mask = (
        lax.broadcasted_iota(jnp.int32, (head_rows, width), 0)
        == lax.broadcasted_iota(jnp.int32, (head_rows, width), 1) // HDIM
    ).astype(F32)
    starts = jnp.concatenate([first[b, 0:1, :] for b in range(count)], 0)
    starts_low = starts.astype(BF)
    tops = []
    places = [jnp.bitwise_xor(me[0], shard) for shard in range(groups)]
    for shard in range(groups):
        query = mm_t(starts_low, weights[shard][0][...]) + shard_bias[pl.ds(2 * groups + places[shard], 1), :]
        query = query.astype(BF).astype(F32)
        spread = jnp.concatenate(
            [jnp.broadcast_to(query[b : b + 1], head_mask.shape) * head_mask for b in range(count)], 0
        )
        tops.append(mm(spread.astype(BF), weights[shard][1][...]))
    bars, masses = [], []
    all_rows = groups * head_rows
    slot_index = lax.broadcasted_iota(jnp.int32, (all_rows, length_slots), 1)
    for b in range(count):
        own = jnp.concatenate([top[b * head_rows : (b + 1) * head_rows] for top in tops], 0)
        high_part, low_part = two_terms(own)
        scores = mm_t(jnp.concatenate([high_part, low_part], 0), state_low[b])
        scores = (scores[:all_rows] + scores[all_rows:]) * HDIM ** (-0.5)
        scores = jnp.where(slot_index < lens[b], scores, -1e30)
        shifted = jnp.exp(scores - jnp.max(scores, -1, keepdims=True))
        prob_low = (shifted / jnp.sum(shifted, -1, keepdims=True)).astype(BF)
        bars.append(mm(prob_low, state_low[b]))
        masses.append(jnp.sum(prob_low.astype(F32), -1, keepdims=True))
    joined = starts + vectors[base + 2 : base + 3, :]
    for shard in range(groups):
        part = slice(shard * head_rows, (shard + 1) * head_rows)
        own = jnp.concatenate([bar[part] for bar in bars], 0)
        mass = jnp.concatenate([mass[part] for mass in masses], 0)
        high_part, low_part = two_terms(own)
        full = mm_t(jnp.concatenate([high_part, low_part], 0), weights[shard][2][...])
        full = full[: count * head_rows] + full[count * head_rows :] + mass * shard_bias[pl.ds(3 * groups + places[shard], 1), :]
        context = jnp.concatenate(
            [
                jnp.sum(full[b * head_rows : (b + 1) * head_rows] * head_mask, 0, keepdims=True)
                for b in range(count)
            ],
            0,
        )
        joined = joined + mm(context.astype(BF), weights[shard][3][...])
    hidden_out[...] = normalise(joined)[0] * vectors[base + 3 : base + 4, :] + vectors[base + 4 : base + 5, :]


def teacher_forward(embedded, shard_bias, shard_pieces, narrow_pieces, cls_pieces, student_parts, feedforward, pooler, vectors, lens, group_index):
    groups, count, width, length_slots = embedded.shape
    model_width = groups * width
    first_attention, wides = shard_pieces
    student_embedded, side_own = student_parts
    local_units = feedforward.shape[-1]
    spread_rows = local_units * groups // model_width
    block_rows = 8 + spread_rows
    one, two = vectors[2 : 2 + block_rows], vectors[2 + block_rows : 2 + 2 * block_rows]
    assert local_units == model_width
    me = group_index.reshape(1)

    def whole(values):
        return pl.BlockSpec(values.shape, lambda i, *scalars: (0,) * values.ndim, pipeline_mode=pl.Buffered(1))

    each = pl.BlockSpec((1, length_slots, model_width), lambda i, *scalars: (i, 0, 0))
    hidden = pl.pallas_call(
        attention_kernel,
        name="teacher_attention",
        grid_spec=pltpu.PrefetchScalarGridSpec(
            num_scalar_prefetch=2,
            grid=(count,),
            in_specs=[
                pl.BlockSpec((groups, 1, width, length_slots), lambda i, *scalars: (0, i, 0, 0)),
                whole(shard_bias),
                whole(vectors),
            ]
            + [whole(piece) for piece in first_attention],
            out_specs=each,
            scratch_shapes=[
                pltpu.VMEM((length_slots, model_width), F32),
                pltpu.VMEM((length_slots, model_width), BF),
                pltpu.VMEM((2, 3, length_slots, width), BF),
                pltpu.VMEM((groups, length_slots, width), BF),
            ],
        ),
        out_shape=jax.ShapeDtypeStruct((count, length_slots, model_width), F32),
        compiler_params=pltpu.CompilerParams(vmem_limit_bytes=40 * MIB),
        cost_estimate=small_cost(),
    )(lens, me, embedded, shard_bias, vectors, *first_attention)
    own, near, far = narrow_pieces
    cls_own, cls_near, cls_far = cls_pieces
    hidden, near, far = lax.optimization_barrier((hidden, near, far))
    narrows = [own, near, far, group_swap(far, 1, groups)]
    state_low, first = pl.pallas_call(
        functools.partial(feed_kernel, spread_rows, 256),
        name="teacher_feed",
        grid_spec=pltpu.PrefetchScalarGridSpec(
            num_scalar_prefetch=2,
            grid=(count,),
            in_specs=[each, whole(vectors)] + [whole(piece) for piece in wides + narrows],
            out_specs=[each, pl.BlockSpec((1, 8, model_width), lambda i, *scalars: (i, 0, 0))],
        ),
        out_shape=[
            jax.ShapeDtypeStruct((count, length_slots, model_width), BF),
            jax.ShapeDtypeStruct((count, 8, model_width), F32),
        ],
        compiler_params=pltpu.CompilerParams(vmem_limit_bytes=50 * MIB),
        cost_estimate=small_cost(),
    )(lens, me, hidden, vectors, *wides, *narrows)
    state_low, cls_near, cls_far, student_embedded = lax.optimization_barrier(
        (state_low, cls_near, cls_far, student_embedded)
    )
    cls_last, side_own = lax.optimization_barrier(([group_swap(part, 1, groups) for part in cls_far], side_own))
    second_attention = [*cls_own, *cls_near, *cls_far, *cls_last]
    side_far = group_swap(side_own, 1, groups)
    hidden = pl.pallas_call(
        functools.partial(cls_kernel, spread_rows),
        name="teacher_cls",
        grid_spec=pltpu.PrefetchScalarGridSpec(
            num_scalar_prefetch=2,
            grid=(1,),
            in_specs=[whole(array) for array in (state_low, first, shard_bias, vectors, *second_attention)],
            out_specs=pl.BlockSpec((count, model_width), lambda i, *scalars: (0, 0)),
        ),
        out_shape=jax.ShapeDtypeStruct((count, model_width), F32),
        compiler_params=pltpu.CompilerParams(vmem_limit_bytes=58 * MIB),
        cost_estimate=small_cost(),
    )(lens, me, state_low, first, shard_bias, vectors, *second_attention)
    everyone = spread_to(hidden.astype(BF), "grp", groups).reshape(-1, model_width)
    unit_bias = lax.dynamic_slice_in_dim(two[5 : 5 + spread_rows].reshape(-1), group_index * local_units, local_units)
    before = ein("sd,df->sf", everyone, feedforward[1, 0]) + unit_bias
    active = jax.nn.gelu(before, approximate=False).astype(BF)
    partial_rows = ein("sf,df->sd", active, feedforward[1, 1]).reshape(groups, count, model_width)
    total = jnp.sum(exchange(partial_rows, "grp"), 0)
    summed = hidden + total + two[5 + spread_rows]
    cls = layer_norm(summed, two[6 + spread_rows], two[7 + spread_rows])
    pool = jnp.tanh(ein("sd,de->se", cls.astype(BF), pooler) + vectors[2 + 2 * block_rows])
    logits = ein("sd,cd->sc", pool.astype(BF), vectors[3 + 2 * block_rows :].astype(BF))
    return cls, logits, (student_embedded, side_own, side_far)


NT = (((1,), (1,)), ((), ()))
HEAD_ROWS = 16
MISC_ROWS = 8
SEQ_ROWS = MISC_ROWS + 2 * HEAD_ROWS
SMALL_ROWS = 24


def mm(left, right):
    return jnp.dot(left, right, preferred_element_type=F32)


def mm_t(left, right):
    return lax.dot_general(left, right, NT, preferred_element_type=F32)


def row_mean(values):
    return jnp.mean(values, -1, keepdims=True)


def normalise(values):
    center = values - row_mean(values)
    rstd = lax.rsqrt(row_mean(center * center) + layer_eps)
    return center * rstd, rstd


def normal_back(normal, rstd, cotangent):
    return rstd * (cotangent - row_mean(cotangent) - normal * row_mean(cotangent * normal))


def phi(values):
    return 0.5 * (1.0 + lax.erf(values * 0.5**0.5))


def log_soft(values, live):
    shifted = jnp.where(live, values, -1e30)
    shifted = shifted - jnp.max(shifted, -1, keepdims=True)
    return shifted - jnp.log(jnp.sum(jnp.where(live, jnp.exp(shifted), 0.0), -1, keepdims=True))


def student_kernel(
    total_count,
    classes,
    lens,
    labels,
    swapped,
    emb,
    side_own,
    side_far,
    small,
    bias,
    teacher_cls,
    teacher_logits,
    message,
    shares,
    rows_in,
    rows_low,
    normal_low,
    stats,
):
    shards, count, own_rows, length_slots = emb.shape
    model_width = shards * own_rows
    half = model_width // 2
    spread_rows = (side_own.shape[1] // half - 5) // 2
    unit_half = spread_rows * half
    far = swapped[0] == 1
    scale = HDIM ** (-0.5)
    block = 128

    def small_row(index, rows=1):
        return small[index : index + rows, :]

    def weight(index):
        span = slice(index * half, (index + 1) * half)
        return side_own[:, span], side_far[:, span]

    def units():
        span = slice(5 * half, 5 * half + unit_half)
        return side_own[:, span], side_far[:, span]

    def narrow(index):
        return weight(5 + spread_rows + index)

    def narrow_parts(values):
        return [
            jnp.concatenate(
                [
                    values[:, (f * spread_rows + j) * own_rows : (f * spread_rows + j + 1) * own_rows]
                    for f in range(shards)
                ],
                1,
            )
            for j in range(spread_rows)
        ]

    def in_units(parts):
        return jnp.concatenate(
            [part[:, f * own_rows : (f + 1) * own_rows] for f in range(shards) for part in parts], 1
        )

    def forward(values, pair):
        one, two = mm(values, pair[0]), mm(values, pair[1])
        return jnp.where(far, jnp.concatenate([two, one], 1), jnp.concatenate([one, two], 1))

    def backward(values, pair):
        middle = values.shape[1] // 2
        low_part, high_part = values[:, :middle].astype(F32), values[:, middle:].astype(F32)
        one = jnp.where(far, high_part, low_part).astype(BF)
        two = jnp.where(far, low_part, high_part).astype(BF)
        return mm_t(one, pair[0]) + mm_t(two, pair[1])

    def both(values):
        return jnp.concatenate(two_terms(values), 0)

    def fold(values):
        middle = values.shape[0] // 2
        return values[:middle] + values[middle:]

    head_mask = (
        lax.broadcasted_iota(jnp.int32, (HEAD_ROWS, model_width), 0)
        == lax.broadcasted_iota(jnp.int32, (HEAD_ROWS, model_width), 1) // HDIM
    ).astype(F32)
    heads = model_width // HDIM

    def by_head(values):
        return jnp.concatenate(
            [jnp.broadcast_to(values[b : b + 1], head_mask.shape) * head_mask for b in range(count)], 0
        )

    def from_head(values):
        return jnp.concatenate(
            [
                jnp.sum(values[b * HEAD_ROWS : (b + 1) * HEAD_ROWS] * head_mask, 0, keepdims=True)
                for b in range(count)
            ],
            0,
        )

    def head_rows(values, b):
        return values[b * HEAD_ROWS : (b + 1) * HEAD_ROWS]

    firsts = []
    for b in range(count):

        def norm_rows(index, carry):
            start = pl.multiple_of(index * block, block)
            span = pl.ds(start, block)
            values = jnp.concatenate([emb[f, b, :, span].astype(F32) for f in range(shards)], 0).T
            mean = row_mean(values)
            center = values - mean
            rstd = lax.rsqrt(row_mean(center * center) + layer_eps)
            normal = center * rstd
            rows_in[b, span, :] = values.astype(BF)
            normal_low[b, span, :] = normal.astype(BF)
            rows_low[b, span, :] = (normal * small_row(0) + small_row(1)).astype(BF)
            stats[b, 0:8, span] = jnp.broadcast_to(mean, (block, LANES)).T[0:8]
            stats[b, 8:16, span] = jnp.broadcast_to(rstd, (block, LANES)).T[0:8]
            return carry

        def no_rows(index, carry):
            span = pl.ds(pl.multiple_of(index * block, block), block)
            for rows in (rows_in, normal_low, rows_low):
                rows[b, span, :] = jnp.zeros((block, model_width), BF)
            stats[b, :, span] = jnp.zeros((16, block), F32)
            return carry

        used = pl.cdiv(lens[b], block)
        lax.fori_loop(0, used, norm_rows, 0)
        lax.fori_loop(used, length_slots // block, no_rows, 0)
        start_row = rows_in[b, 0:16, :].astype(F32)
        firsts.append((normalise(start_row)[0] * small_row(0) + small_row(1))[0:1])
    first = jnp.concatenate(firsts, 0)
    first_low = first.astype(BF)

    query = (forward(first_low, weight(0)) + small_row(2)).astype(BF)
    key_tops = backward(by_head(query.astype(F32)).astype(BF), weight(1))
    row_index = lax.broadcasted_iota(jnp.int32, (HEAD_ROWS, length_slots), 0)
    slot_index = lax.broadcasted_iota(jnp.int32, (HEAD_ROWS, length_slots), 1)
    probs, bars, masses = [], [], []
    for b in range(count):
        scores = fold(mm_t(both(head_rows(key_tops, b)), rows_low[b])) * scale
        scores = jnp.where(slot_index < lens[b], scores, -1e30)
        shifted = jnp.exp(scores - jnp.max(scores, -1, keepdims=True))
        prob = shifted / jnp.sum(shifted, -1, keepdims=True)
        prob = jnp.where(row_index < heads, prob, 0.0)
        prob_low = prob.astype(BF)
        probs.append(prob)
        bars.append(mm(prob_low, rows_low[b]))
        masses.append(jnp.sum(prob_low.astype(F32), -1, keepdims=True))
    bars = jnp.concatenate(bars, 0)
    masses = jnp.concatenate(masses, 0)
    context = from_head(fold(forward(both(bars), weight(2))) + masses * small_row(3))
    context_low = context.astype(BF)
    joined = first + forward(context_low, weight(3)) + small_row(4)
    normal_one, rstd_one = normalise(joined)
    hidden = normal_one * small_row(5) + small_row(6)
    hidden_low = hidden.astype(BF)
    unit_bias = jnp.concatenate([small_row(7 + i) for i in range(spread_rows)], 1)
    before = forward(hidden_low, units()) + unit_bias
    gate = phi(before)
    active = (before * gate).astype(BF)
    s = 7 + spread_rows
    active_parts = [part.astype(BF) for part in narrow_parts(active.astype(F32))]
    summed = hidden + small_row(s)
    for j in range(spread_rows):
        summed = summed + forward(active_parts[j], narrow(j))
    normal_two, rstd_two = normalise(summed)
    vector = normal_two * small_row(s + 1) + small_row(s + 2)
    vector_low = vector.astype(BF)
    pooled = jnp.tanh(forward(vector_low, weight(4)) + small_row(s + 3))
    pooled_low = pooled.astype(BF)
    class_rows = jnp.concatenate(
        [small_row(s + 4, classes), jnp.zeros((LANES - classes, model_width), F32)], 0
    ).astype(BF)
    lane = lax.broadcasted_iota(jnp.int32, (count, LANES), 1)
    live = lane < classes
    logits = mm_t(pooled_low, class_rows) + bias[...]

    label = jnp.concatenate([jnp.full((1, LANES), labels[b], jnp.int32) for b in range(count)], 0)
    hit = (lane == label).astype(F32)
    log_prob = log_soft(logits, live)
    teacher_soft = log_soft(teacher_logits[...] / temper, live)
    student_soft = log_soft(logits / temper, live)
    teacher_prob = jnp.where(live, jnp.exp(teacher_soft), 0.0)
    loss = jnp.sum(jnp.where(hit > 0, -log_prob, 0.0), -1, keepdims=True)
    gap = jnp.where(live, teacher_soft - student_soft, 0.0)
    loss = loss + temper * temper * jnp.sum(teacher_prob * gap, -1, keepdims=True)
    inverse = lax.rsqrt(jnp.sum(vector * vector, -1, keepdims=True) + dist_eps)
    student_unit = vector * inverse
    teacher_rows = teacher_cls[...]
    teacher_unit = teacher_rows * lax.rsqrt(jnp.sum(teacher_rows * teacher_rows, -1, keepdims=True) + dist_eps)
    apart = student_unit - teacher_unit
    loss = loss + 100.0 * jnp.sum(apart * apart, -1, keepdims=True)
    d_logits = jnp.where(live, jnp.exp(log_prob), 0.0) - hit
    soft_mass = jnp.sum(teacher_prob, -1, keepdims=True)
    d_logits = d_logits + temper * (jnp.where(live, jnp.exp(student_soft), 0.0) * soft_mass - teacher_prob)
    d_logits = d_logits / total_count
    d_unit = 200.0 / total_count * apart
    d_vector = inverse * (d_unit - student_unit * jnp.sum(student_unit * d_unit, -1, keepdims=True))

    pooled_wide = pooled_low.astype(F32)
    class_wide = class_rows.astype(F32)
    d_pooled = jnp.zeros((count, model_width), F32)
    class_grads = []
    for c in range(classes):
        part = d_logits[:, c : c + 1]
        d_pooled = d_pooled + part * class_wide[c : c + 1]
        class_grads.append(jnp.sum(part * pooled_wide, 0, keepdims=True))
    d_pool = d_pooled * (1.0 - pooled * pooled)
    pool_high, pool_rest = two_terms(d_pool)
    pool_mid, pool_last = two_terms(d_pool - pool_high.astype(F32))
    pool_back = backward(jnp.concatenate([pool_high, pool_mid, pool_last], 0), weight(4))
    d_vector = d_vector + pool_back[:count] + pool_back[count : 2 * count] + pool_back[2 * count :]
    d_summed = normal_back(normal_two, rstd_two, d_vector * small_row(s + 1))
    d_output = d_summed.astype(BF)
    d_active = in_units([backward(d_output, narrow(j)) for j in range(spread_rows)])
    slope_gate = gate + before * jnp.exp(-0.5 * before * before) * (2.0 * 3.141592653589793) ** -0.5
    d_before = (slope_gate * d_active).astype(BF)
    d_hidden = d_summed + backward(d_before, units())
    d_joined = normal_back(normal_one, rstd_one, d_hidden * small_row(5))
    d_branch = d_joined.astype(BF)
    d_context = backward(d_branch, weight(3)).astype(BF)
    context_heads = by_head(d_context.astype(F32))
    val_tops = backward(context_heads.astype(BF), weight(2))
    constant = jnp.sum(context_heads * small_row(3), -1, keepdims=True)
    d_scores, d_bars = [], []
    for b in range(count):
        d_prob = fold(mm_t(both(head_rows(val_tops, b)), rows_low[b])) + head_rows(constant, b)
        prob = probs[b]
        d_score = (prob * (d_prob - jnp.sum(prob * d_prob, -1, keepdims=True))).astype(BF)
        d_scores.append(d_score)
        d_bars.append(mm(d_score, rows_low[b]))
    d_bars = jnp.concatenate(d_bars, 0)
    d_query = (from_head(fold(forward(both(d_bars), weight(1)))) * scale).astype(BF)
    d_first = d_joined + backward(d_query, weight(0))

    d_gain = jnp.zeros((1, model_width), F32)
    d_shift = jnp.zeros((1, model_width), F32)
    top_row = lax.broadcasted_iota(jnp.int32, (HEAD_ROWS, model_width), 0)
    for b in range(count):
        tops = jnp.concatenate(
            [
                jnp.where(top_row == 12, d_first[b : b + 1], head_rows(val_tops, b)),
                head_rows(key_tops, b) * scale,
            ],
            0,
        )
        start_slot = jnp.where(slot_index == 0, 1.0, 0.0)
        value_side = jnp.where(row_index == 12, start_slot, probs[b].astype(BF).astype(F32))
        score_side = d_scores[b].astype(F32)
        coef = jnp.concatenate([value_side, score_side], 0)
        d_shift = d_shift + jnp.sum(jnp.sum(coef, -1, keepdims=True) * tops, 0, keepdims=True)
        d_gain = d_gain + jnp.sum(mm(coef.astype(BF), normal_low[b]) * tops, 0, keepdims=True)
        scaled = tops * small_row(0)
        scaled_sum = jnp.sum(scaled, -1, keepdims=True)
        along = fold(mm_t(both(scaled), rows_in[b]))
        mean, rstd = stats[b, 0:1, :], stats[b, 8:9, :]
        live_slot = slot_index[0:1] < lens[b]
        slope = rstd * rstd * rstd * (1.0 / model_width) * jnp.sum(coef * (along - mean * scaled_sum), 0, keepdims=True)
        shift = mean * slope - rstd * (1.0 / model_width) * jnp.sum(coef * scaled_sum, 0, keepdims=True)

        def insert(values, first_row, extra):
            for term in two_terms(jnp.where(live_slot, extra, 0.0)):
                values = jnp.where(row_index == first_row, term.astype(F32), values)
                first_row += 1
            return values

        value_side = insert(value_side, 13, rstd)
        score_side = insert(insert(score_side, 12, shift), 14, slope)
        packed = jnp.concatenate([value_side, score_side], 0).astype(BF)
        top_terms = two_terms(scaled)
        for f in range(shards):
            message[f, b] = packed
            for i, term in enumerate(top_terms):
                start = (2 * b + i) * LANES
                part = term[:, f * own_rows : (f + 1) * own_rows].astype(F32)
                part = jnp.concatenate([part, jnp.zeros((COEF, LANES - own_rows), F32)], 1)
                message[f, count, :, start : start + LANES] = part.astype(BF)

    def sum_rows(values):
        return jnp.sum(values.astype(F32), 0, keepdims=True)

    small_grads = jnp.concatenate(
        [
            d_gain,
            d_shift,
            sum_rows(d_query),
            sum_rows(context_heads * masses),
            sum_rows(d_branch),
            sum_rows(d_hidden * normal_one),
            sum_rows(d_hidden),
        ]
        + [sum_rows(d_before[:, i * model_width : (i + 1) * model_width]) for i in range(spread_rows)]
        + [sum_rows(d_output), sum_rows(d_vector * normal_two), sum_rows(d_vector), sum_rows(d_pool)]
        + class_grads
        + [jnp.zeros((SMALL_ROWS - small.shape[0], model_width), F32)],
        0,
    )
    scalars = jnp.where(
        lane[0:1] == classes, jnp.sum(loss, 0, keepdims=True) / total_count, jnp.sum(d_logits, 0, keepdims=True)
    )
    scalars = jnp.where(lane[0:1] <= classes, scalars, 0.0)
    third = own_rows // 3
    small_index = lax.broadcasted_iota(jnp.int32, (SMALL_ROWS, own_rows), 0)
    for f in range(shards):
        span = slice(f * own_rows, (f + 1) * own_rows)
        rows = []
        for b in range(count):
            one = slice(b, b + 1)
            rows += [values[one, span].astype(F32) for values in (first_low, context_low, hidden_low, vector_low)]
            rows += [part[one, span].astype(F32) for part in active_parts]
            rows += [head_rows(bars, b)[:, span], head_rows(d_bars, b)[:, span]]
        rows.append(jnp.where(small_index == small.shape[0], scalars[:, 0:own_rows], small_grads[:, span]))
        rows.append(jnp.zeros((LANES - count * SEQ_ROWS - SMALL_ROWS, own_rows), F32))
        for i, term in enumerate(two_terms(jnp.concatenate(rows, 0).T)):
            for q in range(3):
                start = 2 * q * LANES + i * LANES
                shares[f, count * HEAD_ROWS :, start : start + LANES] = term[q * third : (q + 1) * third]
    for b in range(count):
        one = slice(b, b + 1)
        rows = [values[one].astype(F32) for values in (d_query, query, d_context, d_branch, pool_high, pool_mid)]
        rows += [d_before[one, i * model_width : (i + 1) * model_width].astype(F32) for i in range(spread_rows)]
        rows += [d_output[one].astype(F32), jnp.zeros((HEAD_ROWS - 7 - spread_rows, model_width), F32)]
        rows = jnp.concatenate(rows, 0).astype(BF)
        for f in range(shards):
            shares[f, b * HEAD_ROWS : (b + 1) * HEAD_ROWS, :] = rows


def student_step(emb, sides, small, bias, lens, labels, swapped, teacher_cls, teacher_logits, total_count):
    shards, count, own_rows, length_slots = emb.shape
    assert 2 * count * LANES <= length_slots and count * SEQ_ROWS + SMALL_ROWS <= LANES
    model_width = small.shape[1]
    classes = bias.shape[0]

    def wide(values):
        return jnp.pad(values, ((0, 0), (0, LANES - values.shape[1])))

    smem = pl.BlockSpec(memory_space=pltpu.SMEM)
    vmem = pl.BlockSpec(memory_space=pltpu.VMEM)
    return pl.pallas_call(
        functools.partial(student_kernel, total_count, classes),
        name="student",
        in_specs=[smem] * 3 + [vmem] * 7,
        out_specs=[vmem] * 2,
        out_shape=[
            jax.ShapeDtypeStruct((shards, count + 1, COEF, length_slots), BF),
            jax.ShapeDtypeStruct((shards, count * HEAD_ROWS + own_rows // 3, model_width), BF),
        ],
        scratch_shapes=[pltpu.VMEM((count, length_slots, model_width), BF)] * 3
        + [pltpu.VMEM((count, 16, length_slots), F32)],
        compiler_params=pltpu.CompilerParams(vmem_limit_bytes=52 * MIB),
        cost_estimate=small_cost(),
    )(
        lens,
        labels,
        swapped.reshape(1),
        emb,
        *sides,
        small,
        wide(bias[None]),
        teacher_cls,
        wide(teacher_logits),
    )


def adam_update(weight, moment_one, moment_two, gradient, factor):
    gradient = gradient * factor
    first_new = beta_one * moment_one + (1.0 - beta_one) * gradient
    second_new = beta_two * moment_two + (1.0 - beta_two) * gradient * gradient
    first_hat = first_new / (1.0 - beta_one**adam_steps)
    second_hat = second_new / (1.0 - beta_two**adam_steps)
    weight_new = weight - learn_rate * (first_hat / (jnp.sqrt(second_hat) + adam_eps) + decay_rate * weight)
    return (weight_new, first_new, second_new)


TN = (((0,), (0,)), ((), ()))


def tm(left, right):
    return lax.dot_general(left, right, TN, preferred_element_type=F32)


def grads_kernel(groups, group_index, *refs):
    shares, parts = refs[:groups], refs[groups : 2 * groups]
    word_squares, square, widen, narrow, place, payload = refs[2 * groups : 2 * groups + 6]
    factors, wide, bars, d_bars, masked, place_parts, smalls = refs[2 * groups + 6 :]
    shards, _, model_width = shares[0].shape
    own_rows = square.shape[0]
    third = own_rows // 3
    count = factors.shape[0] // (groups * shards)
    spread_rows = narrow.shape[0] // own_rows
    pairs = groups * shards
    base = count * SEQ_ROWS
    head_mask = (
        lax.broadcasted_iota(jnp.int32, (HEAD_ROWS, model_width), 0)
        == lax.broadcasted_iota(jnp.int32, (HEAD_ROWS, model_width), 1) // HDIM
    ).astype(F32)

    for distance in range(groups):
        group = jnp.bitwise_xor(group_index[0], distance)
        share = shares[distance]
        place_parts[group] = parts[distance][...]

        @pl.loop(0, shards, unroll=4)
        def shard(f):
            pair = group * shards + f
            both = jnp.concatenate(
                [
                    share[f, count * HEAD_ROWS :, 2 * q * LANES : 2 * (q + 1) * LANES].astype(F32)
                    for q in range(3)
                ],
                0,
            )
            left = (both[:, :LANES] + both[:, LANES:]).T
            smalls[pair] = left[base : base + SMALL_ROWS]
            for b in range(count):
                seq = pair * count + b
                start = b * SEQ_ROWS
                factors[seq] = left[start : start + MISC_ROWS]
                bars[seq] = left[start + MISC_ROWS : start + MISC_ROWS + HEAD_ROWS]
                d_bars[seq] = left[start + MISC_ROWS + HEAD_ROWS : start + SEQ_ROWS]
                wide[seq] = share[f, b * HEAD_ROWS : (b + 1) * HEAD_ROWS, :].astype(F32)

    def factor(index):
        return factors[:, index, :].astype(BF)

    def side(index):
        return wide[:, index, :].astype(BF)

    def heads(rows, index):
        @pl.loop(0, pairs * count, unroll=8)
        def spread(seq):
            row = wide[seq, index : index + 1, :]
            start = pl.multiple_of(seq * HEAD_ROWS, HEAD_ROWS)
            masked[pl.ds(start, HEAD_ROWS), :] = (jnp.broadcast_to(row, head_mask.shape) * head_mask).astype(BF)

        high_part, low_part = two_terms(rows[...].reshape(pairs * count * HEAD_ROWS, own_rows))
        return tm(high_part, masked[...]) + tm(low_part, masked[...])

    total = jnp.zeros((), F32)
    blocks = [
        tm(factor(0), side(0)),
        heads(d_bars, 1) * HDIM ** (-0.5),
        heads(bars, 2),
        tm(factor(1), side(3)),
        tm(factor(3), side(4)) + tm(factor(3), side(5)),
    ]
    for i, block in enumerate(blocks):
        square[:, i * model_width : (i + 1) * model_width] = block
        total = total + jnp.sum(block * block)
    for i in range(spread_rows):
        block = tm(factor(2), side(6 + i))
        widen[:, i * model_width : (i + 1) * model_width] = block
        total = total + jnp.sum(block * block)
        block = tm(factor(4 + i), side(6 + spread_rows))
        narrow[i * own_rows : (i + 1) * own_rows, :] = block
        total = total + jnp.sum(block * block)
    places = place_parts[0]
    for g in range(1, groups):
        places = places + place_parts[g]
    places = places[0:own_rows]
    place[...] = places
    total = total + jnp.sum(places * places)
    small = smalls[0]
    for p in range(1, pairs):
        small = small + smalls[p]
    rows = lax.broadcasted_iota(jnp.int32, small.shape, 0)
    lanes = lax.broadcasted_iota(jnp.int32, small.shape, 1)
    small = jnp.where(rows == SMALL_ROWS - 1, jnp.where(lanes == 0, total, jnp.sum(word_squares[...])), small)
    for d in range(payload.shape[0]):
        payload[d] = small


def weight_grads(group_index, shares, place_parts, word_squares, devices, own_rows):
    groups = len(shares)
    shards, share_rows, model_width = shares[0].shape
    count = (share_rows - own_rows // 3) // HEAD_ROWS
    places = place_parts[0].shape[1]
    right_rows = HEAD_ROWS
    spread_rows = MISC_ROWS - 4
    smem = pl.BlockSpec(memory_space=pltpu.SMEM)
    vmem = pl.BlockSpec(memory_space=pltpu.VMEM)
    seqs = groups * shards * count
    return pl.pallas_call(
        functools.partial(grads_kernel, groups),
        name="weight_grads",
        in_specs=[smem] + [vmem] * (2 * groups + 1),
        out_specs=[vmem] * 5,
        out_shape=[
            jax.ShapeDtypeStruct((own_rows, 5 * model_width), F32),
            jax.ShapeDtypeStruct((own_rows, spread_rows * model_width), F32),
            jax.ShapeDtypeStruct((spread_rows * own_rows, model_width), F32),
            jax.ShapeDtypeStruct((own_rows, places), F32),
            jax.ShapeDtypeStruct((devices, SMALL_ROWS, own_rows), F32),
        ],
        scratch_shapes=[
            pltpu.VMEM((seqs, MISC_ROWS, own_rows), F32),
            pltpu.VMEM((seqs, right_rows, model_width), F32),
            pltpu.VMEM((seqs, HEAD_ROWS, own_rows), F32),
            pltpu.VMEM((seqs, HEAD_ROWS, own_rows), F32),
            pltpu.VMEM((seqs * HEAD_ROWS, model_width), BF),
            pltpu.VMEM((groups,) + place_parts[0].shape, F32),
            pltpu.VMEM((groups * shards, SMALL_ROWS, own_rows), F32),
        ],
        compiler_params=pltpu.CompilerParams(vmem_limit_bytes=58 * MIB),
        cost_estimate=small_cost(),
    )(group_index.reshape(1), *shares, *place_parts, word_squares)


def norm_kernel(classes, core, parts, others, *refs):
    grads, refs = refs[:4], refs[4:]
    states, (factor_out, scalars), outs = refs[:18], refs[18:20], refs[20:]
    devices, _, own_rows = parts.shape
    rows_all = states[12].shape[0]
    joined = jnp.concatenate([parts[d] for d in range(devices)], 1)
    last = SMALL_ROWS - 1
    total = jnp.zeros((1, 1), F32)
    mine = jnp.zeros((1, 1), F32)
    other = jnp.zeros((1, 1), F32)
    for d in range(devices):
        total = total + parts[d, last : last + 1, 0:1]
        mine = mine + parts[d, last : last + 1, 1:2]
        other = other + others[d, last : last + 1, 1:2]
    first = jnp.where(core[0] == 0, mine, other)
    second = jnp.where(core[0] == 0, other, mine)
    small_grad = joined[0:rows_all]
    extra = parts[0, rows_all : rows_all + 1, :]
    lane = lax.broadcasted_iota(jnp.int32, extra.shape, 1)
    bias_grad = extra[:, 0:classes]
    total = total + first + second
    total = total + jnp.sum(jnp.sum(small_grad * small_grad, 1, keepdims=True), 0, keepdims=True)
    total = total + jnp.sum(bias_grad * bias_grad, 1, keepdims=True)
    norm = jnp.sqrt(total)
    factor = jnp.minimum(1.0, clip_bound / norm)
    factor_out[...] = jnp.broadcast_to(factor, factor_out.shape)
    loss = jnp.sum(jnp.where(lane == classes, extra, 0.0), 1, keepdims=True)
    lanes = lax.broadcasted_iota(jnp.int32, scalars.shape, 1)
    scalars[...] = jnp.where(lanes == 0, jnp.broadcast_to(loss, scalars.shape), jnp.broadcast_to(norm, scalars.shape))

    def update(index, gradient):
        weight, moment_one, moment_two = (states[3 * index + j][...] for j in range(3))
        new = adam_update(weight, moment_one, moment_two, gradient, factor)
        for j in range(3):
            outs[3 * index + j][...] = new[j]

    for index, grad in enumerate(grads):
        update(index, grad[...])
    update(4, small_grad)
    update(5, bias_grad)


def norm_step(core, parts, others, grads, states):
    classes = states[5][0].shape[0]
    steps = 3

    def whole(array):
        return pl.BlockSpec(array.shape, lambda i, *scalars: (0,) * array.ndim)

    def block(array):
        return pl.BlockSpec((array.shape[0] // steps, array.shape[1]), lambda i, *scalars: (i, 0))

    flat = [array[None] if array.ndim == 1 else array for state in states for array in state]
    flat_specs = [block(array) for array in flat[:12]] + [whole(array) for array in flat[12:]]
    row = jax.ShapeDtypeStruct((1, LANES), F32)
    outs = pl.pallas_call(
        functools.partial(norm_kernel, classes),
        name="norm",
        grid_spec=pltpu.PrefetchScalarGridSpec(
            num_scalar_prefetch=1,
            grid=(steps,),
            in_specs=[whole(parts), whole(others)] + [block(grad) for grad in grads] + flat_specs,
            out_specs=[whole(row), whole(row)] + flat_specs,
        ),
        out_shape=[row, row] + [jax.ShapeDtypeStruct(array.shape, F32) for array in flat],
        compiler_params=pltpu.CompilerParams(vmem_limit_bytes=48 * MIB),
        cost_estimate=small_cost(),
    )(core.reshape(1), parts, others, *grads, *flat)
    rest = [out[0] if out.shape[0] == 1 else out for out in outs[2:]]
    return outs[0], outs[1], rest


def on_device(
    tokens,
    positions,
    lengths,
    labels,
    word_table,
    word_first,
    word_second,
    place_table,
    place_first,
    place_second,
    square_weights,
    square_first,
    square_second,
    widen_weights,
    widen_first,
    widen_second,
    narrow_weights,
    narrow_first,
    narrow_second,
    small_params,
    small_first,
    small_second,
    class_bias,
    class_first,
    class_second,
    teacher_word,
    teacher_place,
    teacher_attention,
    teacher_feedforward,
    teacher_pooler,
    teacher_vectors,
):
    shards = lax.axis_size("fsdp")
    groups = lax.axis_size("grp")
    shard_index = lax.axis_index("fsdp")
    group_index = lax.axis_index("grp")
    count, length_slots = tokens.shape
    model_width = small_params.shape[1]
    own_rows = word_table.shape[0]
    entries = word_table.shape[1]
    places = place_table.shape[1]
    spread_rows = widen_weights.shape[1] // model_width
    classes = class_bias.shape[0]
    head_count = model_width // HDIM
    total_count = count * shards * groups
    core = jnp.bitwise_and(group_index, 1)

    half_entries = half_of(entries)
    codes = tokens * CODE + positions
    slots = jnp.arange(length_slots, dtype=jnp.int32)[None]
    keys = jnp.where(slots < lengths[:, None], codes, LAST_KEY)
    keys = jnp.where(slots == 0, -1, keys)
    ahead = (keys[:, :, None] < keys[:, None, :]) | (
        (keys[:, :, None] == keys[:, None, :]) & (slots[:, :, None] < slots[:, None, :])
    )
    rank = jnp.sum(ahead.astype(jnp.int32), 1)
    codes = jnp.sum(jnp.where(rank[:, :, None] == slots[:, None, :], codes[:, :, None], 0), 1)
    early = jnp.sum(((keys >= 0) & (keys < half_entries * CODE)).astype(jnp.int32), 1)
    words = lax.shift_right_arithmetic(keys, 9)
    same = (words[:, :, None] == words[:, None, :]) & (keys[:, :, None] >= 0) & (keys[:, :, None] < LAST_KEY)
    repeats = jnp.sum(same.astype(jnp.int32), 1)
    runs = []
    for low_half in (True, False):
        there = jnp.where((keys >= 0) & (keys < LAST_KEY) & ((words < half_entries) == low_half), repeats, 0)
        top = jnp.max(there, 1)
        begin = jnp.min(jnp.where((there == top[:, None]) & (there > 0), rank, length_slots), 1)
        inside = (rank >= begin[:, None]) & (rank < (begin + top)[:, None])
        runs += [begin, top, jnp.max(jnp.where(inside, 0, there), 1)]
    facts = jnp.stack([lengths, labels, early] + runs, 1)
    message = jnp.concatenate([codes, facts, jnp.zeros((count, LANES - facts.shape[1]), jnp.int32)], 1)
    everyone = spread_to(message, ALL, shards * groups).reshape(total_count, -1)

    attention_source = jnp.swapaxes(teacher_attention, 2, 3)
    sources = [
        attention_source[0],
        teacher_feedforward[0, 0],
        teacher_feedforward[0, 1],
        (attention_source[1, 0:2], attention_source[1, 2:4]),
    ]

    side = half_weights(core, square_weights, widen_weights, narrow_weights)
    everyone, sources, side = lax.optimization_barrier((everyone, sources, side))

    all_codes = everyone[:, :length_slots].reshape(-1)
    all_words = jnp.pad(lax.shift_right_logical(all_codes, 9) - core * half_entries, (0, LANES))
    all_facts = everyone[:, length_slots:]
    all_lens = all_facts[:, 0]
    index = jnp.arange(total_count, dtype=jnp.int32)
    longer = (all_lens[None] > all_lens[:, None]) | ((all_lens[None] == all_lens[:, None]) & (index[None] < index[:, None]))
    rank = jnp.sum(longer.astype(jnp.int32), 1)
    turn, seat = rank // (shards * groups), rank % (shards * groups)
    seat = jnp.where(turn % 2 == 0, seat, shards * groups - 1 - seat)
    target = seat * count + turn
    deal = jnp.sum(jnp.where(target[None] == index[:, None], index[None], 0), 1, keepdims=True)
    info = jnp.where(jnp.arange(LANES)[None] == DEAL, deal, all_facts)
    mine = (shard_index * groups + group_index) * count + jnp.arange(count, dtype=jnp.int32)
    own = jnp.sum(jnp.where(target[None, :, None] == mine[:, None, None], all_facts[None, :, :2], 0), 1)
    lengths, labels = own[:, 0], own[:, 1]
    row_where = jnp.stack([shard_index * groups * count, jnp.full((), count, jnp.int32)])
    column_where = jnp.stack([group_index * count, jnp.full((), groups * count, jnp.int32)])
    column = column_where[0] + jnp.arange(shards)[:, None] * column_where[1] + jnp.arange(count)[None]
    all_spots = jnp.bitwise_and(everyone[:, :length_slots], CODE - 1)
    column_hits = target[None] == column.reshape(-1)[:, None]
    column_spots = jnp.sum(jnp.where(column_hits[:, :, None], all_spots[None], 0), 1).astype(F32)[:, None]

    shard_bias = [teacher_vectors[row : row + 2] for row in (2, 2 + 8 + spread_rows)]
    shard_bias = jnp.concatenate(shard_bias).reshape(4 * groups, -1)
    near = [group_swap(piece, 1, groups) for piece in sources[:3]]
    near.append([group_swap(piece, 1, groups) for piece in sources[3]])
    far = [group_swap(piece, 2, groups) for piece in sources[:2]]
    index_work = (info, all_words, column_spots, row_where, column_where, lengths, labels, shard_bias)
    index_work = lax.optimization_barrier(index_work)
    info, all_words, column_spots, row_where, column_where, lengths, labels, shard_bias = index_work
    side_own = lax.all_gather(side, "fsdp", axis=0, tiled=True)

    teacher_slices = lookup(
        all_codes, info, row_where, teacher_word, teacher_place, groups, count, length_slots
    )
    teacher_slices, far[0], column_where, sources[2] = lax.optimization_barrier(
        (teacher_slices, far[0], column_where, sources[2])
    )
    teacher_embedded = exchange(teacher_slices, "grp").reshape(groups, count, -1, length_slots)
    far.append(group_swap(sources[2], 2, groups))
    student_slices = lookup(
        all_codes, info, column_where, word_table, place_table, shards, count, length_slots
    )
    student_slices, far[1], near[:2] = lax.optimization_barrier((student_slices, far[1], near[:2]))
    embedded = exchange(student_slices, "fsdp").reshape(shards, count, own_rows, length_slots)
    group_slices = lax.all_gather(student_slices, "grp", axis=0, tiled=True)
    last = [group_swap(piece, 1, groups) for piece in far[:2]]
    last[0], sources[3] = lax.optimization_barrier((last[0], sources[3]))
    far.append([group_swap(piece, 2, groups) for piece in sources[3]])
    teacher_embedded, student_slices = lax.optimization_barrier((teacher_embedded, student_slices))
    shard_pieces = [list(pieces) for pieces in zip(sources[:2], near[:2], far[:2], last)]

    teacher_cls, teacher_logits, (embedded, side_own, side_far) = teacher_forward(
        teacher_embedded,
        shard_bias,
        shard_pieces,
        (sources[2], near[2], far[2]),
        (sources[3], near[3], far[3]),
        (embedded, side_own),
        teacher_feedforward,
        teacher_pooler,
        teacher_vectors,
        lengths,
        group_index,
    )
    message, shares = student_step(
        embedded,
        (side_own, side_far),
        small_params,
        class_bias,
        lengths,
        labels,
        core,
        teacher_cls,
        teacher_logits,
        total_count,
    )

    message = exchange(message, "fsdp")
    message, shares = lax.optimization_barrier((message, shares))
    shares = exchange(shares, "fsdp")
    far_message = group_swap(message, 2, groups)
    place_part = place_sums(info, column_where, message, student_slices, column_spots, places)
    shares, far_message, place_part = lax.optimization_barrier((shares, far_message, place_part))
    all_messages = [message, group_swap(message, 1, groups), far_message, group_swap(far_message, 1, groups)]
    shares, place_part, all_messages = lax.optimization_barrier((shares, place_part, all_messages))
    place_parts, shares = (group_direct(v, groups) for v in (place_part, shares))
    half_rows, word_squares = scatter(
        all_words, info, core, group_index, all_messages, group_slices, half_entries
    )
    shares, place_parts, half_rows, word_squares = lax.optimization_barrier(
        (shares, place_parts, half_rows, word_squares)
    )
    square_grad, widen_grad, narrow_grad, place_grad, payload = weight_grads(
        group_index, shares, place_parts, word_squares, shards, own_rows
    )
    payload, half_rows = lax.optimization_barrier((payload, half_rows))
    other_rows = group_swap(half_rows, 1, groups)
    parts = exchange(payload, "fsdp")
    factor, scalars, rest = norm_step(
        core,
        parts,
        group_swap(parts, 1, groups),
        (place_grad, square_grad, widen_grad, narrow_grad),
        (
            (place_table, place_first, place_second),
            (square_weights, square_first, square_second),
            (widen_weights, widen_first, widen_second),
            (narrow_weights, narrow_first, narrow_second),
            (small_params, small_first, small_second),
            (class_bias, class_first, class_second),
        ),
    )
    word = adam_table(factor[0, 0:1], core, half_rows, other_rows, word_table, word_first, word_second)
    results = [scalars[0, 0], scalars[0, 1], *word, *rest]
    return tuple(results)


def solution(mesh):
    rows = P("fsdp", None)
    seqs = P(("fsdp", "grp"))
    table = [rows] * 15
    placed = (
        [P(("fsdp", "grp"), None)] * 2
        + [seqs] * 2
        + table
        + [P()] * 6
        + [P("grp", None)] * 2
        + [P(None, None, None, "grp")] * 2
        + [P()] * 2
    )
    return jax.shard_map(
        on_device,
        mesh=mesh,
        in_specs=tuple(placed),
        out_specs=tuple([P(), P()] + table + [P()] * 6),
        check_vma=False,
    )
```

```python
import functools

import jax
import jax.numpy as jnp
from jax import lax
from jax.experimental import pallas as pl
from jax.experimental.pallas import tpu as pltpu
from jax.sharding import PartitionSpec as P

HDIM = 64
BF = jnp.bfloat16
F32 = jnp.float32
ALL = ("fsdp", "grp")
MIB = 2**20

highest = lax.Precision.HIGHEST
layer_eps = 1e-06
dist_eps = 1e-06
temper = 10.0
beta_one = 0.9
beta_two = 0.999
learn_rate = 0.05
decay_rate = 0.01
adam_eps = 1e-08
adam_steps = 10
clip_bound = 1.0
LANES = 128
CODE = 512
COEF = 32
LAST_KEY = 2**30
DEAL = 15


def layer_norm(values, scale_row, shift_row):
    center = values - jnp.mean(values, -1, keepdims=True)
    spread = jnp.mean(center * center, -1, keepdims=True)
    return center * lax.rsqrt(spread + layer_eps) * scale_row + shift_row


def norm_back(values, scale_row, shift_row, cotangent):
    outputs, pullback = jax.vjp(layer_norm, values, scale_row, shift_row)
    return pullback(cotangent)


def low(values):
    return lax.reduce_precision(values, exponent_bits=8, mantissa_bits=7)


def ein(spec, left, right):
    return jnp.einsum(spec, left, right, preferred_element_type=F32)


def split_two(values):
    high_part = low(values)
    return high_part.astype(BF), (values - high_part).astype(BF)


def ein_split(spec, left, right):
    high_part, low_part = split_two(left)
    return ein(spec, high_part, right) + ein(spec, low_part, right)


def ein_split_right(spec, left, right):
    high_part, low_part = split_two(right)
    return ein(spec, left, high_part) + ein(spec, left, low_part)


def half_of(entries):
    return pl.cdiv(entries, 4096) * 2048


def small_cost():
    return pl.CostEstimate(flops=0, transcendentals=0, bytes_accessed=0)


def large_cost():
    return pl.CostEstimate(flops=0, transcendentals=0, bytes_accessed=200 * MIB)


def exchange(values, axes):
    return lax.all_to_all(values, axes, split_axis=0, concat_axis=0, tiled=True)


def spread_to(values, axes, count):
    return exchange(jnp.broadcast_to(values[None], (count,) + values.shape), axes)


def group_swap(values, distance, count):
    return lax.ppermute(values, "grp", [(i, i ^ distance) for i in range(count)])


def group_direct(own, count):
    return [own] + [group_swap(own, r, count) for r in range(1, count)]


def half_kernel(core, square, widen, narrow, side):
    own_rows = square.shape[0]
    half = narrow.shape[1] // 2
    second = core[0] == 1
    for i in range(5):
        start = 2 * i * half
        pair = square[:, start : start + half], square[:, start + half : start + 2 * half]
        side[:, i * half : (i + 1) * half] = jnp.where(second, pair[1], pair[0]).astype(BF)
    middle = widen.shape[1] // 2
    side[:, 5 * half : 5 * half + middle] = jnp.where(second, widen[:, middle:], widen[:, :middle]).astype(BF)
    for j in range(narrow.shape[0] // own_rows):
        rows = slice(j * own_rows, (j + 1) * own_rows)
        start = 5 * half + middle + j * half
        side[:, start : start + half] = jnp.where(second, narrow[rows, half:], narrow[rows, :half]).astype(BF)


def half_weights(core, square, widen, narrow):
    vmem = pl.BlockSpec(memory_space=pltpu.VMEM)
    return pl.pallas_call(
        half_kernel,
        name="half_weights",
        in_specs=[pl.BlockSpec(memory_space=pltpu.SMEM)] + [vmem] * 3,
        out_specs=vmem,
        out_shape=jax.ShapeDtypeStruct((square.shape[0], (square.shape[1] + 2 * widen.shape[1]) // 2), BF),
        compiler_params=pltpu.CompilerParams(vmem_limit_bytes=16 * MIB),
        cost_estimate=small_cost(),
    )(core.reshape(1), square, widen, narrow)


def lookup_kernel(width, streams, table_steps, count, codes, info, where, *refs):
    tables, (place, out), scratch = refs[:streams], refs[streams : streams + 2], refs[streams + 2 :]
    groups = len(scratch) // 3
    rows, spots, stages = scratch[:groups], scratch[groups : 2 * groups], scratch[2 * groups :]
    step = pl.program_id(0)
    length_slots = out.shape[2]
    block = tables[0].shape[1]
    piece = block // 2

    def turned(values):
        values = values.astype(BF).astype(F32)
        return [values[g * LANES : min((g + 1) * LANES, width)].T for g in range(groups)]

    @pl.when(step == 0)
    def first():
        for spot, value in zip(spots, turned(place[...])):
            spot[:, 0 : value.shape[1]] = value

    @pl.when(step < table_steps)
    def turn():
        for stream, table in enumerate(tables):

            @pl.loop(0, block // piece)
            def part(i):
                column = pl.multiple_of(i * piece, piece)
                start = pl.multiple_of((stream * table_steps + step) * block + i * piece, piece)
                for row, value in zip(rows, turned(table[:, pl.ds(column, piece)])):
                    row[pl.ds(start, piece), 0 : value.shape[1]] = value

    @pl.when(step >= table_steps)
    def fetch():
        unroll = 16
        for b in range(count):
            seq = info[where[0] + (step - table_steps) * where[1] + b, DEAL]
            base = seq * length_slots
            live = info[seq, 0]

            def some(index, carry):
                for k in range(unroll):
                    slot = index * unroll + k
                    code = codes[base + slot]
                    word = lax.shift_right_logical(code, 9)
                    spot = jnp.bitwise_and(code, CODE - 1)
                    for stage, row, place_row in zip(stages, rows, spots):
                        stage[pl.ds(slot, 1), :] = row[pl.ds(word, 1), :] + place_row[pl.ds(spot, 1), :]
                return carry

            lax.fori_loop(0, pl.cdiv(live, unroll), some, 0)
            slots = lax.broadcasted_iota(jnp.int32, (length_slots, LANES), 0)
            for g, stage in enumerate(stages):
                start, end = g * LANES, min((g + 1) * LANES, width)
                out[b, start:end] = jnp.where(slots < live, stage[...], 0.0).T[0 : end - start].astype(BF)


def lookup(codes, info, where, table, place, steps, count, length_slots):
    width, entries = table.shape
    streams, table_steps = 4, 4
    block = pl.cdiv(entries, streams * table_steps * 4 * LANES) * 4 * LANES
    groups = pl.cdiv(width, LANES)
    last = pl.cdiv(entries, block) - 1

    def stream_spec(stream):
        def index(i, *scalars):
            return (0, jnp.minimum(stream * table_steps + jnp.minimum(i, table_steps - 1), last))

        return pl.BlockSpec((width, block), index)

    return pl.pallas_call(
        functools.partial(lookup_kernel, width, streams, table_steps, count),
        name="lookup",
        grid_spec=pltpu.PrefetchScalarGridSpec(
            num_scalar_prefetch=3,
            grid=(table_steps + steps,),
            in_specs=[stream_spec(stream) for stream in range(streams)]
            + [pl.BlockSpec(place.shape, lambda i, *scalars: (0, 0))],
            out_specs=pl.BlockSpec(
                (count, width, length_slots), lambda i, *scalars: (jnp.maximum(i - table_steps, 0), 0, 0)
            ),
            scratch_shapes=[pltpu.VMEM((streams * table_steps * block, LANES), F32)] * groups
            + [pltpu.VMEM((place.shape[1], LANES), F32)] * groups
            + [pltpu.VMEM((length_slots, LANES), F32)] * groups,
        ),
        out_shape=jax.ShapeDtypeStruct((steps * count, width, length_slots), BF),
        compiler_params=pltpu.CompilerParams(vmem_limit_bytes=58 * MIB),
        cost_estimate=small_cost(),
    )(codes, info, where, *[table] * streams, place)


def two_terms(values):
    high_part = values.astype(BF)
    return high_part, (values - high_part.astype(F32)).astype(BF)


def slot_gradients(b, message, emb, span):
    own_rows = emb.shape[1]
    both = message[0, message.shape[1] - 1, :, b * 2 * LANES : (b + 1) * 2 * LANES]
    mix = message[0, b, :, span]
    extra = mix.astype(F32)
    back = lax.dot_general(both, mix, (((0,), (0,)), ((), ())), preferred_element_type=F32)
    back = back[:LANES] + back[LANES:]
    scale = extra[13:14] + extra[14:15]
    shift = extra[28:29] + extra[29:30]
    slope = extra[30:31] + extra[31:32]
    rows = back[:own_rows] * scale + shift - emb[b, :, span].astype(F32) * slope
    if own_rows < LANES:
        rows = jnp.concatenate([rows, jnp.zeros((LANES - own_rows, rows.shape[1]), F32)], 0)
    return rows


def row_gradients(b, message, emb, stage, low, high, begin, finish):
    length_slots = emb.shape[2]
    rows = slot_gradients(b, message, emb, slice(0, length_slots))
    slots = lax.broadcasted_iota(jnp.int32, (1, length_slots), 1)
    keep = (slots < high) & ((slots >= low) | (slots == 0))
    rows = jnp.where(keep, rows, 0.0).T
    slots = lax.broadcasted_iota(jnp.int32, rows.shape, 0)
    inside = (slots >= begin) & (slots < finish)
    stage[0:length_slots, :] = jnp.where(inside, 0.0, rows)
    return jnp.sum(jnp.sum(jnp.where(inside, rows, 0.0).reshape(length_slots // 8, 8, LANES), 0), 0, keepdims=True)


def scatter_kernel(half_entries, groups, codes, info, core, *refs):
    pieces, (emb, out, squares, acc, stages, messages, sem) = refs[:groups], refs[groups:]
    step = pl.program_id(0)
    count, own_rows, length_slots = emb.shape
    clear = 512
    batch = 8

    @pl.when(step == 0)
    def first():
        stages[...] = jnp.zeros_like(stages)
        for distance, piece in enumerate(pieces):
            messages[jnp.bitwise_xor(core[1], distance)] = piece[...]

        @pl.loop(0, half_entries // clear)
        def wipe(i):
            acc[pl.ds(pl.multiple_of(i * clear, clear), clear), :] = jnp.zeros((clear, LANES), F32)

    shards = pl.num_programs(0) // groups
    group, shard = step // shards, step % shards
    def add_many(stage, base, slots, last_word=None):
        words = [codes[base + slot] for slot in slots]
        if last_word is None:
            sums = [acc[pl.ds(w, 1), :] + stage[pl.ds(s, 1), :] for w, s in zip(words, slots)]
            for w, total in zip(words, sums):
                acc[pl.ds(w, 1), :] = total
        else:
            for w, s in zip(words, slots):
                w = jnp.clip(w, 0, last_word)
                acc[pl.ds(w, 1), :] += stage[pl.ds(s, 1), :]

    plans = []
    for b in range(count):
        seq = info[(shard * groups + group) * count + b, DEAL]
        base = seq * length_slots
        middle = 1 + info[seq, 2]
        start = jnp.where(core[0] == 0, 1, middle)
        end = jnp.where(core[0] == 0, middle, info[seq, 0])
        begin = info[seq, 3 + 3 * core[0]]
        finish = begin + info[seq, 4 + 3 * core[0]]
        most = info[seq, 5 + 3 * core[0]]
        total = row_gradients(b, messages.at[group, pl.ds(shard, 1)], emb, stages.at[b], start, end, begin, finish)
        plans.append((base, start, end, begin, finish, most, total))

    for b, (base, start, end, begin, finish, most, total) in enumerate(plans):
        stage = stages.at[b]
        word = codes[base]

        @pl.when(finish > begin)
        def run():
            acc[pl.ds(codes[base + begin], 1), :] += total

        @pl.when((word >= 0) & (word < half_entries))
        def first_slot():
            add_many(stage, base, [0])

        stride = (end - start) // batch

        @pl.when(most <= stride)
        def apart():
            def some(index, carry):
                for u in range(4):
                    add_many(stage, base, [start + 4 * index + u + k * stride for k in range(batch)])
                return carry

            def rest(index, carry):
                add_many(stage, base, [start + index + k * stride for k in range(batch)])
                return carry

            lax.fori_loop(0, stride // 4, some, 0)
            lax.fori_loop(stride // 4 * 4, stride, rest, 0)

        @pl.when(most > stride)
        def repeated():
            def some(index, carry):
                for k in range(batch):
                    slot = start + index * batch + k
                    acc[pl.ds(codes[base + slot], 1), :] += stage[pl.ds(slot, 1), :]
                return carry

            lax.fori_loop(0, stride, some, 0)

        add_many(stage, base, [start + stride * batch + k for k in range(batch)], half_entries - 1)

    @pl.when(step == pl.num_programs(0) - 1)
    def last():
        copy = pltpu.make_async_copy(acc, out, sem)
        copy.start()

        def add(i, total):
            part = acc[pl.ds(pl.multiple_of(i * clear, clear), clear), :]
            return total + jnp.sum((part * part).reshape(clear // 8, 8, LANES), 0)

        squares[...] = lax.fori_loop(0, half_entries // clear, add, jnp.zeros((8, LANES), F32))
        copy.wait()


def place_kernel(info, where, message, emb, spots, out):
    step = pl.program_id(0)
    count, own_rows, length_slots = emb.shape
    places = out.shape[1]

    @pl.when(step == 0)
    def first():
        out[...] = jnp.zeros_like(out)

    for b in range(count):
        live = info[info[where[0] + step * where[1] + b, DEAL], 0]

        rows = slot_gradients(b, message, emb, slice(0, length_slots))
        rows = jnp.where(lax.broadcasted_iota(jnp.int32, (1, length_slots), 1) < live, rows, 0.0)
        index = lax.broadcasted_iota(jnp.int32, (places, length_slots), 0).astype(F32)
        hit = (index == spots[b, 0:1, :]).astype(F32).astype(BF)
        high_part, low_part = two_terms(rows)
        sums = mm_t(jnp.concatenate([high_part, low_part], 0), hit)
        out[...] += sums[:LANES] + sums[LANES:]


def row_specs(message, emb, count):
    return [
        pl.BlockSpec((1,) + message.shape[1:], lambda i, *scalars: (i, 0, 0, 0)),
        pl.BlockSpec((count,) + emb.shape[1:], lambda i, *scalars: (i, 0, 0)),
    ]


def scatter(codes, info, core, group_index, pieces, emb, half_entries):
    groups = len(pieces)
    shards, count = pieces[0].shape[0], pieces[0].shape[1] - 1
    length_slots = emb.shape[2]
    whole = pl.BlockSpec(pieces[0].shape, lambda i, *scalars: (0, 0, 0, 0), pipeline_mode=pl.Buffered(1))
    return pl.pallas_call(
        functools.partial(scatter_kernel, half_entries, groups),
        name="scatter_rows",
        grid_spec=pltpu.PrefetchScalarGridSpec(
            num_scalar_prefetch=3,
            grid=(groups * shards,),
            in_specs=[whole] * groups + [pl.BlockSpec((count,) + emb.shape[1:], lambda i, *scalars: (i, 0, 0))],
            out_specs=[
                pl.BlockSpec(memory_space=pl.ANY),
                pl.BlockSpec((8, LANES), lambda i, *scalars: (0, 0)),
            ],
            scratch_shapes=[
                pltpu.VMEM((half_entries, LANES), F32),
                pltpu.VMEM((count, length_slots + LANES, LANES), F32),
                pltpu.VMEM((groups,) + pieces[0].shape, BF),
                pltpu.SemaphoreType.DMA,
            ],
        ),
        out_shape=[
            jax.ShapeDtypeStruct((half_entries, LANES), F32),
            jax.ShapeDtypeStruct((8, LANES), F32),
        ],
        compiler_params=pltpu.CompilerParams(vmem_limit_bytes=48 * MIB),
        cost_estimate=large_cost(),
    )(codes, info, jnp.stack([core, group_index]), *pieces, emb)


def place_sums(info, where, message, emb, spots, places):
    count = message.shape[1] - 1
    return pl.pallas_call(
        place_kernel,
        name="place_rows",
        grid_spec=pltpu.PrefetchScalarGridSpec(
            num_scalar_prefetch=2,
            grid=(message.shape[0],),
            in_specs=row_specs(message, emb, count)
            + [pl.BlockSpec((count,) + spots.shape[1:], lambda i, *scalars: (i, 0, 0))],
            out_specs=pl.BlockSpec((LANES, places), lambda i, *scalars: (0, 0)),
        ),
        out_shape=jax.ShapeDtypeStruct((LANES, places), F32),
        compiler_params=pltpu.CompilerParams(vmem_limit_bytes=16 * MIB),
        cost_estimate=large_cost(),
    )(info, where, message, emb, spots)


def adam_kernel(width, half_steps, factor, core, own, other, weight, first, second, new_weight, new_first, new_second):
    mine = (pl.program_id(0) // half_steps) == core[0]
    rows = jnp.where(mine, own[...], other[...]).T[0:width]
    out = adam_update(weight[...], first[...], second[...], rows, factor[0])
    new_weight[...], new_first[...], new_second[...] = out


def adam_table(factor, core, own, other, weight, first, second):
    width, entries = weight.shape
    block = 4096
    half_steps = own.shape[0] // block
    spec = pl.BlockSpec((width, block), lambda i, f, c: (0, i))

    def half_spec(flip):
        def index(i, f, c):
            start = jnp.bitwise_xor(c[0], flip) * half_steps
            return (jnp.clip(i - start, 0, half_steps - 1), 0)

        return pl.BlockSpec((block, LANES), index)

    return pl.pallas_call(
        functools.partial(adam_kernel, width, half_steps),
        name="adam_table",
        grid_spec=pltpu.PrefetchScalarGridSpec(
            num_scalar_prefetch=2,
            grid=(pl.cdiv(entries, block),),
            in_specs=[half_spec(0), half_spec(1), spec, spec, spec],
            out_specs=[spec, spec, spec],
        ),
        out_shape=[jax.ShapeDtypeStruct(weight.shape, F32)] * 3,
        compiler_params=pltpu.CompilerParams(vmem_limit_bytes=56 * MIB),
        cost_estimate=small_cost(),
    )(factor.reshape(1), core.reshape(1), own, other, weight, first, second)


def attention_kernel(lens, me, embedded, shard_bias, vectors, *rest):
    groups, _, width, length_slots = embedded.shape
    weights, (hidden_out, rows, rows_low, heads, context) = rest[:groups], rest[groups:]
    live = lens[pl.program_id(0)]
    big, small = 256, 128

    def over_blocks(block, work, blank):
        @pl.loop(0, length_slots // block)
        def one(index):
            span = pl.ds(pl.multiple_of(index * block, block), block)
            pl.when(index * block < live)(lambda: work(span))
            pl.when(index * block >= live)(lambda: blank(span))

    def norm_in(span):
        values = jnp.concatenate([embedded[g, 0, :, span].astype(F32) for g in range(groups)], 0).T
        state = normalise(values)[0] * vectors[0:1, :] + vectors[1:2, :]
        rows[span, :] = state
        rows_low[span, :] = state.astype(BF)

    def no_rows(span):
        rows[span, :] = jnp.zeros((small, groups * width), F32)
        rows_low[span, :] = jnp.zeros((small, groups * width), BF)

    over_blocks(small, norm_in, no_rows)

    def project(shard, span):
        weight, values = weights[shard], rows_low[span, :]
        place = jnp.bitwise_xor(me[0], shard)
        query = (mm_t(values, weight[0]) + shard_bias[pl.ds(place, 1), :]).astype(BF)
        heads[shard % 2, 0, span, :] = query * jnp.asarray(HDIM ** (-0.5), BF)
        heads[shard % 2, 1, span, :] = mm_t(values, weight[1]).astype(BF)
        heads[shard % 2, 2, span, :] = (mm_t(values, weight[2]) + shard_bias[pl.ds(groups + place, 1), :]).astype(BF)

    def no_heads(span):
        for i in range(6):
            heads[i // 3, i % 3, span, :] = jnp.zeros((big, width), BF)

    over_blocks(big, functools.partial(project, 0), no_heads)

    def attend(shard, reach, span):
        mask = jnp.where(lax.broadcasted_iota(jnp.int32, (1, reach), 1) < live, 0.0, -1e30)
        pieces = []
        for head in range(width // HDIM):
            part = slice(head * HDIM, (head + 1) * HDIM)
            scores = mm_t(heads[shard % 2, 0, span, part], heads[shard % 2, 1, 0:reach, part]) + mask
            shifted = jnp.exp(scores - jnp.max(scores, -1, keepdims=True))
            prob = shifted * (1.0 / jnp.sum(shifted, -1, keepdims=True))
            pieces.append(mm(prob.astype(BF), heads[shard % 2, 2, 0:reach, part]))
        context[shard, span, :] = jnp.concatenate(pieces, 1).astype(BF)
        if shard + 1 < groups:
            project(shard + 1, span)

    for shard in range(groups):

        @pl.when(live <= big)
        def short():
            attend(shard, big, pl.ds(0, big))

        @pl.when(live > big)
        def long():
            @pl.loop(0, length_slots // big)
            def one(index):
                span = pl.ds(pl.multiple_of(index * big, big), big)
                pl.when(index * big < live)(lambda: attend(shard, length_slots, span))

    def join(span):
        joined = rows[span, :] + vectors[4:5, :]
        for shard in range(groups):
            joined = joined + mm(context[shard, span, :], weights[shard][3])
        hidden_out[0, span, :] = normalise(joined)[0] * vectors[5:6, :] + vectors[6:7, :]

    def no_hidden(span):
        hidden_out[0, span, :] = jnp.zeros((big, groups * width), F32)

    over_blocks(big, join, no_hidden)


def feed_kernel(spread_rows, block, lens, me, hidden, vectors, *rest):
    groups = (len(rest) - 2) // 2
    wides, narrows, (state_low, first) = rest[:groups], rest[groups : 2 * groups], rest[2 * groups :]
    _, length_slots, model_width = hidden.shape
    live = lens[pl.program_id(0)]
    tail = 2 + 5 + spread_rows

    @pl.loop(0, length_slots // block)
    def one(index):
        span = pl.ds(pl.multiple_of(index * block, block), block)

        @pl.when(index * block < live)
        def work():
            rows = hidden[0, span, :]
            rows_low = rows.astype(BF)
            summed = rows + vectors[tail : tail + 1, :]
            for shard in range(groups):
                before = mm(rows_low, wides[shard][...]) + vectors[pl.ds(7 + jnp.bitwise_xor(me[0], shard), 1), :]
                active = (before * phi(before)).astype(BF)
                summed = summed + mm_t(active, narrows[shard][...])
            state = normalise(summed)[0] * vectors[tail + 1 : tail + 2, :] + vectors[tail + 2 : tail + 3, :]
            state_low[0, span, :] = state.astype(BF)

            @pl.when(index == 0)
            def keep():
                first[0] = state[0:8, :]

        @pl.when(index * block >= live)
        def blank():
            state_low[0, span, :] = jnp.zeros((block, model_width), BF)


def cls_kernel(spread_rows, lens, me, state_low, first, shard_bias, vectors, *rest):
    groups = (len(rest) - 1) // 2
    hidden_out = rest[-1]
    weights = [[rest[2 * i + j // 2].at[j % 2] for j in range(4)] for i in range(groups)]
    count, length_slots, model_width = state_low.shape
    width = model_width // groups
    shard_heads = width // HDIM
    base = 2 + 8 + spread_rows
    head_rows = 8
    head_mask = (
        lax.broadcasted_iota(jnp.int32, (head_rows, width), 0)
        == lax.broadcasted_iota(jnp.int32, (head_rows, width), 1) // HDIM
    ).astype(F32)
    starts = jnp.concatenate([first[b, 0:1, :] for b in range(count)], 0)
    starts_low = starts.astype(BF)
    tops = []
    places = [jnp.bitwise_xor(me[0], shard) for shard in range(groups)]
    for shard in range(groups):
        query = mm_t(starts_low, weights[shard][0][...]) + shard_bias[pl.ds(2 * groups + places[shard], 1), :]
        query = query.astype(BF).astype(F32)
        spread = jnp.concatenate(
            [jnp.broadcast_to(query[b : b + 1], head_mask.shape) * head_mask for b in range(count)], 0
        )
        tops.append(mm(spread.astype(BF), weights[shard][1][...]))
    bars, masses = [], []
    all_rows = groups * head_rows
    slot_index = lax.broadcasted_iota(jnp.int32, (all_rows, length_slots), 1)
    for b in range(count):
        own = jnp.concatenate([top[b * head_rows : (b + 1) * head_rows] for top in tops], 0)
        high_part, low_part = two_terms(own)
        scores = mm_t(jnp.concatenate([high_part, low_part], 0), state_low[b])
        scores = (scores[:all_rows] + scores[all_rows:]) * HDIM ** (-0.5)
        scores = jnp.where(slot_index < lens[b], scores, -1e30)
        shifted = jnp.exp(scores - jnp.max(scores, -1, keepdims=True))
        prob_low = (shifted / jnp.sum(shifted, -1, keepdims=True)).astype(BF)
        bars.append(mm(prob_low, state_low[b]))
        masses.append(jnp.sum(prob_low.astype(F32), -1, keepdims=True))
    joined = starts + vectors[base + 2 : base + 3, :]
    for shard in range(groups):
        part = slice(shard * head_rows, (shard + 1) * head_rows)
        own = jnp.concatenate([bar[part] for bar in bars], 0)
        mass = jnp.concatenate([mass[part] for mass in masses], 0)
        high_part, low_part = two_terms(own)
        full = mm_t(jnp.concatenate([high_part, low_part], 0), weights[shard][2][...])
        full = full[: count * head_rows] + full[count * head_rows :] + mass * shard_bias[pl.ds(3 * groups + places[shard], 1), :]
        context = jnp.concatenate(
            [
                jnp.sum(full[b * head_rows : (b + 1) * head_rows] * head_mask, 0, keepdims=True)
                for b in range(count)
            ],
            0,
        )
        joined = joined + mm(context.astype(BF), weights[shard][3][...])
    hidden_out[...] = normalise(joined)[0] * vectors[base + 3 : base + 4, :] + vectors[base + 4 : base + 5, :]


def teacher_forward(embedded, shard_bias, shard_pieces, narrow_pieces, cls_pieces, student_parts, feedforward, pooler, vectors, lens, group_index):
    groups, count, width, length_slots = embedded.shape
    model_width = groups * width
    first_attention, wides = shard_pieces
    student_embedded, side_own = student_parts
    local_units = feedforward.shape[-1]
    spread_rows = local_units * groups // model_width
    block_rows = 8 + spread_rows
    one, two = vectors[2 : 2 + block_rows], vectors[2 + block_rows : 2 + 2 * block_rows]
    assert local_units == model_width
    me = group_index.reshape(1)

    def whole(values):
        return pl.BlockSpec(values.shape, lambda i, *scalars: (0,) * values.ndim, pipeline_mode=pl.Buffered(1))

    each = pl.BlockSpec((1, length_slots, model_width), lambda i, *scalars: (i, 0, 0))
    hidden = pl.pallas_call(
        attention_kernel,
        name="teacher_attention",
        grid_spec=pltpu.PrefetchScalarGridSpec(
            num_scalar_prefetch=2,
            grid=(count,),
            in_specs=[
                pl.BlockSpec((groups, 1, width, length_slots), lambda i, *scalars: (0, i, 0, 0)),
                whole(shard_bias),
                whole(vectors),
            ]
            + [whole(piece) for piece in first_attention],
            out_specs=each,
            scratch_shapes=[
                pltpu.VMEM((length_slots, model_width), F32),
                pltpu.VMEM((length_slots, model_width), BF),
                pltpu.VMEM((2, 3, length_slots, width), BF),
                pltpu.VMEM((groups, length_slots, width), BF),
            ],
        ),
        out_shape=jax.ShapeDtypeStruct((count, length_slots, model_width), F32),
        compiler_params=pltpu.CompilerParams(vmem_limit_bytes=40 * MIB),
        cost_estimate=small_cost(),
    )(lens, me, embedded, shard_bias, vectors, *first_attention)
    own, near, far = narrow_pieces
    cls_own, cls_near, cls_far = cls_pieces
    hidden, near, far = lax.optimization_barrier((hidden, near, far))
    narrows = [own, near, far, group_swap(far, 1, groups)]
    state_low, first = pl.pallas_call(
        functools.partial(feed_kernel, spread_rows, 256),
        name="teacher_feed",
        grid_spec=pltpu.PrefetchScalarGridSpec(
            num_scalar_prefetch=2,
            grid=(count,),
            in_specs=[each, whole(vectors)] + [whole(piece) for piece in wides + narrows],
            out_specs=[each, pl.BlockSpec((1, 8, model_width), lambda i, *scalars: (i, 0, 0))],
        ),
        out_shape=[
            jax.ShapeDtypeStruct((count, length_slots, model_width), BF),
            jax.ShapeDtypeStruct((count, 8, model_width), F32),
        ],
        compiler_params=pltpu.CompilerParams(vmem_limit_bytes=50 * MIB),
        cost_estimate=small_cost(),
    )(lens, me, hidden, vectors, *wides, *narrows)
    state_low, cls_near, cls_far, student_embedded = lax.optimization_barrier(
        (state_low, cls_near, cls_far, student_embedded)
    )
    cls_last, side_own = lax.optimization_barrier(([group_swap(part, 1, groups) for part in cls_far], side_own))
    second_attention = [*cls_own, *cls_near, *cls_far, *cls_last]
    side_far = group_swap(side_own, 1, groups)
    hidden = pl.pallas_call(
        functools.partial(cls_kernel, spread_rows),
        name="teacher_cls",
        grid_spec=pltpu.PrefetchScalarGridSpec(
            num_scalar_prefetch=2,
            grid=(1,),
            in_specs=[whole(array) for array in (state_low, first, shard_bias, vectors, *second_attention)],
            out_specs=pl.BlockSpec((count, model_width), lambda i, *scalars: (0, 0)),
        ),
        out_shape=jax.ShapeDtypeStruct((count, model_width), F32),
        compiler_params=pltpu.CompilerParams(vmem_limit_bytes=58 * MIB),
        cost_estimate=small_cost(),
    )(lens, me, state_low, first, shard_bias, vectors, *second_attention)
    everyone = spread_to(hidden.astype(BF), "grp", groups).reshape(-1, model_width)
    unit_bias = lax.dynamic_slice_in_dim(two[5 : 5 + spread_rows].reshape(-1), group_index * local_units, local_units)
    before = ein("sd,df->sf", everyone, feedforward[1, 0]) + unit_bias
    active = jax.nn.gelu(before, approximate=False).astype(BF)
    partial_rows = ein("sf,df->sd", active, feedforward[1, 1]).reshape(groups, count, model_width)
    total = jnp.sum(exchange(partial_rows, "grp"), 0)
    summed = hidden + total + two[5 + spread_rows]
    cls = layer_norm(summed, two[6 + spread_rows], two[7 + spread_rows])
    pool = jnp.tanh(ein("sd,de->se", cls.astype(BF), pooler) + vectors[2 + 2 * block_rows])
    logits = ein("sd,cd->sc", pool.astype(BF), vectors[3 + 2 * block_rows :].astype(BF))
    return cls, logits, (student_embedded, side_own, side_far)


NT = (((1,), (1,)), ((), ()))
HEAD_ROWS = 16
MISC_ROWS = 8
SEQ_ROWS = MISC_ROWS + 2 * HEAD_ROWS
SMALL_ROWS = 24


def mm(left, right):
    return jnp.dot(left, right, preferred_element_type=F32)


def mm_t(left, right):
    return lax.dot_general(left, right, NT, preferred_element_type=F32)


def row_mean(values):
    return jnp.mean(values, -1, keepdims=True)


def normalise(values):
    center = values - row_mean(values)
    rstd = lax.rsqrt(row_mean(center * center) + layer_eps)
    return center * rstd, rstd


def normal_back(normal, rstd, cotangent):
    return rstd * (cotangent - row_mean(cotangent) - normal * row_mean(cotangent * normal))


def phi(values):
    return 0.5 * (1.0 + lax.erf(values * 0.5**0.5))


def log_soft(values, live):
    shifted = jnp.where(live, values, -1e30)
    shifted = shifted - jnp.max(shifted, -1, keepdims=True)
    return shifted - jnp.log(jnp.sum(jnp.where(live, jnp.exp(shifted), 0.0), -1, keepdims=True))


def student_kernel(
    total_count,
    classes,
    lens,
    labels,
    swapped,
    emb,
    side_own,
    side_far,
    small,
    bias,
    teacher_cls,
    teacher_logits,
    message,
    shares,
    rows_in,
    rows_low,
    normal_low,
    stats,
):
    shards, count, own_rows, length_slots = emb.shape
    model_width = shards * own_rows
    half = model_width // 2
    spread_rows = (side_own.shape[1] // half - 5) // 2
    unit_half = spread_rows * half
    far = swapped[0] == 1
    scale = HDIM ** (-0.5)
    block = 128

    def small_row(index, rows=1):
        return small[index : index + rows, :]

    def weight(index):
        span = slice(index * half, (index + 1) * half)
        return side_own[:, span], side_far[:, span]

    def units():
        span = slice(5 * half, 5 * half + unit_half)
        return side_own[:, span], side_far[:, span]

    def narrow(index):
        return weight(5 + spread_rows + index)

    def narrow_parts(values):
        return [
            jnp.concatenate(
                [
                    values[:, (f * spread_rows + j) * own_rows : (f * spread_rows + j + 1) * own_rows]
                    for f in range(shards)
                ],
                1,
            )
            for j in range(spread_rows)
        ]

    def in_units(parts):
        return jnp.concatenate(
            [part[:, f * own_rows : (f + 1) * own_rows] for f in range(shards) for part in parts], 1
        )

    def forward(values, pair):
        one, two = mm(values, pair[0]), mm(values, pair[1])
        return jnp.where(far, jnp.concatenate([two, one], 1), jnp.concatenate([one, two], 1))

    def backward(values, pair):
        middle = values.shape[1] // 2
        low_part, high_part = values[:, :middle].astype(F32), values[:, middle:].astype(F32)
        one = jnp.where(far, high_part, low_part).astype(BF)
        two = jnp.where(far, low_part, high_part).astype(BF)
        return mm_t(one, pair[0]) + mm_t(two, pair[1])

    def both(values):
        return jnp.concatenate(two_terms(values), 0)

    def fold(values):
        middle = values.shape[0] // 2
        return values[:middle] + values[middle:]

    head_mask = (
        lax.broadcasted_iota(jnp.int32, (HEAD_ROWS, model_width), 0)
        == lax.broadcasted_iota(jnp.int32, (HEAD_ROWS, model_width), 1) // HDIM
    ).astype(F32)
    heads = model_width // HDIM

    def by_head(values):
        return jnp.concatenate(
            [jnp.broadcast_to(values[b : b + 1], head_mask.shape) * head_mask for b in range(count)], 0
        )

    def from_head(values):
        return jnp.concatenate(
            [
                jnp.sum(values[b * HEAD_ROWS : (b + 1) * HEAD_ROWS] * head_mask, 0, keepdims=True)
                for b in range(count)
            ],
            0,
        )

    def head_rows(values, b):
        return values[b * HEAD_ROWS : (b + 1) * HEAD_ROWS]

    firsts = []
    for b in range(count):

        def norm_rows(index, carry):
            start = pl.multiple_of(index * block, block)
            span = pl.ds(start, block)
            values = jnp.concatenate([emb[f, b, :, span].astype(F32) for f in range(shards)], 0).T
            mean = row_mean(values)
            center = values - mean
            rstd = lax.rsqrt(row_mean(center * center) + layer_eps)
            normal = center * rstd
            rows_in[b, span, :] = values.astype(BF)
            normal_low[b, span, :] = normal.astype(BF)
            rows_low[b, span, :] = (normal * small_row(0) + small_row(1)).astype(BF)
            stats[b, 0:8, span] = jnp.broadcast_to(mean, (block, LANES)).T[0:8]
            stats[b, 8:16, span] = jnp.broadcast_to(rstd, (block, LANES)).T[0:8]
            return carry

        def no_rows(index, carry):
            span = pl.ds(pl.multiple_of(index * block, block), block)
            for rows in (rows_in, normal_low, rows_low):
                rows[b, span, :] = jnp.zeros((block, model_width), BF)
            stats[b, :, span] = jnp.zeros((16, block), F32)
            return carry

        used = pl.cdiv(lens[b], block)
        lax.fori_loop(0, used, norm_rows, 0)
        lax.fori_loop(used, length_slots // block, no_rows, 0)
        start_row = rows_in[b, 0:16, :].astype(F32)
        firsts.append((normalise(start_row)[0] * small_row(0) + small_row(1))[0:1])
    first = jnp.concatenate(firsts, 0)
    first_low = first.astype(BF)

    query = (forward(first_low, weight(0)) + small_row(2)).astype(BF)
    key_tops = backward(by_head(query.astype(F32)).astype(BF), weight(1))
    row_index = lax.broadcasted_iota(jnp.int32, (HEAD_ROWS, length_slots), 0)
    slot_index = lax.broadcasted_iota(jnp.int32, (HEAD_ROWS, length_slots), 1)
    probs, bars, masses = [], [], []
    for b in range(count):
        scores = fold(mm_t(both(head_rows(key_tops, b)), rows_low[b])) * scale
        scores = jnp.where(slot_index < lens[b], scores, -1e30)
        shifted = jnp.exp(scores - jnp.max(scores, -1, keepdims=True))
        prob = shifted / jnp.sum(shifted, -1, keepdims=True)
        prob = jnp.where(row_index < heads, prob, 0.0)
        prob_low = prob.astype(BF)
        probs.append(prob)
        bars.append(mm(prob_low, rows_low[b]))
        masses.append(jnp.sum(prob_low.astype(F32), -1, keepdims=True))
    bars = jnp.concatenate(bars, 0)
    masses = jnp.concatenate(masses, 0)
    context = from_head(fold(forward(both(bars), weight(2))) + masses * small_row(3))
    context_low = context.astype(BF)
    joined = first + forward(context_low, weight(3)) + small_row(4)
    normal_one, rstd_one = normalise(joined)
    hidden = normal_one * small_row(5) + small_row(6)
    hidden_low = hidden.astype(BF)
    unit_bias = jnp.concatenate([small_row(7 + i) for i in range(spread_rows)], 1)
    before = forward(hidden_low, units()) + unit_bias
    gate = phi(before)
    active = (before * gate).astype(BF)
    s = 7 + spread_rows
    active_parts = [part.astype(BF) for part in narrow_parts(active.astype(F32))]
    summed = hidden + small_row(s)
    for j in range(spread_rows):
        summed = summed + forward(active_parts[j], narrow(j))
    normal_two, rstd_two = normalise(summed)
    vector = normal_two * small_row(s + 1) + small_row(s + 2)
    vector_low = vector.astype(BF)
    pooled = jnp.tanh(forward(vector_low, weight(4)) + small_row(s + 3))
    pooled_low = pooled.astype(BF)
    class_rows = jnp.concatenate(
        [small_row(s + 4, classes), jnp.zeros((LANES - classes, model_width), F32)], 0
    ).astype(BF)
    lane = lax.broadcasted_iota(jnp.int32, (count, LANES), 1)
    live = lane < classes
    logits = mm_t(pooled_low, class_rows) + bias[...]

    label = jnp.concatenate([jnp.full((1, LANES), labels[b], jnp.int32) for b in range(count)], 0)
    hit = (lane == label).astype(F32)
    log_prob = log_soft(logits, live)
    teacher_soft = log_soft(teacher_logits[...] / temper, live)
    student_soft = log_soft(logits / temper, live)
    teacher_prob = jnp.where(live, jnp.exp(teacher_soft), 0.0)
    loss = jnp.sum(jnp.where(hit > 0, -log_prob, 0.0), -1, keepdims=True)
    gap = jnp.where(live, teacher_soft - student_soft, 0.0)
    loss = loss + temper * temper * jnp.sum(teacher_prob * gap, -1, keepdims=True)
    inverse = lax.rsqrt(jnp.sum(vector * vector, -1, keepdims=True) + dist_eps)
    student_unit = vector * inverse
    teacher_rows = teacher_cls[...]
    teacher_unit = teacher_rows * lax.rsqrt(jnp.sum(teacher_rows * teacher_rows, -1, keepdims=True) + dist_eps)
    apart = student_unit - teacher_unit
    loss = loss + 100.0 * jnp.sum(apart * apart, -1, keepdims=True)
    d_logits = jnp.where(live, jnp.exp(log_prob), 0.0) - hit
    soft_mass = jnp.sum(teacher_prob, -1, keepdims=True)
    d_logits = d_logits + temper * (jnp.where(live, jnp.exp(student_soft), 0.0) * soft_mass - teacher_prob)
    d_logits = d_logits / total_count
    d_unit = 200.0 / total_count * apart
    d_vector = inverse * (d_unit - student_unit * jnp.sum(student_unit * d_unit, -1, keepdims=True))

    pooled_wide = pooled_low.astype(F32)
    class_wide = class_rows.astype(F32)
    d_pooled = jnp.zeros((count, model_width), F32)
    class_grads = []
    for c in range(classes):
        part = d_logits[:, c : c + 1]
        d_pooled = d_pooled + part * class_wide[c : c + 1]
        class_grads.append(jnp.sum(part * pooled_wide, 0, keepdims=True))
    d_pool = d_pooled * (1.0 - pooled * pooled)
    pool_high, pool_rest = two_terms(d_pool)
    pool_mid, pool_last = two_terms(d_pool - pool_high.astype(F32))
    pool_back = backward(jnp.concatenate([pool_high, pool_mid, pool_last], 0), weight(4))
    d_vector = d_vector + pool_back[:count] + pool_back[count : 2 * count] + pool_back[2 * count :]
    d_summed = normal_back(normal_two, rstd_two, d_vector * small_row(s + 1))
    d_output = d_summed.astype(BF)
    d_active = in_units([backward(d_output, narrow(j)) for j in range(spread_rows)])
    slope_gate = gate + before * jnp.exp(-0.5 * before * before) * (2.0 * 3.141592653589793) ** -0.5
    d_before = (slope_gate * d_active).astype(BF)
    d_hidden = d_summed + backward(d_before, units())
    d_joined = normal_back(normal_one, rstd_one, d_hidden * small_row(5))
    d_branch = d_joined.astype(BF)
    d_context = backward(d_branch, weight(3)).astype(BF)
    context_heads = by_head(d_context.astype(F32))
    val_tops = backward(context_heads.astype(BF), weight(2))
    constant = jnp.sum(context_heads * small_row(3), -1, keepdims=True)
    d_scores, d_bars = [], []
    for b in range(count):
        d_prob = fold(mm_t(both(head_rows(val_tops, b)), rows_low[b])) + head_rows(constant, b)
        prob = probs[b]
        d_score = (prob * (d_prob - jnp.sum(prob * d_prob, -1, keepdims=True))).astype(BF)
        d_scores.append(d_score)
        d_bars.append(mm(d_score, rows_low[b]))
    d_bars = jnp.concatenate(d_bars, 0)
    d_query = (from_head(fold(forward(both(d_bars), weight(1)))) * scale).astype(BF)
    d_first = d_joined + backward(d_query, weight(0))

    d_gain = jnp.zeros((1, model_width), F32)
    d_shift = jnp.zeros((1, model_width), F32)
    top_row = lax.broadcasted_iota(jnp.int32, (HEAD_ROWS, model_width), 0)
    for b in range(count):
        tops = jnp.concatenate(
            [
                jnp.where(top_row == 12, d_first[b : b + 1], head_rows(val_tops, b)),
                head_rows(key_tops, b) * scale,
            ],
            0,
        )
        start_slot = jnp.where(slot_index == 0, 1.0, 0.0)
        value_side = jnp.where(row_index == 12, start_slot, probs[b].astype(BF).astype(F32))
        score_side = d_scores[b].astype(F32)
        coef = jnp.concatenate([value_side, score_side], 0)
        d_shift = d_shift + jnp.sum(jnp.sum(coef, -1, keepdims=True) * tops, 0, keepdims=True)
        d_gain = d_gain + jnp.sum(mm(coef.astype(BF), normal_low[b]) * tops, 0, keepdims=True)
        scaled = tops * small_row(0)
        scaled_sum = jnp.sum(scaled, -1, keepdims=True)
        along = fold(mm_t(both(scaled), rows_in[b]))
        mean, rstd = stats[b, 0:1, :], stats[b, 8:9, :]
        live_slot = slot_index[0:1] < lens[b]
        slope = rstd * rstd * rstd * (1.0 / model_width) * jnp.sum(coef * (along - mean * scaled_sum), 0, keepdims=True)
        shift = mean * slope - rstd * (1.0 / model_width) * jnp.sum(coef * scaled_sum, 0, keepdims=True)

        def insert(values, first_row, extra):
            for term in two_terms(jnp.where(live_slot, extra, 0.0)):
                values = jnp.where(row_index == first_row, term.astype(F32), values)
                first_row += 1
            return values

        value_side = insert(value_side, 13, rstd)
        score_side = insert(insert(score_side, 12, shift), 14, slope)
        packed = jnp.concatenate([value_side, score_side], 0).astype(BF)
        top_terms = two_terms(scaled)
        for f in range(shards):
            message[f, b] = packed
            for i, term in enumerate(top_terms):
                start = (2 * b + i) * LANES
                part = term[:, f * own_rows : (f + 1) * own_rows].astype(F32)
                part = jnp.concatenate([part, jnp.zeros((COEF, LANES - own_rows), F32)], 1)
                message[f, count, :, start : start + LANES] = part.astype(BF)

    def sum_rows(values):
        return jnp.sum(values.astype(F32), 0, keepdims=True)

    small_grads = jnp.concatenate(
        [
            d_gain,
            d_shift,
            sum_rows(d_query),
            sum_rows(context_heads * masses),
            sum_rows(d_branch),
            sum_rows(d_hidden * normal_one),
            sum_rows(d_hidden),
        ]
        + [sum_rows(d_before[:, i * model_width : (i + 1) * model_width]) for i in range(spread_rows)]
        + [sum_rows(d_output), sum_rows(d_vector * normal_two), sum_rows(d_vector), sum_rows(d_pool)]
        + class_grads
        + [jnp.zeros((SMALL_ROWS - small.shape[0], model_width), F32)],
        0,
    )
    scalars = jnp.where(
        lane[0:1] == classes, jnp.sum(loss, 0, keepdims=True) / total_count, jnp.sum(d_logits, 0, keepdims=True)
    )
    scalars = jnp.where(lane[0:1] <= classes, scalars, 0.0)
    third = own_rows // 3
    small_index = lax.broadcasted_iota(jnp.int32, (SMALL_ROWS, own_rows), 0)
    for f in range(shards):
        span = slice(f * own_rows, (f + 1) * own_rows)
        rows = []
        for b in range(count):
            one = slice(b, b + 1)
            rows += [values[one, span].astype(F32) for values in (first_low, context_low, hidden_low, vector_low)]
            rows += [part[one, span].astype(F32) for part in active_parts]
            rows += [head_rows(bars, b)[:, span], head_rows(d_bars, b)[:, span]]
        rows.append(jnp.where(small_index == small.shape[0], scalars[:, 0:own_rows], small_grads[:, span]))
        rows.append(jnp.zeros((LANES - count * SEQ_ROWS - SMALL_ROWS, own_rows), F32))
        for i, term in enumerate(two_terms(jnp.concatenate(rows, 0).T)):
            for q in range(3):
                start = 2 * q * LANES + i * LANES
                shares[f, count * HEAD_ROWS :, start : start + LANES] = term[q * third : (q + 1) * third]
    for b in range(count):
        one = slice(b, b + 1)
        rows = [values[one].astype(F32) for values in (d_query, query, d_context, d_branch, pool_high, pool_mid)]
        rows += [d_before[one, i * model_width : (i + 1) * model_width].astype(F32) for i in range(spread_rows)]
        rows += [d_output[one].astype(F32), jnp.zeros((HEAD_ROWS - 7 - spread_rows, model_width), F32)]
        rows = jnp.concatenate(rows, 0).astype(BF)
        for f in range(shards):
            shares[f, b * HEAD_ROWS : (b + 1) * HEAD_ROWS, :] = rows


def student_step(emb, sides, small, bias, lens, labels, swapped, teacher_cls, teacher_logits, total_count):
    shards, count, own_rows, length_slots = emb.shape
    assert 2 * count * LANES <= length_slots and count * SEQ_ROWS + SMALL_ROWS <= LANES
    model_width = small.shape[1]
    classes = bias.shape[0]

    def wide(values):
        return jnp.pad(values, ((0, 0), (0, LANES - values.shape[1])))

    smem = pl.BlockSpec(memory_space=pltpu.SMEM)
    vmem = pl.BlockSpec(memory_space=pltpu.VMEM)
    return pl.pallas_call(
        functools.partial(student_kernel, total_count, classes),
        name="student",
        in_specs=[smem] * 3 + [vmem] * 7,
        out_specs=[vmem] * 2,
        out_shape=[
            jax.ShapeDtypeStruct((shards, count + 1, COEF, length_slots), BF),
            jax.ShapeDtypeStruct((shards, count * HEAD_ROWS + own_rows // 3, model_width), BF),
        ],
        scratch_shapes=[pltpu.VMEM((count, length_slots, model_width), BF)] * 3
        + [pltpu.VMEM((count, 16, length_slots), F32)],
        compiler_params=pltpu.CompilerParams(vmem_limit_bytes=52 * MIB),
        cost_estimate=small_cost(),
    )(
        lens,
        labels,
        swapped.reshape(1),
        emb,
        *sides,
        small,
        wide(bias[None]),
        teacher_cls,
        wide(teacher_logits),
    )


def adam_update(weight, moment_one, moment_two, gradient, factor):
    gradient = gradient * factor
    first_new = beta_one * moment_one + (1.0 - beta_one) * gradient
    second_new = beta_two * moment_two + (1.0 - beta_two) * gradient * gradient
    first_hat = first_new / (1.0 - beta_one**adam_steps)
    second_hat = second_new / (1.0 - beta_two**adam_steps)
    weight_new = weight - learn_rate * (first_hat / (jnp.sqrt(second_hat) + adam_eps) + decay_rate * weight)
    return (weight_new, first_new, second_new)


TN = (((0,), (0,)), ((), ()))


def tm(left, right):
    return lax.dot_general(left, right, TN, preferred_element_type=F32)


def grads_kernel(groups, group_index, *refs):
    shares, parts = refs[:groups], refs[groups : 2 * groups]
    word_squares, square, widen, narrow, place, payload = refs[2 * groups : 2 * groups + 6]
    factors, wide, bars, d_bars, masked, place_parts, smalls = refs[2 * groups + 6 :]
    shards, _, model_width = shares[0].shape
    own_rows = square.shape[0]
    third = own_rows // 3
    count = factors.shape[0] // (groups * shards)
    spread_rows = narrow.shape[0] // own_rows
    pairs = groups * shards
    base = count * SEQ_ROWS
    head_mask = (
        lax.broadcasted_iota(jnp.int32, (HEAD_ROWS, model_width), 0)
        == lax.broadcasted_iota(jnp.int32, (HEAD_ROWS, model_width), 1) // HDIM
    ).astype(F32)

    for distance in range(groups):
        group = jnp.bitwise_xor(group_index[0], distance)
        share = shares[distance]
        place_parts[group] = parts[distance][...]

        @pl.loop(0, shards, unroll=4)
        def shard(f):
            pair = group * shards + f
            both = jnp.concatenate(
                [
                    share[f, count * HEAD_ROWS :, 2 * q * LANES : 2 * (q + 1) * LANES].astype(F32)
                    for q in range(3)
                ],
                0,
            )
            left = (both[:, :LANES] + both[:, LANES:]).T
            smalls[pair] = left[base : base + SMALL_ROWS]
            for b in range(count):
                seq = pair * count + b
                start = b * SEQ_ROWS
                factors[seq] = left[start : start + MISC_ROWS]
                bars[seq] = left[start + MISC_ROWS : start + MISC_ROWS + HEAD_ROWS]
                d_bars[seq] = left[start + MISC_ROWS + HEAD_ROWS : start + SEQ_ROWS]
                wide[seq] = share[f, b * HEAD_ROWS : (b + 1) * HEAD_ROWS, :].astype(F32)

    def factor(index):
        return factors[:, index, :].astype(BF)

    def side(index):
        return wide[:, index, :].astype(BF)

    def heads(rows, index):
        @pl.loop(0, pairs * count, unroll=8)
        def spread(seq):
            row = wide[seq, index : index + 1, :]
            start = pl.multiple_of(seq * HEAD_ROWS, HEAD_ROWS)
            masked[pl.ds(start, HEAD_ROWS), :] = (jnp.broadcast_to(row, head_mask.shape) * head_mask).astype(BF)

        high_part, low_part = two_terms(rows[...].reshape(pairs * count * HEAD_ROWS, own_rows))
        return tm(high_part, masked[...]) + tm(low_part, masked[...])

    total = jnp.zeros((), F32)
    blocks = [
        tm(factor(0), side(0)),
        heads(d_bars, 1) * HDIM ** (-0.5),
        heads(bars, 2),
        tm(factor(1), side(3)),
        tm(factor(3), side(4)) + tm(factor(3), side(5)),
    ]
    for i, block in enumerate(blocks):
        square[:, i * model_width : (i + 1) * model_width] = block
        total = total + jnp.sum(block * block)
    for i in range(spread_rows):
        block = tm(factor(2), side(6 + i))
        widen[:, i * model_width : (i + 1) * model_width] = block
        total = total + jnp.sum(block * block)
        block = tm(factor(4 + i), side(6 + spread_rows))
        narrow[i * own_rows : (i + 1) * own_rows, :] = block
        total = total + jnp.sum(block * block)
    places = place_parts[0]
    for g in range(1, groups):
        places = places + place_parts[g]
    places = places[0:own_rows]
    place[...] = places
    total = total + jnp.sum(places * places)
    small = smalls[0]
    for p in range(1, pairs):
        small = small + smalls[p]
    rows = lax.broadcasted_iota(jnp.int32, small.shape, 0)
    lanes = lax.broadcasted_iota(jnp.int32, small.shape, 1)
    small = jnp.where(rows == SMALL_ROWS - 1, jnp.where(lanes == 0, total, jnp.sum(word_squares[...])), small)
    for d in range(payload.shape[0]):
        payload[d] = small


def weight_grads(group_index, shares, place_parts, word_squares, devices, own_rows):
    groups = len(shares)
    shards, share_rows, model_width = shares[0].shape
    count = (share_rows - own_rows // 3) // HEAD_ROWS
    places = place_parts[0].shape[1]
    right_rows = HEAD_ROWS
    spread_rows = MISC_ROWS - 4
    smem = pl.BlockSpec(memory_space=pltpu.SMEM)
    vmem = pl.BlockSpec(memory_space=pltpu.VMEM)
    seqs = groups * shards * count
    return pl.pallas_call(
        functools.partial(grads_kernel, groups),
        name="weight_grads",
        in_specs=[smem] + [vmem] * (2 * groups + 1),
        out_specs=[vmem] * 5,
        out_shape=[
            jax.ShapeDtypeStruct((own_rows, 5 * model_width), F32),
            jax.ShapeDtypeStruct((own_rows, spread_rows * model_width), F32),
            jax.ShapeDtypeStruct((spread_rows * own_rows, model_width), F32),
            jax.ShapeDtypeStruct((own_rows, places), F32),
            jax.ShapeDtypeStruct((devices, SMALL_ROWS, own_rows), F32),
        ],
        scratch_shapes=[
            pltpu.VMEM((seqs, MISC_ROWS, own_rows), F32),
            pltpu.VMEM((seqs, right_rows, model_width), F32),
            pltpu.VMEM((seqs, HEAD_ROWS, own_rows), F32),
            pltpu.VMEM((seqs, HEAD_ROWS, own_rows), F32),
            pltpu.VMEM((seqs * HEAD_ROWS, model_width), BF),
            pltpu.VMEM((groups,) + place_parts[0].shape, F32),
            pltpu.VMEM((groups * shards, SMALL_ROWS, own_rows), F32),
        ],
        compiler_params=pltpu.CompilerParams(vmem_limit_bytes=58 * MIB),
        cost_estimate=small_cost(),
    )(group_index.reshape(1), *shares, *place_parts, word_squares)


def norm_kernel(classes, core, parts, others, *refs):
    grads, refs = refs[:4], refs[4:]
    states, (factor_out, scalars), outs = refs[:18], refs[18:20], refs[20:]
    devices, _, own_rows = parts.shape
    rows_all = states[12].shape[0]
    joined = jnp.concatenate([parts[d] for d in range(devices)], 1)
    last = SMALL_ROWS - 1
    total = jnp.zeros((1, 1), F32)
    mine = jnp.zeros((1, 1), F32)
    other = jnp.zeros((1, 1), F32)
    for d in range(devices):
        total = total + parts[d, last : last + 1, 0:1]
        mine = mine + parts[d, last : last + 1, 1:2]
        other = other + others[d, last : last + 1, 1:2]
    first = jnp.where(core[0] == 0, mine, other)
    second = jnp.where(core[0] == 0, other, mine)
    small_grad = joined[0:rows_all]
    extra = parts[0, rows_all : rows_all + 1, :]
    lane = lax.broadcasted_iota(jnp.int32, extra.shape, 1)
    bias_grad = extra[:, 0:classes]
    total = total + first + second
    total = total + jnp.sum(jnp.sum(small_grad * small_grad, 1, keepdims=True), 0, keepdims=True)
    total = total + jnp.sum(bias_grad * bias_grad, 1, keepdims=True)
    norm = jnp.sqrt(total)
    factor = jnp.minimum(1.0, clip_bound / norm)
    factor_out[...] = jnp.broadcast_to(factor, factor_out.shape)
    loss = jnp.sum(jnp.where(lane == classes, extra, 0.0), 1, keepdims=True)
    lanes = lax.broadcasted_iota(jnp.int32, scalars.shape, 1)
    scalars[...] = jnp.where(lanes == 0, jnp.broadcast_to(loss, scalars.shape), jnp.broadcast_to(norm, scalars.shape))

    def update(index, gradient):
        weight, moment_one, moment_two = (states[3 * index + j][...] for j in range(3))
        new = adam_update(weight, moment_one, moment_two, gradient, factor)
        for j in range(3):
            outs[3 * index + j][...] = new[j]

    for index, grad in enumerate(grads):
        update(index, grad[...])
    update(4, small_grad)
    update(5, bias_grad)


def norm_step(core, parts, others, grads, states):
    classes = states[5][0].shape[0]
    steps = 3

    def whole(array):
        return pl.BlockSpec(array.shape, lambda i, *scalars: (0,) * array.ndim)

    def block(array):
        return pl.BlockSpec((array.shape[0] // steps, array.shape[1]), lambda i, *scalars: (i, 0))

    flat = [array[None] if array.ndim == 1 else array for state in states for array in state]
    flat_specs = [block(array) for array in flat[:12]] + [whole(array) for array in flat[12:]]
    row = jax.ShapeDtypeStruct((1, LANES), F32)
    outs = pl.pallas_call(
        functools.partial(norm_kernel, classes),
        name="norm",
        grid_spec=pltpu.PrefetchScalarGridSpec(
            num_scalar_prefetch=1,
            grid=(steps,),
            in_specs=[whole(parts), whole(others)] + [block(grad) for grad in grads] + flat_specs,
            out_specs=[whole(row), whole(row)] + flat_specs,
        ),
        out_shape=[row, row] + [jax.ShapeDtypeStruct(array.shape, F32) for array in flat],
        compiler_params=pltpu.CompilerParams(vmem_limit_bytes=48 * MIB),
        cost_estimate=small_cost(),
    )(core.reshape(1), parts, others, *grads, *flat)
    rest = [out[0] if out.shape[0] == 1 else out for out in outs[2:]]
    return outs[0], outs[1], rest


def on_device(
    tokens,
    positions,
    lengths,
    labels,
    word_table,
    word_first,
    word_second,
    place_table,
    place_first,
    place_second,
    square_weights,
    square_first,
    square_second,
    widen_weights,
    widen_first,
    widen_second,
    narrow_weights,
    narrow_first,
    narrow_second,
    small_params,
    small_first,
    small_second,
    class_bias,
    class_first,
    class_second,
    teacher_word,
    teacher_place,
    teacher_attention,
    teacher_feedforward,
    teacher_pooler,
    teacher_vectors,
):
    shards = lax.axis_size("fsdp")
    groups = lax.axis_size("grp")
    shard_index = lax.axis_index("fsdp")
    group_index = lax.axis_index("grp")
    count, length_slots = tokens.shape
    model_width = small_params.shape[1]
    own_rows = word_table.shape[0]
    entries = word_table.shape[1]
    places = place_table.shape[1]
    spread_rows = widen_weights.shape[1] // model_width
    classes = class_bias.shape[0]
    head_count = model_width // HDIM
    total_count = count * shards * groups
    core = jnp.bitwise_and(group_index, 1)

    half_entries = half_of(entries)
    codes = tokens * CODE + positions
    slots = jnp.arange(length_slots, dtype=jnp.int32)[None]
    keys = jnp.where(slots < lengths[:, None], codes, LAST_KEY)
    keys = jnp.where(slots == 0, -1, keys)
    ahead = (keys[:, :, None] < keys[:, None, :]) | (
        (keys[:, :, None] == keys[:, None, :]) & (slots[:, :, None] < slots[:, None, :])
    )
    rank = jnp.sum(ahead.astype(jnp.int32), 1)
    codes = jnp.sum(jnp.where(rank[:, :, None] == slots[:, None, :], codes[:, :, None], 0), 1)
    early = jnp.sum(((keys >= 0) & (keys < half_entries * CODE)).astype(jnp.int32), 1)
    words = lax.shift_right_arithmetic(keys, 9)
    same = (words[:, :, None] == words[:, None, :]) & (keys[:, :, None] >= 0) & (keys[:, :, None] < LAST_KEY)
    repeats = jnp.sum(same.astype(jnp.int32), 1)
    runs = []
    for low_half in (True, False):
        there = jnp.where((keys >= 0) & (keys < LAST_KEY) & ((words < half_entries) == low_half), repeats, 0)
        top = jnp.max(there, 1)
        begin = jnp.min(jnp.where((there == top[:, None]) & (there > 0), rank, length_slots), 1)
        inside = (rank >= begin[:, None]) & (rank < (begin + top)[:, None])
        runs += [begin, top, jnp.max(jnp.where(inside, 0, there), 1)]
    facts = jnp.stack([lengths, labels, early] + runs, 1)
    message = jnp.concatenate([codes, facts, jnp.zeros((count, LANES - facts.shape[1]), jnp.int32)], 1)
    everyone = spread_to(message, ALL, shards * groups).reshape(total_count, -1)

    attention_source = jnp.swapaxes(teacher_attention, 2, 3)
    sources = [
        attention_source[0],
        teacher_feedforward[0, 0],
        teacher_feedforward[0, 1],
        (attention_source[1, 0:2], attention_source[1, 2:4]),
    ]

    side = half_weights(core, square_weights, widen_weights, narrow_weights)
    everyone, sources, side = lax.optimization_barrier((everyone, sources, side))

    all_codes = everyone[:, :length_slots].reshape(-1)
    all_words = jnp.pad(lax.shift_right_logical(all_codes, 9) - core * half_entries, (0, LANES))
    all_facts = everyone[:, length_slots:]
    all_lens = all_facts[:, 0]
    index = jnp.arange(total_count, dtype=jnp.int32)
    longer = (all_lens[None] > all_lens[:, None]) | ((all_lens[None] == all_lens[:, None]) & (index[None] < index[:, None]))
    rank = jnp.sum(longer.astype(jnp.int32), 1)
    turn, seat = rank // (shards * groups), rank % (shards * groups)
    seat = jnp.where(turn % 2 == 0, seat, shards * groups - 1 - seat)
    target = seat * count + turn
    deal = jnp.sum(jnp.where(target[None] == index[:, None], index[None], 0), 1, keepdims=True)
    info = jnp.where(jnp.arange(LANES)[None] == DEAL, deal, all_facts)
    mine = (shard_index * groups + group_index) * count + jnp.arange(count, dtype=jnp.int32)
    own = jnp.sum(jnp.where(target[None, :, None] == mine[:, None, None], all_facts[None, :, :2], 0), 1)
    lengths, labels = own[:, 0], own[:, 1]
    row_where = jnp.stack([shard_index * groups * count, jnp.full((), count, jnp.int32)])
    column_where = jnp.stack([group_index * count, jnp.full((), groups * count, jnp.int32)])
    column = column_where[0] + jnp.arange(shards)[:, None] * column_where[1] + jnp.arange(count)[None]
    all_spots = jnp.bitwise_and(everyone[:, :length_slots], CODE - 1)
    column_hits = target[None] == column.reshape(-1)[:, None]
    column_spots = jnp.sum(jnp.where(column_hits[:, :, None], all_spots[None], 0), 1).astype(F32)[:, None]

    shard_bias = [teacher_vectors[row : row + 2] for row in (2, 2 + 8 + spread_rows)]
    shard_bias = jnp.concatenate(shard_bias).reshape(4 * groups, -1)
    near = [group_swap(piece, 1, groups) for piece in sources[:3]]
    near.append([group_swap(piece, 1, groups) for piece in sources[3]])
    far = [group_swap(piece, 2, groups) for piece in sources[:2]]
    index_work = (info, all_words, column_spots, row_where, column_where, lengths, labels, shard_bias)
    index_work = lax.optimization_barrier(index_work)
    info, all_words, column_spots, row_where, column_where, lengths, labels, shard_bias = index_work
    side_own = lax.all_gather(side, "fsdp", axis=0, tiled=True)

    teacher_slices = lookup(
        all_codes, info, row_where, teacher_word, teacher_place, groups, count, length_slots
    )
    teacher_slices, far[0], column_where, sources[2] = lax.optimization_barrier(
        (teacher_slices, far[0], column_where, sources[2])
    )
    teacher_embedded = exchange(teacher_slices, "grp").reshape(groups, count, -1, length_slots)
    far.append(group_swap(sources[2], 2, groups))
    student_slices = lookup(
        all_codes, info, column_where, word_table, place_table, shards, count, length_slots
    )
    student_slices, far[1], near[:2] = lax.optimization_barrier((student_slices, far[1], near[:2]))
    embedded = exchange(student_slices, "fsdp").reshape(shards, count, own_rows, length_slots)
    group_slices = lax.all_gather(student_slices, "grp", axis=0, tiled=True)
    last = [group_swap(piece, 1, groups) for piece in far[:2]]
    last[0], sources[3] = lax.optimization_barrier((last[0], sources[3]))
    far.append([group_swap(piece, 2, groups) for piece in sources[3]])
    teacher_embedded, student_slices = lax.optimization_barrier((teacher_embedded, student_slices))
    shard_pieces = [list(pieces) for pieces in zip(sources[:2], near[:2], far[:2], last)]

    teacher_cls, teacher_logits, (embedded, side_own, side_far) = teacher_forward(
        teacher_embedded,
        shard_bias,
        shard_pieces,
        (sources[2], near[2], far[2]),
        (sources[3], near[3], far[3]),
        (embedded, side_own),
        teacher_feedforward,
        teacher_pooler,
        teacher_vectors,
        lengths,
        group_index,
    )
    message, shares = student_step(
        embedded,
        (side_own, side_far),
        small_params,
        class_bias,
        lengths,
        labels,
        core,
        teacher_cls,
        teacher_logits,
        total_count,
    )

    message = exchange(message, "fsdp")
    message, shares = lax.optimization_barrier((message, shares))
    shares = exchange(shares, "fsdp")
    far_message = group_swap(message, 2, groups)
    place_part = place_sums(info, column_where, message, student_slices, column_spots, places)
    shares, far_message, place_part = lax.optimization_barrier((shares, far_message, place_part))
    all_messages = [message, group_swap(message, 1, groups), far_message, group_swap(far_message, 1, groups)]
    shares, place_part, all_messages = lax.optimization_barrier((shares, place_part, all_messages))
    place_parts, shares = (group_direct(v, groups) for v in (place_part, shares))
    half_rows, word_squares = scatter(
        all_words, info, core, group_index, all_messages, group_slices, half_entries
    )
    shares, place_parts, half_rows, word_squares = lax.optimization_barrier(
        (shares, place_parts, half_rows, word_squares)
    )
    square_grad, widen_grad, narrow_grad, place_grad, payload = weight_grads(
        group_index, shares, place_parts, word_squares, shards, own_rows
    )
    payload, half_rows = lax.optimization_barrier((payload, half_rows))
    other_rows = group_swap(half_rows, 1, groups)
    parts = exchange(payload, "fsdp")
    factor, scalars, rest = norm_step(
        core,
        parts,
        group_swap(parts, 1, groups),
        (place_grad, square_grad, widen_grad, narrow_grad),
        (
            (place_table, place_first, place_second),
            (square_weights, square_first, square_second),
            (widen_weights, widen_first, widen_second),
            (narrow_weights, narrow_first, narrow_second),
            (small_params, small_first, small_second),
            (class_bias, class_first, class_second),
        ),
    )
    word = adam_table(factor[0, 0:1], core, half_rows, other_rows, word_table, word_first, word_second)
    results = [scalars[0, 0], scalars[0, 1], *word, *rest]
    return tuple(results)


def solution(mesh):
    rows = P("fsdp", None)
    seqs = P(("fsdp", "grp"))
    table = [rows] * 15
    placed = (
        [P(("fsdp", "grp"), None)] * 2
        + [seqs] * 2
        + table
        + [P()] * 6
        + [P("grp", None)] * 2
        + [P(None, None, None, "grp")] * 2
        + [P()] * 2
    )
    return jax.shard_map(
        on_device,
        mesh=mesh,
        in_specs=tuple(placed),
        out_specs=tuple([P(), P()] + table + [P()] * 6),
        check_vma=False,
    )
```
